256 devices in a mesh: grow: 32 (over y_hi, z, core), gy: 4 (over x), gz: 2 (over y_lo).
Axes of the slice: x: 4, y: 4 (y_hi: 2, y_lo: 2; y = y_hi * 2 + y_lo), z: 8, core: 2. Of those that a mesh axis runs over, the one named last changes fastest.
Arguments:
- labels: int32 [1024, 32, 256], P('grow', 'gy', 'gz'), may hold values from 0 to 3
- potential: float32 [2, 1024, 32, 256], P(None, 'grow', 'gy', 'gz'), may hold values from -3 to 3
- melt_codes: int32 [16, 32, 256], P(None, 'gy', 'gz'), may hold values from 0 to 7
- melt_table: float32 [2, 8], replicated, may hold values from -1 to 1
Outputs:
- phases: float32 [4, 1024, 32, 256], P(None, 'grow', 'gy', 'gz')
- potentials: float32 [2, 1024, 32, 256], P(None, 'grow', 'gy', 'gz')
The draws below stay inside these ranges and needn't reach their ends.
All inputs are finite; a program needn't handle non-finite values.
Results may differ from the reference program's by a relative error of at most 0.0001.
Values sent between devices are 32-bit elements; how exact they have to be, the bound alone decides.
No kernel may reach another device: no remote copies, remote signals or barrier semaphores. Data moves between devices by JAX's collectives and lax.ppermute only.
A program may use at most 64 MiB of HBM per device.

```python
import jax
import jax.numpy as jnp
from jax import lax

SHIFT = 16
LEVELS = 8
STEPS_BEFORE = 3
STEPS_AFTER = 2
NG = 1024
NY = 32
NZ = 256


def plant(values, stream_key, smallest, largest):
    place = [jax.random.randint(jax.random.fold_in(stream_key, axis), (), 0, length) for axis, length in enumerate(values.shape)]
    longest = values.shape.index(max(values.shape))
    next_to = place[:longest] + [(place[longest] + 1) % values.shape[longest]] + place[longest + 1:]
    return values.at[tuple(place)].set(smallest).at[tuple(next_to)].set(largest)


def block_levels(own_key, shape, cuts, low, top_value):
    level = 1.0
    for position, parts in cuts:
        draws = jax.random.uniform(jax.random.fold_in(jax.random.fold_in(own_key, 6), position), (parts,), jnp.float32, low / len(cuts), top_value / len(cuts))
        level = level * jnp.repeat(jnp.exp(draws), shape[position] // parts).reshape((-1,) + (1,) * (len(shape) - 1 - position))
    return level


def scatter_about(stream_key, shape, scale, limit, cuts=(), held_as=jnp.bfloat16):
    entries = scale * jax.random.normal(stream_key, shape, jnp.float32)
    if cuts:
        entries = entries * block_levels(stream_key, shape, cuts, -0.22, 0.18)
    return jnp.clip(entries, -limit, limit).astype(held_as)


def setup_inputs(seed: int = 0) -> dict:
    keys = jax.random.split(jax.random.key(seed), 5)
    labels = plant(jax.random.randint(keys[0], (NG, NY, NZ), 0, 4), jax.random.fold_in(keys[0], 1), 0, 3).astype(jnp.int32)
    potential = scatter_about(keys[1], (2, NG, NY, NZ), 0.5, 3.0, ((1, 32), (2, 4), (3, 2)), jnp.float32)
    melt_codes = plant(jax.random.randint(keys[2], (SHIFT, NY, NZ), 0, LEVELS), jax.random.fold_in(keys[2], 1), 0, LEVELS - 1).astype(jnp.int32)
    melt_table = jnp.clip(jax.random.uniform(keys[3], (2, LEVELS), jnp.float32, -1.0, 1.0), -1.0, 1.0)
    return {"labels": labels, "potential": potential, "melt_codes": melt_codes, "melt_table": melt_table}


comp_table = ((0.8, 0.1), (0.1, 0.8), (0.1, 0.1), (0.35, 0.35))
free_energy = (-0.05, -0.05, -0.05, 0.0)
diffusivity = (0.05, 0.05, 0.05, 1.0)
grad_rate = 0.12
well_rate = 0.3
drive_rate = 0.5
diff_rate = 0.15


def laplacian(fields, grow_padded, side_padded):
    total = grow_padded[:, 2:] + grow_padded[:, :-2]
    total = total + (side_padded[:, :, 2:, 1:-1] + side_padded[:, :, :-2, 1:-1])
    total = total + (side_padded[:, :, 1:-1, 2:] + side_padded[:, :, 1:-1, :-2])
    return total - 6.0 * fields


def advance(fields, grow_padded, side_padded):
    phases = fields[:4]
    chem_pot = fields[4:]
    laplace = laplacian(fields, grow_padded, side_padded)
    comp = jnp.array(comp_table, jnp.float32)
    comp_first = comp[:, 0].reshape(4, 1, 1, 1)
    comp_second = comp[:, 1].reshape(4, 1, 1, 1)
    energy = jnp.array(free_energy, jnp.float32).reshape(4, 1, 1, 1)
    spread = jnp.array(diffusivity, jnp.float32).reshape(4, 1, 1, 1)
    grand_pot = energy - (chem_pot[0:1] * comp_first + chem_pot[1:2] * comp_second)
    squares = phases * phases
    others = jnp.sum(squares, axis=0, keepdims=True) - squares
    slope = 6.0 * phases * (1.0 - phases)
    increment = grad_rate * laplace[:4] - 2.0 * well_rate * phases * others - drive_rate * slope * grand_pot
    increment = increment - jnp.mean(increment, axis=0, keepdims=True)
    clipped = jnp.clip(phases + increment, 0.0, 1.0)
    new_phases = clipped / jnp.sum(clipped, axis=0, keepdims=True)
    change = new_phases * new_phases * (3.0 - 2.0 * new_phases) - phases * phases * (3.0 - 2.0 * phases)
    mobility = jnp.sum(phases * spread, axis=0, keepdims=True)
    release = jnp.concatenate([jnp.sum(change * comp_first, axis=0, keepdims=True), jnp.sum(change * comp_second, axis=0, keepdims=True)], axis=0)
    new_chem = chem_pot + diff_rate * mobility * laplace[4:] - release
    return jnp.concatenate([new_phases, new_chem], axis=0)


def pad_faces(fields):
    grow_padded = jnp.concatenate([fields[:, :1], fields, fields[:, -1:]], axis=1)
    side_padded = jnp.concatenate([fields[:, :, -1:], fields, fields[:, :, :1]], axis=2)
    side_padded = jnp.concatenate([side_padded[:, :, :, -1:], side_padded, side_padded[:, :, :, :1]], axis=3)
    return grow_padded, side_padded


def melt_planes(melt_codes, melt_table):
    levels = melt_table.shape[1]
    onehot = (melt_codes[None] == jnp.arange(levels, dtype=jnp.int32).reshape(levels, 1, 1, 1)).astype(jnp.float32)
    chem_pot = jnp.einsum("ik,kabc->iabc", melt_table.astype(jnp.float32), onehot, precision=lax.Precision.HIGHEST)
    liquid = (jnp.arange(4, dtype=jnp.int32) == 3).astype(jnp.float32).reshape(4, 1, 1, 1)
    phases = jnp.broadcast_to(liquid, (4,) + melt_codes.shape)
    return jnp.concatenate([phases, chem_pot], axis=0)


def reference(labels, potential, melt_codes, melt_table):
    phases = (labels[None] == jnp.arange(4, dtype=jnp.int32).reshape(4, 1, 1, 1)).astype(jnp.float32)
    fields = jnp.concatenate([phases, potential], axis=0)
    for iteration in range(STEPS_BEFORE):
        grow_padded, side_padded = pad_faces(fields)
        fields = advance(fields, grow_padded, side_padded)
    fields = jnp.concatenate([fields[:, SHIFT:], melt_planes(melt_codes, melt_table)], axis=1)
    for iteration in range(STEPS_AFTER):
        grow_padded, side_padded = pad_faces(fields)
        fields = advance(fields, grow_padded, side_padded)
    return fields[:4], fields[4:]
```

```python
import jax
import jax.numpy as jnp
from jax import lax
from jax.experimental import pallas as pl
from jax.experimental.pallas import tpu as pltpu
from jax.sharding import PartitionSpec as P

K = 5.0**0.5
ALPHA = 5.0 * K**3
BETA = 2.5 / (K * ALPHA)
TOP = K / 0.12
DRIFT = 0.15 / (0.12 * K)
HALF = 0.5 * K**3

SHIFT = 16
OWN = 21
PLANES = 2 * OWN
PITCH = 32
ROW0 = 12
DEEP = 5
PACK = 11
AXES = ("grow", "gy", "gz")
VMEM = pl.BlockSpec(memory_space=pltpu.VMEM)
SMEM = pl.BlockSpec(memory_space=pltpu.SMEM)


def lanes():
    return lax.broadcasted_iota(jnp.int32, (8, 128), 1)


def first_pack(where_ref, labels, potential, codes, table, upper, edges):
    first = where_ref[0] == 0

    @pl.when(first)
    def _():
        for e in range(OWN):
            upper[0, e] = jnp.full((8, 128), 3.0, jnp.float32)
            for i in range(2):
                value = jnp.zeros((8, 128), jnp.float32)
                if e < SHIFT:
                    code = codes[e]
                    for level in range(8):
                        value = jnp.where(code == level, table[i, level], value)
                upper[1 + i, e] = value

    @pl.when(jnp.logical_not(first))
    def _():
        for e in range(OWN):
            upper[0, e] = labels[e].astype(jnp.float32)
            for i in range(2):
                upper[1 + i, e] = potential[i, e]

    lane = lanes()
    for f in range(3):

        def own(p, f=f):
            return labels[p].astype(jnp.float32) if f == 0 else potential[f - 1, p]

        groups = (
            [upper[f, e] for e in range(PACK)],
            [upper[f, e] for e in range(PACK, OWN)],
            [own(p) for p in range(11, 22)],
            [own(p) for p in range(22, 32)],
        )
        for q, group in enumerate(groups):
            total = jnp.zeros((8, 128), jnp.float32)
            for c, tile in enumerate(group):
                there = (lane >= 10 * c) & (lane < 10 * c + 10)
                total = jnp.where(there, pltpu.roll(tile, (10 * c + 5) % 128, 1), total)
            edges[f, q] = total


def second_pack(labels, potential, upper, across, grow, own_lo, own_hi, up_lo, up_hi):
    for f in range(3):
        for p in range(OWN + 2):
            n = 5 * (f * (OWN + 2) + p)
            tile = upper[f, p] if p < OWN else across[f, p - OWN]
            grow[f, p] = tile
            up_lo[n : n + 5] = tile[0:5]
            up_hi[n : n + 5] = tile[3:8]
            if p >= OWN:
                tile = across[f, p - OWN + 2]
            elif f == 0:
                tile = labels[p + 11].astype(jnp.float32)
            else:
                tile = potential[f - 1, p + 11]
            own_lo[n : n + 5] = tile[0:5]
            own_hi[n : n + 5] = tile[3:8]


def react(phases, sums, chem, chem_sums, held):
    p0, p1, p2 = phases
    p3 = K - ((p0 + p1) + p2)
    n3 = 6.0 * K - ((sums[0] + sums[1]) + sums[2])
    ps = (p0, p1, p2, p3)
    ns = (sums[0], sums[1], sums[2], n3)
    squares = [p * p for p in ps]
    base = (0.28 / 0.12) - ((squares[0] + squares[1]) + (squares[2] + squares[3]))
    m0, m1 = chem
    both = BETA * (m0 + m1)
    w2 = both + DRIFT
    ws = (w2 + (7.0 * BETA) * m0, w2 + (7.0 * BETA) * m1, w2, 3.5 * both)
    moved = [
        ns[a] + ps[a] * ((base + squares[a]) + ws[a] * (K - ps[a])) for a in range(4)
    ]
    excess = 0.25 * ((moved[0] + moved[1]) + (moved[2] + moved[3])) - 0.25 * TOP
    clipped = [jnp.minimum(jnp.maximum(u - excess, 0.0), TOP) for u in moved]
    scale = K / ((clipped[0] + clipped[1]) + (clipped[2] + clipped[3]))
    new = [s * scale for s in clipped]
    h = [x * x * (1.5 * K - x) for x in new]
    shared = (h[0] + h[1]) + (h[2] + 3.5 * h[3])
    solute = (shared + 7.0 * h[0], shared + 7.0 * h[1])
    mobility = 0.0075 + (0.1425 / K) * p3
    new_held = [held[i] + mobility * (chem_sums[i] - 6.0 * chem[i]) for i in range(2)]
    new_chem = [new_held[i] - solute[i] for i in range(2)]
    return new, new_chem, new_held


def evolve(
    where_ref, labels, potential, across, grow, own_lo, own_hi, up_lo, up_hi,
    phases_out, chem_out, one, two,
):
    first = where_ref[0] == 0
    last = where_ref[0] == where_ref[1] - 1
    lane = lanes()

    def start(dst, z, p, rows, label, m0, m1):
        solids = [jnp.where(label == a, K, 0.0) for a in range(3)]
        for a in range(3):
            dst[a, z, p, rows, :] = solids[a]
        melt = jnp.where(label == 3.0, 3.5 * HALF, HALF)
        for i, m in enumerate((m0, m1)):
            m = ALPHA * m
            dst[3 + i, z, p, rows, :] = m
            dst[5 + i, z, p, rows, :] = m + jnp.where(label == i, 8.0 * HALF, melt)

    def fill(dst, p):
        low = p < OWN
        s = p if low else p - OWN
        q, c = divmod(s, PACK)
        for z in range(2):

            def turned(x, z=z):
                return pltpu.roll(x, (123 - 10 * c) % 128, 1) if z else x

            body = []
            for f in range(3):
                if z:
                    tile = across[f, q + 2] if low else grow[f, OWN + q]
                elif not low:
                    tile = grow[f, s]
                elif f == 0:
                    tile = labels[s + 11].astype(jnp.float32)
                else:
                    tile = potential[f - 1, s + 11]
                body.append(turned(tile))
            start(dst, z, p, slice(ROW0, ROW0 + 8), *body)
            at = OWN + q if z else s
            for ref, row in ((own_lo if low else up_lo, 8), (own_hi if low else up_hi, -5)):
                body = []
                for f in range(3):
                    n = 5 * (f * (OWN + 2) + at)
                    body.append(turned(ref[n : n + 5]))
                start(dst, z, p, slice(ROW0 + row, ROW0 + row + 5), *body)

    def repeat(ref, p, source):
        for f in range(5):
            for z in range(2):
                ref[f, z, p, 7:25, :] = ref[f, z, source, 7:25, :]

    def gather(src, f, z, p, row):
        rows = slice(row, row + 8)
        here = src[f, z, p, rows, :]
        there = src[f, 1 - z, p, rows, :]
        total = src[f, z, p - 1, rows, :] + src[f, z, p + 1, rows, :]
        total = total + (
            src[f, z, p, row - 1 : row + 7, :] + src[f, z, p, row + 1 : row + 9, :]
        )
        left = pltpu.roll(jnp.where(lane == 127, there, here), 1, 1)
        right = pltpu.roll(jnp.where(lane == 0, there, here), 127, 1)
        return here, total + (left + right)

    def tile_step(src, z, p, row):
        pairs = [gather(src, f, z, p, row) for f in range(5)]
        held = [src[f, z, p, row : row + 8, :] for f in (5, 6)]
        here = [a for a, _ in pairs]
        sums = [b for _, b in pairs]
        return react(here[:3], sums[:3], here[3:], sums[3:], held)

    def sweep(src, dst, s):
        count = PLANES - 2 * s

        @pl.loop(s, PLANES - s, unroll=4 if count % 4 == 0 else 2)
        def _(p):
            for z in range(2):
                for row in (8, 16):
                    new, chem, held = tile_step(src, z, p, row)
                    for f, value in enumerate((*new[:3], *chem, *held)):
                        dst[f, z, p, row : row + 8, :] = value

    for p in range(PLANES):
        fill(one, p)
    src, dst = one, two
    for s in range(1, 4):

        @pl.when(last)
        def _(src=src):
            repeat(src, OWN, OWN - 1)

        sweep(src, dst, s)
        src, dst = dst, src

    @pl.when(last)
    def _(src=src):
        for p in range(OWN, OWN + SHIFT):
            fill(src, p)
        repeat(src, OWN + SHIFT, OWN + SHIFT - 1)

    @pl.when(first)
    def _(src=src):
        repeat(src, 4, 5)

    sweep(src, dst, 4)
    src, dst = dst, src

    @pl.when(last)
    def _(src=src):
        repeat(src, OWN + SHIFT, OWN + SHIFT - 1)

    @pl.when(first)
    def _(src=src):
        repeat(src, 4, 5)

    @pl.loop(5, PLANES - 5, unroll=4)
    def _(p):
        new, chem, _ = tile_step(src, 0, p, ROW0)
        for a in range(4):
            phases_out[a, p - 5] = new[a] * (1.0 / K)
        for i in range(2):
            chem_out[i, p - 5] = chem[i] * (1.0 / ALPHA)


def on_device(labels, potential, melt_codes, melt_table):
    n_grow, n_gy, n_gz = (lax.axis_size(a) for a in AXES)
    where = jnp.stack([lax.axis_index("grow"), n_grow]).astype(jnp.int32)

    def send(value, dg, dy, dz):
        pairs = []
        for g in range(n_grow):
            for y in range(n_gy):
                for z in range(n_gz):
                    to = ((g + dg) % n_grow * n_gy + (y + dy) % n_gy) * n_gz + (z + dz) % n_gz
                    pairs.append(((g * n_gy + y) * n_gz + z, to))
        return lax.ppermute(value, AXES, pairs)

    def f32(*shape):
        return jax.ShapeDtypeStruct(shape, jnp.float32)

    params = pltpu.CompilerParams(vmem_limit_bytes=48 << 20)
    upper, edges = pl.pallas_call(
        first_pack,
        in_specs=[SMEM, VMEM, VMEM, VMEM, SMEM],
        out_specs=[VMEM, VMEM],
        out_shape=[f32(3, OWN, 8, 128), f32(3, 4, 8, 128)],
        compiler_params=params,
        name="first_pack",
    )(where, labels, potential, melt_codes, melt_table)
    across = send(edges, 0, 0, 1)
    rows = 5 * 3 * (OWN + 2)
    grow, own_lo, own_hi, up_lo, up_hi = pl.pallas_call(
        second_pack,
        in_specs=[VMEM] * 4,
        out_specs=[VMEM] * 5,
        out_shape=[f32(3, OWN + 2, 8, 128)] + [f32(rows, 128)] * 4,
        compiler_params=params,
        name="second_pack",
    )(labels, potential, upper, across)
    own_lo = send(own_lo, 0, -1, 0)
    own_hi = send(own_hi, 0, 1, 0)
    grow = send(grow, -1, 0, 0)
    up_lo = send(up_lo, -1, -1, 0)
    up_hi = send(up_hi, -1, 1, 0)
    held = pltpu.VMEM((7, 2, PLANES, PITCH, 128), jnp.float32)
    return pl.pallas_call(
        evolve,
        in_specs=[SMEM] + [VMEM] * 8,
        out_specs=[VMEM, VMEM],
        out_shape=[f32(4, 32, 8, 128), f32(2, 32, 8, 128)],
        scratch_shapes=[held, held],
        compiler_params=params,
        name="evolve",
    )(where, labels, potential, across, grow, own_lo, own_hi, up_lo, up_hi)


def solution(mesh):
    return jax.shard_map(
        on_device,
        mesh=mesh,
        in_specs=(P("grow", "gy", "gz"), P(None, "grow", "gy", "gz"), P(None, "gy", "gz"), P()),
        out_specs=(P(None, "grow", "gy", "gz"), P(None, "grow", "gy", "gz")),
        check_vma=False,
    )
```

```python
import jax
import jax.numpy as jnp
from jax import lax
from jax.experimental import pallas as pl
from jax.experimental.pallas import tpu as pltpu
from jax.sharding import PartitionSpec as P

K = 5.0**0.5
ALPHA = 5.0 * K**3
BETA = 2.5 / (K * ALPHA)
TOP = K / 0.12
DRIFT = 0.15 / (0.12 * K)
HALF = 0.5 * K**3

SHIFT = 16
OWN = 21
PLANES = 2 * OWN
PITCH = 32
ROW0 = 12
DEEP = 5
PACK = 11
AXES = ("grow", "gy", "gz")
VMEM = pl.BlockSpec(memory_space=pltpu.VMEM)
HBM = pl.BlockSpec(memory_space=pltpu.MemorySpace.HBM)
SMEM = pl.BlockSpec(memory_space=pltpu.SMEM)


def lanes():
    return lax.broadcasted_iota(jnp.int32, (8, 128), 1)


def reach(i, up):
    return min(DEEP, OWN - 1 - i if up else i)


def plan(up):
    places, at = {}, 0
    for f in range(3):
        for i in range(OWN):
            places["cell", f, i] = (at, reach(i, up))
            at += reach(i, up)
        for q in range(2):
            places["edge", f, q] = (at, DEEP)
            at += DEEP
    if not up:
        for e in range(SHIFT):
            places["code", 0, e] = (at, 2)
            at += 2
        places["code_edge", 0, 0] = (at, 2)
        at += 2
    return places, -(-at // 8) * 8


OWN_PLAN, OWN_ROWS = plan(False)
UP_PLAN, UP_ROWS = plan(True)


def first_pack(labels, potential, codes, cells, codes_out, edges, labels_in, codes_in, sems):
    copies = [
        pltpu.make_async_copy(labels, labels_in, sems.at[0]),
        pltpu.make_async_copy(potential, cells.at[1:3], sems.at[1]),
        pltpu.make_async_copy(codes, codes_in, sems.at[2]),
    ]
    for copy in copies:
        copy.start()
    lane = lanes()

    def packed(tiles, width, offset):
        total = jnp.zeros((8, 128), jnp.float32)
        for c, tile in enumerate(tiles):
            there = (lane >= width * c) & (lane < width * (c + 1))
            total = jnp.where(there, pltpu.roll(tile, (width * c + offset) % 128, 1), total)
        return total

    copies[0].wait()
    for p in range(32):
        cells[0, p] = labels_in[p].astype(jnp.float32)
    copies[2].wait()
    for e in range(SHIFT):
        codes_out[e] = codes_in[e].astype(jnp.float32)
    edges[9] = packed([codes_out[e] for e in range(SHIFT)], 8, 4)
    copies[1].wait()
    for f in range(3):
        for q in range(3):
            planes = range(PACK * q, min(PACK * q + PACK, 32))
            edges[3 * f + q] = packed([cells[f, p] for p in planes], 10, 5)


def second_pack(cells, codes, edges, across, own_lo, own_hi, up_lo, up_hi, grow):
    def put(lo, hi, place, tile):
        at, count = place
        if count:
            lo[at : at + count] = tile[0:count]
            hi[at : at + count] = tile[8 - count : 8]

    for f in range(3):
        for i in range(OWN):
            put(own_lo, own_hi, OWN_PLAN["cell", f, i], cells[f, i + 11])
            put(up_lo, up_hi, UP_PLAN["cell", f, i], cells[f, i])
            grow[f, i] = cells[f, i]
        for q in range(2):
            put(own_lo, own_hi, OWN_PLAN["edge", f, q], across[3 * f + q + 1])
            put(up_lo, up_hi, UP_PLAN["edge", f, q], across[3 * f + q])
            grow[f, OWN + q] = across[3 * f + q]
    for e in range(SHIFT):
        put(own_lo, own_hi, OWN_PLAN["code", 0, e], codes[e])
    put(own_lo, own_hi, OWN_PLAN["code_edge", 0, 0], across[9])
    for ref, rows, used in ((own_lo, OWN_ROWS, 334), (own_hi, OWN_ROWS, 334), (up_lo, UP_ROWS, 300), (up_hi, UP_ROWS, 300)):
        ref[used:rows] = jnp.zeros((rows - used, 128), jnp.float32)


def react(phases, sums, chem, chem_sums, held):
    p0, p1, p2 = phases
    p3 = K - ((p0 + p1) + p2)
    n3 = 6.0 * K - ((sums[0] + sums[1]) + sums[2])
    ps = (p0, p1, p2, p3)
    ns = (sums[0], sums[1], sums[2], n3)
    squares = [p * p for p in ps]
    base = (0.28 / 0.12) - ((squares[0] + squares[1]) + (squares[2] + squares[3]))
    m0, m1 = chem
    both = BETA * (m0 + m1)
    w2 = both + DRIFT
    ws = (w2 + (7.0 * BETA) * m0, w2 + (7.0 * BETA) * m1, w2, 3.5 * both)
    moved = [
        ns[a] + ps[a] * ((base + squares[a]) + ws[a] * (K - ps[a])) for a in range(4)
    ]
    excess = 0.25 * ((moved[0] + moved[1]) + (moved[2] + moved[3])) - 0.25 * TOP
    clipped = [jnp.minimum(jnp.maximum(u - excess, 0.0), TOP) for u in moved]
    scale = K / ((clipped[0] + clipped[1]) + (clipped[2] + clipped[3]))
    new = [s * scale for s in clipped]
    h = [x * x * (1.5 * K - x) for x in new]
    shared = (h[0] + h[1]) + (h[2] + 3.5 * h[3])
    solute = (shared + 7.0 * h[0], shared + 7.0 * h[1])
    mobility = 0.0075 + (0.1425 / K) * p3
    new_held = [held[i] + mobility * (chem_sums[i] - 6.0 * chem[i]) for i in range(2)]
    new_chem = [new_held[i] - solute[i] for i in range(2)]
    return new, new_chem, new_held


def evolve(
    where_ref, cells, codes, table_in, across, own_lo, own_hi, up_lo, up_hi, grow,
    phases_out, chem_out, one, two, table, sem,
):
    first = where_ref[0] == 0
    last = where_ref[0] == where_ref[1] - 1
    lane = lanes()

    def start(dst, z, p, rows, label, m0, m1):
        for a in range(3):
            dst[a, z, p, rows, :] = jnp.where(label == a, K, 0.0)
        melt = jnp.where(label == 3.0, 3.5 * HALF, HALF)
        for i, m in enumerate((m0, m1)):
            m = ALPHA * m
            dst[3 + i, z, p, rows, :] = m
            dst[5 + i, z, p, rows, :] = m + jnp.where(label == i, 8.0 * HALF, melt)

    def fill(dst, p):
        up = p >= OWN
        i = p - OWN if up else p
        q, c = divmod(i, PACK)
        places = UP_PLAN if up else OWN_PLAN
        for z in range(2):

            def turned(x, z=z):
                return pltpu.roll(x, (123 - 10 * c) % 128, 1) if z else x

            def inside(f, z=z):
                if up:
                    return grow[f, OWN + q] if z else grow[f, i]
                return across[3 * f + q + 1] if z else cells[f, i + 11]

            body = [turned(inside(f)) for f in range(3)]
            start(dst, z, p, slice(ROW0, ROW0 + 8), *body)
            for ref, hi in ((up_lo if up else own_lo, False), (up_hi if up else own_hi, True)):
                count = reach(i, up)
                if not count:
                    continue
                body = []
                for f in range(3):
                    at, held = places["edge", f, q] if z else places["cell", f, i]
                    skip = held - count if hi else 0
                    body.append(turned(ref[at + skip : at + skip + count]))
                row = ROW0 - count if hi else ROW0 + 8
                start(dst, z, p, slice(row, row + count), *body)

    def melt(dst, e):
        def chem(code, i):
            value = jnp.zeros_like(code)
            for level in range(8):
                value = jnp.where(code == level, table[i, level], value)
            return value

        for z in range(2):
            at, _ = OWN_PLAN["code_edge", 0, 0] if z else OWN_PLAN["code", 0, e]
            parts = (
                (across[9] if z else codes[e], ROW0, 8),
                (own_hi[at : at + 2], ROW0 - 2, 2),
                (own_lo[at : at + 2], ROW0 + 8, 2),
            )
            for code, row, count in parts:
                code = pltpu.roll(code, (124 - 8 * e) % 128, 1) if z else code
                label = jnp.full_like(code, 3.0)
                start(dst, z, OWN + e, slice(row, row + count), label, chem(code, 0), chem(code, 1))

    def repeat(ref, p, source):
        for f in range(5):
            for z in range(2):
                ref[f, z, p, 7:25, :] = ref[f, z, source, 7:25, :]

    def gather(src, f, z, p, row):
        rows = slice(row, row + 8)
        here = src[f, z, p, rows, :]
        there = src[f, 1 - z, p, rows, :]
        total = src[f, z, p - 1, rows, :] + src[f, z, p + 1, rows, :]
        total = total + (
            src[f, z, p, row - 1 : row + 7, :] + src[f, z, p, row + 1 : row + 9, :]
        )
        left = pltpu.roll(jnp.where(lane == 127, there, here), 1, 1)
        right = pltpu.roll(jnp.where(lane == 0, there, here), 127, 1)
        return here, total + (left + right)

    def tile_step(src, z, p, row):
        pairs = [gather(src, f, z, p, row) for f in range(5)]
        held = [src[f, z, p, row : row + 8, :] for f in (5, 6)]
        here = [a for a, _ in pairs]
        sums = [b for _, b in pairs]
        return react(here[:3], sums[:3], here[3:], sums[3:], held)

    def sweep(src, dst, s):
        count = PLANES - 2 * s

        @pl.loop(s, PLANES - s, unroll=4 if count % 4 == 0 else 2)
        def _(p):
            for z in range(2):
                for row in (8, 16):
                    new, chem, held = tile_step(src, z, p, row)
                    for f, value in enumerate((*new[:3], *chem, *held)):
                        dst[f, z, p, row : row + 8, :] = value

    for p in range(PLANES):
        fill(one, p)
    src, dst = one, two
    for s in range(1, 4):

        @pl.when(last)
        def _(src=src):
            repeat(src, OWN, OWN - 1)

        sweep(src, dst, s)
        src, dst = dst, src

    @pl.when(last)
    def _(src=src):
        copy = pltpu.make_async_copy(table_in, table, sem)
        copy.start()
        copy.wait()
        for e in range(SHIFT):
            melt(src, e)
        repeat(src, OWN + SHIFT, OWN + SHIFT - 1)

    @pl.when(first)
    def _(src=src):
        repeat(src, 4, 5)

    sweep(src, dst, 4)
    src, dst = dst, src

    @pl.when(last)
    def _(src=src):
        repeat(src, OWN + SHIFT, OWN + SHIFT - 1)

    @pl.when(first)
    def _(src=src):
        repeat(src, 4, 5)

    @pl.loop(5, PLANES - 5, unroll=4)
    def _(p):
        new, chem, _ = tile_step(src, 0, p, ROW0)
        for a in range(4):
            phases_out[a, p - 5] = new[a] * (1.0 / K)
        for i in range(2):
            chem_out[i, p - 5] = chem[i] * (1.0 / ALPHA)


def on_device(labels, potential, melt_codes, melt_table):
    n_grow, n_gy, n_gz = (lax.axis_size(a) for a in AXES)
    where = jnp.stack([lax.axis_index("grow"), n_grow]).astype(jnp.int32)

    def send(value, dg, dy, dz):
        pairs = []
        for g in range(max(0, -dg), n_grow):
            for y in range(n_gy):
                for z in range(n_gz):
                    to = ((g + dg) * n_gy + (y + dy) % n_gy) * n_gz + (z + dz) % n_gz
                    pairs.append(((g * n_gy + y) * n_gz + z, to))
        return lax.ppermute(value, AXES, pairs)

    def f32(*shape):
        return jax.ShapeDtypeStruct(shape, jnp.float32)

    params = pltpu.CompilerParams(vmem_limit_bytes=48 << 20)
    cells, codes, edges = pl.pallas_call(
        first_pack,
        in_specs=[HBM] * 3,
        out_specs=[VMEM] * 3,
        out_shape=[f32(3, 32, 8, 128), f32(SHIFT, 8, 128), f32(10, 8, 128)],
        scratch_shapes=[
            pltpu.VMEM((32, 8, 128), jnp.int32),
            pltpu.VMEM((SHIFT, 8, 128), jnp.int32),
            pltpu.SemaphoreType.DMA((3,)),
        ],
        compiler_params=params,
        name="first_pack",
    )(*(pltpu.with_memory_space_constraint(x, pltpu.MemorySpace.HBM) for x in (labels, potential, melt_codes)))
    across = send(edges, 0, 0, 1)
    own_lo, own_hi, up_lo, up_hi, grow = pl.pallas_call(
        second_pack,
        in_specs=[VMEM] * 4,
        out_specs=[VMEM] * 5,
        out_shape=[f32(OWN_ROWS, 128)] * 2 + [f32(UP_ROWS, 128)] * 2 + [f32(3, OWN + 2, 8, 128)],
        compiler_params=params,
        name="second_pack",
    )(cells, codes, edges, across)
    own_lo = send(own_lo, 0, -1, 0)
    own_hi = send(own_hi, 0, 1, 0)
    up_lo = send(up_lo, -1, -1, 0)
    up_hi = send(up_hi, -1, 1, 0)
    grow = send(grow, -1, 0, 0)
    held = pltpu.VMEM((7, 2, PLANES, PITCH, 128), jnp.float32)
    return pl.pallas_call(
        evolve,
        in_specs=[SMEM, VMEM, VMEM, HBM] + [VMEM] * 6,
        out_specs=[VMEM, VMEM],
        out_shape=[f32(4, 32, 8, 128), f32(2, 32, 8, 128)],
        scratch_shapes=[held, held, pltpu.SMEM((2, 8), jnp.float32), pltpu.SemaphoreType.DMA],
        compiler_params=params,
        name="evolve",
    )(where, cells, codes, pltpu.with_memory_space_constraint(melt_table, pltpu.MemorySpace.HBM), across, own_lo, own_hi, up_lo, up_hi, grow)


def solution(mesh):
    return jax.shard_map(
        on_device,
        mesh=mesh,
        in_specs=(P("grow", "gy", "gz"), P(None, "grow", "gy", "gz"), P(None, "gy", "gz"), P()),
        out_specs=(P(None, "grow", "gy", "gz"), P(None, "grow", "gy", "gz")),
        check_vma=False,
    )
```

```python
import jax
import jax.numpy as jnp
from jax import lax
from jax.experimental import pallas as pl
from jax.experimental.pallas import tpu as pltpu
from jax.sharding import PartitionSpec as P

K = 5.0**0.5
ALPHA = 5.0 * K**3
BETA = 2.5 / (K * ALPHA)
TOP = K / 0.12
DRIFT = 0.15 / (0.12 * K)
HALF = 0.5 * K**3

SHIFT = 16
OWN = 21
PLANES = 2 * OWN
PITCH = 32
ROW0 = 12
DEEP = 5
PACK = 11
AXES = ("grow", "gy", "gz")
VMEM = pl.BlockSpec(memory_space=pltpu.VMEM)
HBM = pl.BlockSpec(memory_space=pltpu.MemorySpace.HBM)
SMEM = pl.BlockSpec(memory_space=pltpu.SMEM)


def lanes():
    return lax.broadcasted_iota(jnp.int32, (8, 128), 1)


def reach(i, up):
    return min(DEEP, OWN - 1 - i if up else i)


def plan(up):
    places, at = {}, 8
    for f in range(3):
        for i in range(OWN):
            places["cell", f, i] = (at, reach(i, up))
            at += reach(i, up)
        for q in range(2):
            places["edge", f, q] = (at, DEEP)
            at += DEEP
    if not up:
        for e in range(SHIFT):
            places["code", 0, e] = (at, 2)
            at += 2
        places["code_edge", 0, 0] = (at, 2)
        at += 2
    return places, -(-at // 8) * 8


OWN_PLAN, OWN_ROWS = plan(False)
UP_PLAN, UP_ROWS = plan(True)


def first_pack(labels, potential, codes, cells, codes_out, edges, labels_in, codes_in, sems):
    copies = [
        pltpu.make_async_copy(labels, labels_in, sems.at[0]),
        pltpu.make_async_copy(potential, cells.at[1:3], sems.at[1]),
        pltpu.make_async_copy(codes, codes_in, sems.at[2]),
    ]
    for copy in copies:
        copy.start()
    lane = lanes()

    def packed(tiles, width, offset):
        total = jnp.zeros((8, 128), jnp.float32)
        for c, tile in enumerate(tiles):
            there = (lane >= width * c) & (lane < width * (c + 1))
            total = jnp.where(there, pltpu.roll(tile, (width * c + offset) % 128, 1), total)
        return total

    copies[0].wait()
    for p in range(32):
        cells[0, p] = labels_in[p].astype(jnp.float32)
    copies[2].wait()
    for e in range(SHIFT):
        codes_out[e] = codes_in[e].astype(jnp.float32)
    edges[9] = packed([codes_out[e] for e in range(SHIFT)], 8, 4)
    copies[1].wait()
    for f in range(3):
        for q in range(3):
            planes = range(PACK * q, min(PACK * q + PACK, 32))
            edges[3 * f + q] = packed([cells[f, p] for p in planes], 10, 5)


def put(lo, hi, place, tile):
    at, count = place
    if count:
        lo[at : at + count] = tile[0:count]
        hi[at : at + count] = tile[8 - count : 8]


def second_pack(cells, codes, across, own_lo, own_hi, grow):
    for f in range(3):
        for i in range(OWN):
            put(own_lo, own_hi, OWN_PLAN["cell", f, i], cells[f, i + 11])
            grow[f, i] = cells[f, i]
        for q in range(2):
            put(own_lo, own_hi, OWN_PLAN["edge", f, q], across[3 * f + q + 1])
            grow[f, OWN + q] = across[3 * f + q]
    for e in range(SHIFT):
        put(own_lo, own_hi, OWN_PLAN["code", 0, e], codes[e])
    put(own_lo, own_hi, OWN_PLAN["code_edge", 0, 0], across[9])
    for ref in (own_lo, own_hi):
        blank(ref, OWN_PLAN, OWN_ROWS)


def blank(ref, places, rows):
    used = max(at + count for at, count in places.values())
    ref[0:8] = jnp.zeros((8, 128), jnp.float32)
    ref[used:rows] = jnp.zeros((rows - used, 128), jnp.float32)


def third_pack(grow, up_lo, up_hi):
    for f in range(3):
        for i in range(OWN):
            put(up_lo, up_hi, UP_PLAN["cell", f, i], grow[f, i])
        for q in range(2):
            put(up_lo, up_hi, UP_PLAN["edge", f, q], grow[f, OWN + q])
    for ref in (up_lo, up_hi):
        blank(ref, UP_PLAN, UP_ROWS)


def react(phases, sums, chem, chem_sums, held):
    p0, p1, p2 = phases
    p3 = K - ((p0 + p1) + p2)
    n3 = 6.0 * K - ((sums[0] + sums[1]) + sums[2])
    ps = (p0, p1, p2, p3)
    ns = (sums[0], sums[1], sums[2], n3)
    squares = [p * p for p in ps]
    base = (0.28 / 0.12) - ((squares[0] + squares[1]) + (squares[2] + squares[3]))
    m0, m1 = chem
    both = BETA * (m0 + m1)
    w2 = both + DRIFT
    ws = (w2 + (7.0 * BETA) * m0, w2 + (7.0 * BETA) * m1, w2, 3.5 * both)
    moved = [
        ns[a] + ps[a] * ((base + squares[a]) + ws[a] * (K - ps[a])) for a in range(4)
    ]
    excess = 0.25 * ((moved[0] + moved[1]) + (moved[2] + moved[3])) - 0.25 * TOP
    clipped = [jnp.minimum(jnp.maximum(u - excess, 0.0), TOP) for u in moved]
    scale = K / ((clipped[0] + clipped[1]) + (clipped[2] + clipped[3]))
    new = [s * scale for s in clipped]
    h = [x * x * (1.5 * K - x) for x in new]
    shared = (h[0] + h[1]) + (h[2] + 3.5 * h[3])
    solute = (shared + 7.0 * h[0], shared + 7.0 * h[1])
    mobility = 0.0075 + (0.1425 / K) * p3
    new_held = [held[i] + mobility * (chem_sums[i] - 6.0 * chem[i]) for i in range(2)]
    new_chem = [new_held[i] - solute[i] for i in range(2)]
    return new, new_chem, new_held


class Half:
    def __init__(self, base, strip_base, n, cells, codes, across, own, up, grow, lane):
        self.base, self.strip_base, self.n = base, strip_base, n
        self.cells, self.codes, self.across = cells, codes, across
        self.own, self.up, self.grow, self.lane = own, up, grow, lane

    def source(self, p):
        up = p >= OWN
        i = p - OWN if up else p
        q, c = divmod(i, PACK)
        return up, i, q, c

    def store(self, dst, index, rows, label, m0, m1, mask=None):
        values = [jnp.where(label == a, K, 0.0) for a in range(3)]
        rest = jnp.where(label == 3.0, 3.5 * HALF, HALF)
        values += [ALPHA * m0, ALPHA * m1]
        values += [values[3 + i] + jnp.where(label == i, 8.0 * HALF, rest) for i in range(2)]
        for f, value in enumerate(values):
            if mask is not None:
                value = jnp.where(mask, value, dst[f, index, rows, :])
            dst[f, index, rows, :] = value

    def fill(self, dst, p):
        up, i, _, _ = self.source(p)
        body = [self.grow[f, i] if up else self.cells[f, i + 11] for f in range(3)]
        self.store(dst, p - self.base, slice(ROW0, ROW0 + 8), *body)
        for hi, ref in enumerate(self.up if up else self.own):
            count = reach(i, up)
            if count:
                places = UP_PLAN if up else OWN_PLAN
                body = []
                for f in range(3):
                    at, _ = places["cell", f, i]
                    body.append(ref[at : at + count])
                row = ROW0 - count if hi else ROW0 + 8
                self.store(dst, p - self.base, slice(row, row + count), *body)

    def pieces(self, p, f, block):
        up, i, q, _ = self.source(p)
        if block == 0:
            if up:
                return self.grow[f, i], self.grow[f, OWN + q]
            return self.cells[f, i + 11], self.across[3 * f + q + 1]
        places = UP_PLAN if up else OWN_PLAN
        ref = (self.up if up else self.own)[block - 1]
        at, count = places["cell", f, i]
        at = at if block == 1 else at + count - DEEP
        edge, _ = places["edge", f, q]
        return ref[at : at + DEEP], ref[edge : edge + DEEP]

    def joined(self, parts):
        rows = next(part for part in parts if part is not None)[0].shape[0]
        lane = lax.broadcasted_iota(jnp.int32, (rows, 128), 1)
        total = jnp.zeros((rows, 128), jnp.float32)
        for j, part in enumerate(parts):
            if part is None:
                continue
            value, edge, before, after = part
            at = 20 * j
            tile = jnp.where(
                lane < at + 10,
                jnp.where(lane < at + 5, pltpu.roll(edge, before % 128, 1), pltpu.roll(value, at + 5, 1)),
                jnp.where(lane < at + 15, pltpu.roll(value, (at + 15) % 128, 1), pltpu.roll(edge, after % 128, 1)),
            )
            total = jnp.where(lane >= at, tile, total)
        return total

    def fill_strips(self, dst, top):
        for index in range(self.n):
            for block, row, _ in BLOCKS:
                body = []
                for f in range(3):
                    parts = []
                    for j in range(6):
                        p = self.strip_base + self.n * j + index
                        if p >= top:
                            parts.append(None)
                            continue
                        c = self.source(p)[3]
                        parts.append(
                            (*self.pieces(p, f, block), 20 * j - 10 * c, 20 * j + 10 - 10 * c)
                        )
                    body.append(self.joined(parts))
                self.store(dst, index, slice(row, row + body[0].shape[0]), *body)

    def melt(self, dst, strips, table):
        def chem(code, i):
            value = jnp.zeros_like(code)
            for level in range(8):
                value = jnp.where(code == level, table[i, level], value)
            return value

        def rows(block, e):
            if block == 0:
                return self.codes[e], self.across[9]
            ref = self.own[block - 1]
            at, _ = OWN_PLAN["code", 0, e]
            edge, _ = OWN_PLAN["code_edge", 0, 0]
            return ref[at : at + 2], ref[edge : edge + 2]

        for e in range(SHIFT):
            for block, row, count in MELT_BLOCKS:
                code = rows(block, e)[0]
                label = jnp.full_like(code, 3.0)
                where = slice(row, row + count)
                self.store(dst, OWN + e - self.base, where, label, chem(code, 0), chem(code, 1))
        for index in range(self.n):
            for block, row, count in MELT_BLOCKS:
                parts, groups = [], []
                for j in range(6):
                    e = self.strip_base + self.n * j + index - OWN
                    if not 0 <= e < SHIFT:
                        parts.append(None)
                        continue
                    groups.append(j)
                    parts.append((*rows(block, e), 20 * j + 1 - 8 * e, 20 * j + 11 - 8 * e))
                code = self.joined(parts)
                lane = lax.broadcasted_iota(jnp.int32, code.shape, 1)
                mask = (lane >= 20 * groups[0]) & (lane < 20 * groups[-1] + 20)
                label = jnp.full_like(code, 3.0)
                where = slice(row, row + count)
                self.store(strips, index, where, label, chem(code, 0), chem(code, 1), mask)

    def repeat(self, dst, p, source):
        for f in range(5):
            dst[f, p - self.base, 7:25, :] = dst[f, source - self.base, 7:25, :]

    def repeat_strip(self, strips, p, source):
        j, index = divmod(p - self.strip_base, self.n)
        j_from, index_from = divmod(source - self.strip_base, self.n)
        lane = lax.broadcasted_iota(jnp.int32, (18, 128), 1)
        mask = (lane >= 20 * j) & (lane < 20 * j + 20)
        for f in range(5):
            value = strips[f, index_from, 7:25, :]
            if j != j_from:
                value = pltpu.roll(value, 20 * (j - j_from), 1)
            strips[f, index, 7:25, :] = jnp.where(mask, value, strips[f, index, 7:25, :])

    def advance(self, src, index, row, fetch, sides):
        here, sums = [], []
        for f in range(5):
            mid = src[f, index, row : row + 8, :]
            below, above = fetch(f)
            total = (below + above) + (
                src[f, index, row - 1 : row + 7, :] + src[f, index, row + 1 : row + 9, :]
            )
            left, right = sides(f, pltpu.roll(mid, 1, 1), pltpu.roll(mid, 127, 1))
            here.append(mid)
            sums.append(total + (left + right))
        held = [src[f, index, row : row + 8, :] for f in (5, 6)]
        return react(here[:3], sums[:3], here[3:], sums[3:], held)

    def plane_step(self, src, strips, p, row):
        index = p - self.base
        q = p - self.strip_base
        j = (q * 13) >> 6 if self.n == 5 else q >> 2
        at = q - self.n * j
        to_first, to_last = 124 - 20 * j, 112 - 20 * j
        rows = slice(row, row + 8)

        def fetch(f):
            return src[f, index - 1, rows, :], src[f, index + 1, rows, :]

        def sides(f, left, right):
            strip = strips[f, at, rows, :]
            left = jnp.where(self.lane == 0, pltpu.roll(strip, to_first, 1), left)
            return left, jnp.where(self.lane == 127, pltpu.roll(strip, to_last, 1), right)

        return self.advance(src, index, row, fetch, sides)

    def planes(self, first, count, body):
        whole = count - count % 4
        if whole:
            pl.loop(first, first + whole, unroll=4)(body)
        for p in range(first + whole, first + count):
            body(p)

    def sweep(self, src, dst, src_strips, dst_strips, first, count):
        def body(p):
            for row in (8, 16):
                new, chem, held = self.plane_step(src, src_strips, p, row)
                for f, value in enumerate((*new[:3], *chem, *held)):
                    dst[f, p - self.base, row : row + 8, :] = value

        self.planes(first, count, body)
        last = self.n - 1
        for index in range(self.n):
            for row in (8, 16):
                rows = slice(row, row + 8)

                def fetch(f, index=index, rows=rows):
                    if index:
                        below = src_strips[f, index - 1, rows, :]
                    else:
                        below = pltpu.roll(src_strips[f, last, rows, :], 20, 1)
                    if index < last:
                        above = src_strips[f, index + 1, rows, :]
                    else:
                        above = pltpu.roll(src_strips[f, 0, rows, :], 108, 1)
                    return below, above

                new, chem, held = self.advance(
                    src_strips, index, row, fetch, lambda f, left, right: (left, right)
                )
                for f, value in enumerate((*new[:3], *chem, *held)):
                    dst_strips[f, index, row : row + 8, :] = value

    def finish(self, src, strips, first, count, phases, chems):
        def body(p):
            new, chem, _ = self.plane_step(src, strips, p, ROW0)
            for a in range(4):
                phases[a, p - first] = new[a] * (1.0 / K)
            for i in range(2):
                chems[i, p - first] = chem[i] * (1.0 / ALPHA)

        self.planes(first, count, body)


BLOCKS = ((0, ROW0, 8), (1, ROW0 + 8, DEEP), (2, ROW0 - DEEP, DEEP))
MELT_BLOCKS = ((0, ROW0, 8), (1, ROW0 + 8, 2), (2, ROW0 - 2, 2))
LOWER = 11


def lower_half(
    where_ref, cells, codes, across, own_lo, own_hi, phases_out, chem_out, seam,
    one, two, strip_one, strip_two, phases, chems, sems,
):
    first = where_ref[0] == 0
    half = Half(0, 0, 4, cells, codes, across, (own_lo, own_hi), None, None, lanes())
    for p in range(OWN):
        half.fill(one, p)
    half.fill_strips(strip_one, OWN)
    src, dst, src_strips, dst_strips = one, two, strip_one, strip_two
    for s in range(1, 5):
        if s == 4:

            @pl.when(first)
            def _(src=src, src_strips=src_strips):
                half.repeat(src, 4, 5)
                half.repeat_strip(src_strips, 4, 5)

        half.sweep(src, dst, src_strips, dst_strips, s, OWN - 2 * s)
        for f in range(7):
            for i in range(2):
                seam[s - 1, f, i] = dst[f, OWN - 1 - s + i - 1, 8:24, :]
        src, dst, src_strips, dst_strips = dst, src, dst_strips, src_strips

    @pl.when(first)
    def _(src=src):
        half.repeat(src, 4, 5)

    half.finish(src, src_strips, 5, LOWER, phases, chems)
    deliver(phases, chems, phases_out, chem_out, 0, LOWER, sems)


def deliver(phases, chems, phases_out, chem_out, first, count, sems):
    copies = [
        pltpu.make_async_copy(phases, phases_out.at[:, pl.ds(first, count)], sems.at[0]),
        pltpu.make_async_copy(chems, chem_out.at[:, pl.ds(first, count)], sems.at[1]),
    ]
    for copy in copies:
        copy.start()
    for copy in copies:
        copy.wait()


def upper_half(
    where_ref, cells, codes, table_in, across, own_lo, own_hi, up_lo, up_hi, grow, seam,
    phases_in, chem_in, phases_out, chem_out,
    one, two, strip_one, strip_two, phases, chems, table, sem, sems,
):
    del phases_in, chem_in
    last = where_ref[0] == where_ref[1] - 1
    half = Half(
        15, 12, 5, cells, codes, across, (own_lo, own_hi), (up_lo, up_hi), grow, lanes()
    )
    for p in range(OWN - 2, PLANES):
        half.fill(one, p)
    half.fill_strips(strip_one, PLANES)
    src, dst, src_strips, dst_strips = one, two, strip_one, strip_two
    for s in range(1, 6):
        if s > 1:
            for f in range(7):
                for i in range(2):
                    src[f, OWN - 1 - s + i - half.base, 8:24, :] = seam[s - 2, f, i]
        if s < 4:

            @pl.when(last)
            def _(src=src, src_strips=src_strips):
                half.repeat(src, OWN, OWN - 1)
                half.repeat_strip(src_strips, OWN, OWN - 1)

        if s == 4:

            @pl.when(last)
            def _(src=src, src_strips=src_strips):
                copy = pltpu.make_async_copy(table_in, table, sem)
                copy.start()
                copy.wait()
                half.melt(src, src_strips, table)
                half.repeat_strip(src_strips, OWN + SHIFT, OWN + SHIFT - 1)

        if s >= 4:

            @pl.when(last)
            def _(src=src):
                half.repeat(src, OWN + SHIFT, OWN + SHIFT - 1)

        if s < 5:
            half.sweep(src, dst, src_strips, dst_strips, OWN - s, OWN)
            src, dst, src_strips, dst_strips = dst, src, dst_strips, src_strips
    half.finish(src, src_strips, OWN - 5, OWN, phases, chems)
    deliver(phases, chems, phases_out, chem_out, LOWER, OWN, sems)


def on_device(labels, potential, melt_codes, melt_table):
    n_grow, n_gy, n_gz = (lax.axis_size(a) for a in AXES)
    where = jnp.stack([lax.axis_index("grow"), n_grow]).astype(jnp.int32)

    def send(value, dg, dy, dz):
        pairs = []
        for g in range(max(0, -dg), n_grow):
            for y in range(n_gy):
                for z in range(n_gz):
                    to = ((g + dg) * n_gy + (y + dy) % n_gy) * n_gz + (z + dz) % n_gz
                    pairs.append(((g * n_gy + y) * n_gz + z, to))
        return lax.ppermute(value, AXES, pairs)

    def f32(*shape):
        return jax.ShapeDtypeStruct(shape, jnp.float32)

    params = pltpu.CompilerParams(vmem_limit_bytes=48 << 20)
    cells, codes, edges = pl.pallas_call(
        first_pack,
        in_specs=[HBM] * 3,
        out_specs=[VMEM] * 3,
        out_shape=[f32(3, 32, 8, 128), f32(SHIFT, 8, 128), f32(10, 8, 128)],
        scratch_shapes=[
            pltpu.VMEM((32, 8, 128), jnp.int32),
            pltpu.VMEM((SHIFT, 8, 128), jnp.int32),
            pltpu.SemaphoreType.DMA((3,)),
        ],
        compiler_params=params,
        name="first_pack",
    )(*(pltpu.with_memory_space_constraint(x, pltpu.MemorySpace.HBM) for x in (labels, potential, melt_codes)))
    across = send(edges, 0, 0, 1)
    own_lo, own_hi, grow = pl.pallas_call(
        second_pack,
        in_specs=[VMEM] * 3,
        out_specs=[VMEM] * 3,
        out_shape=[f32(OWN_ROWS, 128)] * 2 + [f32(3, OWN + 2, 8, 128)],
        compiler_params=params,
        name="second_pack",
    )(cells, codes, across)
    own_lo = send(own_lo, 0, -1, 0)
    own_hi = send(own_hi, 0, 1, 0)
    grow = send(grow, -1, 0, 0)
    up_lo, up_hi = pl.pallas_call(
        third_pack,
        in_specs=[VMEM],
        out_specs=[VMEM] * 2,
        out_shape=[f32(UP_ROWS, 128)] * 2,
        compiler_params=params,
        name="third_pack",
    )(grow)
    up_lo = send(up_lo, 0, -1, 0)
    up_hi = send(up_hi, 0, 1, 0)

    def buffers(planes, strips, count):
        return (
            [pltpu.VMEM((7, planes, PITCH, 128), jnp.float32)] * 2
            + [pltpu.VMEM((7, strips, PITCH, 128), jnp.float32)] * 2
            + [pltpu.VMEM((4, count, 8, 128), jnp.float32)]
            + [pltpu.VMEM((2, count, 8, 128), jnp.float32)]
        )

    outputs = [f32(4, 32, 8, 128), f32(2, 32, 8, 128)]
    phases, chems, seam = pl.pallas_call(
        lower_half,
        in_specs=[SMEM] + [VMEM] * 5,
        out_specs=[HBM, HBM, VMEM],
        out_shape=outputs + [f32(4, 7, 2, 16, 128)],
        scratch_shapes=buffers(OWN, 4, LOWER) + [pltpu.SemaphoreType.DMA((2,))],
        compiler_params=params,
        cost_estimate=pl.CostEstimate(
            flops=60_000_000, bytes_accessed=12_000_000, transcendentals=0
        ),
        name="lower_half",
    )(where, cells, codes, across, own_lo, own_hi)
    table = pltpu.with_memory_space_constraint(melt_table, pltpu.MemorySpace.HBM)
    return pl.pallas_call(
        upper_half,
        in_specs=[SMEM, VMEM, VMEM, HBM] + [VMEM] * 7 + [HBM, HBM],
        out_specs=[HBM, HBM],
        out_shape=outputs,
        scratch_shapes=buffers(27, 5, OWN)
        + [pltpu.SMEM((2, 8), jnp.float32), pltpu.SemaphoreType.DMA, pltpu.SemaphoreType.DMA((2,))],
        input_output_aliases={11: 0, 12: 1},
        compiler_params=params,
        name="upper_half",
    )(where, cells, codes, table, across, own_lo, own_hi, up_lo, up_hi, grow, seam, phases, chems)


def solution(mesh):
    return jax.shard_map(
        on_device,
        mesh=mesh,
        in_specs=(P("grow", "gy", "gz"), P(None, "grow", "gy", "gz"), P(None, "gy", "gz"), P()),
        out_specs=(P(None, "grow", "gy", "gz"), P(None, "grow", "gy", "gz")),
        check_vma=False,
    )
```

```python
import jax
import jax.numpy as jnp
from jax import lax
from jax.experimental import pallas as pl
from jax.experimental.pallas import tpu as pltpu
from jax.sharding import PartitionSpec as P

K = 5.0**0.5
ALPHA = 5.0 * K**3
BETA = 2.5 / (K * ALPHA)
TOP = K / 0.12
DRIFT = 0.15 / (0.12 * K)
HALF = 0.5 * K**3

SHIFT = 16
OWN = 21
PLANES = 2 * OWN
PITCH = 32
ROW0 = 12
DEEP = 5
PACK = 11
AXES = ("grow", "gy", "gz")
VMEM = pl.BlockSpec(memory_space=pltpu.VMEM)
HBM = pl.BlockSpec(memory_space=pltpu.MemorySpace.HBM)
SMEM = pl.BlockSpec(memory_space=pltpu.SMEM)


def lanes():
    return lax.broadcasted_iota(jnp.int32, (8, 128), 1)


def reach(i, up):
    return min(DEEP, OWN - 1 - i if up else i)


def plan(up):
    places, at = {}, 8
    for f in range(3):
        for i in range(OWN):
            places["cell", f, i] = (at, reach(i, up))
            at += reach(i, up)
        for q in range(2):
            places["edge", f, q] = (at, DEEP)
            at += DEEP
    if not up:
        for e in range(SHIFT):
            places["code", 0, e] = (at, 2)
            at += 2
        places["code_edge", 0, 0] = (at, 2)
        at += 2
    return places, -(-at // 8) * 8


OWN_PLAN, OWN_ROWS = plan(False)
UP_PLAN, UP_ROWS = plan(True)


def first_pack(labels, potential, codes, cells, codes_out, edges, labels_in, codes_in, sems):
    copies = [
        pltpu.make_async_copy(labels, labels_in, sems.at[0]),
        pltpu.make_async_copy(potential, cells.at[1:3], sems.at[1]),
        pltpu.make_async_copy(codes, codes_in, sems.at[2]),
    ]
    for copy in copies:
        copy.start()
    lane = lanes()

    def packed(tiles, width, offset):
        total = jnp.zeros((8, 128), jnp.float32)
        for c, tile in enumerate(tiles):
            there = (lane >= width * c) & (lane < width * (c + 1))
            total = jnp.where(there, pltpu.roll(tile, (width * c + offset) % 128, 1), total)
        return total

    copies[0].wait()
    for p in range(32):
        cells[0, p] = labels_in[p].astype(jnp.float32)
    copies[2].wait()
    for e in range(SHIFT):
        codes_out[e] = codes_in[e].astype(jnp.float32)
    edges[9] = packed([codes_out[e] for e in range(SHIFT)], 8, 4)
    copies[1].wait()
    for f in range(3):
        for q in range(3):
            planes = range(PACK * q, min(PACK * q + PACK, 32))
            edges[3 * f + q] = packed([cells[f, p] for p in planes], 10, 5)


def put(lo, hi, place, tile):
    at, count = place
    if count:
        lo[at : at + count] = tile[0:count]
        hi[at : at + count] = tile[8 - count : 8]


def second_pack(cells, codes, across, own_lo, own_hi, grow):
    for f in range(3):
        for i in range(OWN):
            put(own_lo, own_hi, OWN_PLAN["cell", f, i], cells[f, i + 11])
            grow[f, i] = cells[f, i]
        for q in range(2):
            put(own_lo, own_hi, OWN_PLAN["edge", f, q], across[3 * f + q + 1])
            grow[f, OWN + q] = across[3 * f + q]
    for e in range(SHIFT):
        put(own_lo, own_hi, OWN_PLAN["code", 0, e], codes[e])
    put(own_lo, own_hi, OWN_PLAN["code_edge", 0, 0], across[9])
    for ref in (own_lo, own_hi):
        blank(ref, OWN_PLAN, OWN_ROWS)


def blank(ref, places, rows):
    used = max(at + count for at, count in places.values())
    ref[0:8] = jnp.zeros((8, 128), jnp.float32)
    ref[used:rows] = jnp.zeros((rows - used, 128), jnp.float32)


def third_pack(grow, up_lo, up_hi):
    for f in range(3):
        for i in range(OWN):
            put(up_lo, up_hi, UP_PLAN["cell", f, i], grow[f, i])
        for q in range(2):
            put(up_lo, up_hi, UP_PLAN["edge", f, q], grow[f, OWN + q])
    for ref in (up_lo, up_hi):
        blank(ref, UP_PLAN, UP_ROWS)


def react(phases, sums, chem, chem_sums, held):
    p0, p1, p2, p3 = phases
    n3 = 6.0 * K - ((sums[0] + sums[1]) + sums[2])
    ps = (p0, p1, p2, p3)
    ns = (sums[0], sums[1], sums[2], n3)
    squares = [p * p for p in ps]
    base = (0.28 / 0.12) - ((squares[0] + squares[1]) + (squares[2] + squares[3]))
    m0, m1 = chem
    both = BETA * (m0 + m1)
    w2 = both + DRIFT
    ws = (w2 + (7.0 * BETA) * m0, w2 + (7.0 * BETA) * m1, w2, 3.5 * both)
    moved = [
        ns[a] + ps[a] * ((base + squares[a]) + ws[a] * (K - ps[a])) for a in range(4)
    ]
    excess = 0.25 * ((moved[0] + moved[1]) + (moved[2] + moved[3])) - 0.25 * TOP
    clipped = [jnp.minimum(jnp.maximum(u - excess, 0.0), TOP) for u in moved]
    scale = K / ((clipped[0] + clipped[1]) + (clipped[2] + clipped[3]))
    new = [s * scale for s in clipped]
    h = [x * x * (1.5 * K - x) for x in new]
    shared = (h[0] + h[1]) + (h[2] + 3.5 * h[3])
    solute = (shared + 7.0 * h[0], shared + 7.0 * h[1])
    mobility = 0.0075 + (0.1425 / K) * p3
    new_held = [held[i] + mobility * (chem_sums[i] - 6.0 * chem[i]) for i in range(2)]
    new_chem = [new_held[i] - solute[i] for i in range(2)]
    return new, new_chem, new_held


class Half:
    def __init__(self, base, strip_base, n, cells, codes, across, own, up, grow, wing):
        self.base, self.strip_base, self.n = base, strip_base, n
        self.cells, self.codes, self.across = cells, codes, across
        self.own, self.up, self.grow, self.wing, self.lane = own, up, grow, wing, lanes()

    def source(self, p):
        up = p >= OWN
        i = p - OWN if up else p
        q, c = divmod(i, PACK)
        return up, i, q, c

    def store(self, dst, index, rows, label, m0, m1, mask=None):
        values = [jnp.where(label == a, K, 0.0) for a in range(3)]
        rest = jnp.where(label == 3.0, 3.5 * HALF, HALF)
        values += [ALPHA * m0, ALPHA * m1]
        values += [values[3 + i] + jnp.where(label == i, 8.0 * HALF, rest) for i in range(2)]
        values.append(jnp.where(label == 3.0, K, 0.0))
        for f, value in enumerate(values):
            if mask is not None:
                value = jnp.where(mask, value, dst[f, index, rows, :])
            dst[f, index, rows, :] = value

    def fill(self, dst, p):
        up, i, _, _ = self.source(p)
        body = [self.grow[f, i] if up else self.cells[f, i + 11] for f in range(3)]
        self.store(dst, p - self.base, slice(ROW0, ROW0 + 8), *body)
        for hi, ref in enumerate(self.up if up else self.own):
            count = reach(i, up)
            if count:
                places = UP_PLAN if up else OWN_PLAN
                body = []
                for f in range(3):
                    at, _ = places["cell", f, i]
                    body.append(ref[at : at + count])
                row = ROW0 - count if hi else ROW0 + 8
                self.store(dst, p - self.base, slice(row, row + count), *body)

    def pieces(self, p, f, block):
        up, i, q, _ = self.source(p)
        if block == 0:
            if up:
                return self.grow[f, i], self.grow[f, OWN + q]
            return self.cells[f, i + 11], self.across[3 * f + q + 1]
        places = UP_PLAN if up else OWN_PLAN
        ref = (self.up if up else self.own)[block - 1]
        at, count = places["cell", f, i]
        at = at if block == 1 else at + count - DEEP
        edge, _ = places["edge", f, q]
        return ref[at : at + DEEP], ref[edge : edge + DEEP]

    def joined(self, parts):
        rows = next(part for part in parts if part is not None)[0].shape[0]
        lane = lax.broadcasted_iota(jnp.int32, (rows, 128), 1)
        total = jnp.zeros((rows, 128), jnp.float32)
        for j, part in enumerate(parts):
            if part is None:
                continue
            value, edge, before, after = part
            at = 20 * j
            tile = jnp.where(
                lane < at + 10,
                jnp.where(lane < at + 5, pltpu.roll(edge, before % 128, 1), pltpu.roll(value, at + 5, 1)),
                jnp.where(lane < at + 15, pltpu.roll(value, (at + 15) % 128, 1), pltpu.roll(edge, after % 128, 1)),
            )
            total = jnp.where(lane >= at, tile, total)
        return total

    def fill_strips(self, dst, top):
        for index in range(self.n):
            for block, row, _ in BLOCKS:
                body = []
                for f in range(3):
                    parts = []
                    for j in range(6):
                        p = self.strip_base + self.n * j + index
                        if p >= top:
                            parts.append(None)
                            continue
                        c = self.source(p)[3]
                        parts.append(
                            (*self.pieces(p, f, block), 20 * j - 10 * c, 20 * j + 10 - 10 * c)
                        )
                    body.append(self.joined(parts))
                self.store(dst, index, slice(row, row + body[0].shape[0]), *body)

    def melt(self, dst, strips, table):
        def chem(code, i):
            value = jnp.zeros_like(code)
            for level in range(8):
                value = jnp.where(code == level, table[i, level], value)
            return value

        def rows(block, e):
            if block == 0:
                return self.codes[e], self.across[9]
            ref = self.own[block - 1]
            at, _ = OWN_PLAN["code", 0, e]
            edge, _ = OWN_PLAN["code_edge", 0, 0]
            return ref[at : at + 2], ref[edge : edge + 2]

        for e in range(SHIFT):
            for block, row, count in MELT_BLOCKS:
                code = rows(block, e)[0]
                label = jnp.full_like(code, 3.0)
                where = slice(row, row + count)
                self.store(dst, OWN + e - self.base, where, label, chem(code, 0), chem(code, 1))
        for index in range(self.n):
            for block, row, count in MELT_BLOCKS:
                parts, groups = [], []
                for j in range(6):
                    e = self.strip_base + self.n * j + index - OWN
                    if not 0 <= e < SHIFT:
                        parts.append(None)
                        continue
                    groups.append(j)
                    parts.append((*rows(block, e), 20 * j + 1 - 8 * e, 20 * j + 11 - 8 * e))
                code = self.joined(parts)
                lane = lax.broadcasted_iota(jnp.int32, code.shape, 1)
                mask = (lane >= 20 * groups[0]) & (lane < 20 * groups[-1] + 20)
                label = jnp.full_like(code, 3.0)
                where = slice(row, row + count)
                self.store(strips, index, where, label, chem(code, 0), chem(code, 1), mask)

    def repeat(self, dst, p, source):
        for f in range(5):
            dst[f, p - self.base, 7:25, :] = dst[f, source - self.base, 7:25, :]

    def repeat_strip(self, strips, p, source):
        j, index = divmod(p - self.strip_base, self.n)
        j_from, index_from = divmod(source - self.strip_base, self.n)
        lane = lax.broadcasted_iota(jnp.int32, (18, 128), 1)
        mask = (lane >= 20 * j) & (lane < 20 * j + 20)
        for f in range(5):
            value = strips[f, index_from, 7:25, :]
            if j != j_from:
                value = pltpu.roll(value, 20 * (j - j_from), 1)
            strips[f, index, 7:25, :] = jnp.where(mask, value, strips[f, index, 7:25, :])

    def advance(self, src, index, row, fetch, sides):
        here, sums = [], []
        for f in range(5):
            mid = src[f, index, row : row + 8, :]
            below, above = fetch(f)
            total = (below + above) + (
                src[f, index, row - 1 : row + 7, :] + src[f, index, row + 1 : row + 9, :]
            )
            left, right = sides(f, mid)
            here.append(mid)
            sums.append(total + (left + right))
        held = [src[f, index, row : row + 8, :] for f in (5, 6)]
        liquid = src[7, index, row : row + 8, :]
        return react((*here[:3], liquid), sums[:3], here[3:], sums[3:], held)

    def spread(self, strips, rows):
        second = self.lane == 5
        for j in range(1, 6):
            second = second | (self.lane == 20 * j + 5)
        for f in range(5):
            for index in range(self.n):
                for row in rows:
                    tile = strips[f, index, row : row + 8, :]
                    tile = jnp.where(second, pltpu.roll(tile, 118, 1), tile)
                    self.wing[f, index, row : row + 8, :] = tile

    def plane_step(self, src, p, row):
        index = p - self.base
        q = p - self.strip_base
        j = (q * 13) >> 6 if self.n == 5 else q >> 2
        at = q - self.n * j
        turn = 123 - 20 * j
        rows = slice(row, row + 8)

        def fetch(f):
            return src[f, index - 1, rows, :], src[f, index + 1, rows, :]

        def sides(f, mid):
            beyond = pltpu.roll(self.wing[f, at, rows, :], turn, 1)
            left = jnp.where(self.lane == 127, beyond, mid)
            right = jnp.where(self.lane == 0, beyond, mid)
            return pltpu.roll(left, 1, 1), pltpu.roll(right, 127, 1)

        return self.advance(src, index, row, fetch, sides)

    def planes(self, first, count, body):
        whole = count - count % 4
        if whole:
            pl.loop(first, first + whole, unroll=4)(body)
        for p in range(first + whole, first + count):
            body(p)

    def sweep(self, src, dst, src_strips, dst_strips, first, count):
        self.spread(src_strips, (8, 16))

        def body(p):
            for row in (8, 16):
                new, chem, held = self.plane_step(src, p, row)
                for f, value in enumerate((*new[:3], *chem, *held, new[3])):
                    dst[f, p - self.base, row : row + 8, :] = value

        self.planes(first, count, body)
        last = self.n - 1

        def inside(f, mid):
            return pltpu.roll(mid, 1, 1), pltpu.roll(mid, 127, 1)

        for index in range(self.n):
            for row in (8, 16):
                rows = slice(row, row + 8)

                def fetch(f, index=index, rows=rows):
                    if index:
                        below = src_strips[f, index - 1, rows, :]
                    else:
                        below = pltpu.roll(src_strips[f, last, rows, :], 20, 1)
                    if index < last:
                        above = src_strips[f, index + 1, rows, :]
                    else:
                        above = pltpu.roll(src_strips[f, 0, rows, :], 108, 1)
                    return below, above

                new, chem, held = self.advance(
                    src_strips, index, row, fetch, inside
                )
                for f, value in enumerate((*new[:3], *chem, *held, new[3])):
                    dst_strips[f, index, row : row + 8, :] = value

    def finish(self, src, first, count, phases, chems, at=0):
        def body(p):
            new, chem, _ = self.plane_step(src, p, ROW0)
            for a in range(4):
                phases[a, p - first + at] = new[a] * (1.0 / K)
            for i in range(2):
                chems[i, p - first + at] = chem[i] * (1.0 / ALPHA)

        self.planes(first, count, body)


BLOCKS = ((0, ROW0, 8), (1, ROW0 + 8, DEEP), (2, ROW0 - DEEP, DEEP))
MELT_BLOCKS = ((0, ROW0, 8), (1, ROW0 + 8, 2), (2, ROW0 - 2, 2))
LOWER = 11


def lower_half(
    where_ref, cells, codes, across, own_lo, own_hi, phases, chems, seam,
    one, two, strip_one, strip_two, wing,
):
    first = where_ref[0] == 0
    half = Half(0, 0, 4, cells, codes, across, (own_lo, own_hi), None, None, wing)
    for p in range(OWN):
        half.fill(one, p)
    half.fill_strips(strip_one, OWN)
    src, dst, src_strips, dst_strips = one, two, strip_one, strip_two
    for s in range(1, 5):
        if s == 4:

            @pl.when(first)
            def _(src=src, src_strips=src_strips):
                half.repeat(src, 4, 5)
                half.repeat_strip(src_strips, 4, 5)

        half.sweep(src, dst, src_strips, dst_strips, s, OWN - 2 * s)
        for f in range(8):
            for i in range(2):
                seam[s - 1, f, i] = dst[f, OWN - 1 - s + i - 1, 8:24, :]
        src, dst, src_strips, dst_strips = dst, src, dst_strips, src_strips

    @pl.when(first)
    def _(src=src):
        half.repeat(src, 4, 5)

    half.spread(src_strips, (ROW0,))
    half.finish(src, 5, LOWER, phases, chems)


def delivery(phases, chems, phases_out, chem_out, first, at, count, sems, s):
    source, target = pl.ds(at, count), pl.ds(first, count)
    copies = [
        pltpu.make_async_copy(phases.at[:, source], phases_out.at[:, target], sems.at[s]),
        pltpu.make_async_copy(chems.at[:, source], chem_out.at[:, target], sems.at[s + 1]),
    ]
    for copy in copies:
        copy.start()
    return copies


def upper_half(
    where_ref, cells, codes, table_in, across, own_lo, own_hi, up_lo, up_hi, grow, seam,
    lower_phases, lower_chems, phases_out, chem_out,
    one, two, strip_one, strip_two, wing, phases, chems, table, sem, sems,
):
    outs = (phases_out, chem_out)
    copies = delivery(lower_phases, lower_chems, *outs, 0, 0, LOWER, sems, 0)
    last = where_ref[0] == where_ref[1] - 1
    half = Half(
        15, 12, 5, cells, codes, across, (own_lo, own_hi), (up_lo, up_hi), grow, wing
    )
    for p in range(OWN - 2, PLANES):
        half.fill(one, p)
    half.fill_strips(strip_one, PLANES)
    src, dst, src_strips, dst_strips = one, two, strip_one, strip_two
    for s in range(1, 6):
        if s > 1:
            for f in range(8):
                for i in range(2):
                    src[f, OWN - 1 - s + i - half.base, 8:24, :] = seam[s - 2, f, i]
        if s < 4:

            @pl.when(last)
            def _(src=src, src_strips=src_strips):
                half.repeat(src, OWN, OWN - 1)
                half.repeat_strip(src_strips, OWN, OWN - 1)

        if s == 4:

            @pl.when(last)
            def _(src=src, src_strips=src_strips):
                copy = pltpu.make_async_copy(table_in, table, sem)
                copy.start()
                copy.wait()
                half.melt(src, src_strips, table)
                half.repeat_strip(src_strips, OWN + SHIFT, OWN + SHIFT - 1)

        if s >= 4:

            @pl.when(last)
            def _(src=src):
                half.repeat(src, OWN + SHIFT, OWN + SHIFT - 1)

        if s < 5:
            half.sweep(src, dst, src_strips, dst_strips, OWN - s, OWN)
            src, dst, src_strips, dst_strips = dst, src, dst_strips, src_strips
    half.spread(src_strips, (ROW0,))
    half.finish(src, OWN - 5, 12, phases, chems)
    copies += delivery(phases, chems, *outs, LOWER, 0, 12, sems, 2)
    half.finish(src, OWN + 7, 9, phases, chems, 12)
    copies += delivery(phases, chems, *outs, LOWER + 12, 12, 9, sems, 4)
    for copy in copies:
        copy.wait()


def on_device(labels, potential, melt_codes, melt_table):
    n_grow, n_gy, n_gz = (lax.axis_size(a) for a in AXES)
    where = jnp.stack([lax.axis_index("grow"), n_grow]).astype(jnp.int32)

    def send(value, dg, dy, dz):
        pairs = []
        for g in range(max(0, -dg), n_grow):
            for y in range(n_gy):
                for z in range(n_gz):
                    to = ((g + dg) * n_gy + (y + dy) % n_gy) * n_gz + (z + dz) % n_gz
                    pairs.append(((g * n_gy + y) * n_gz + z, to))
        return lax.ppermute(value, AXES, pairs)

    def f32(*shape):
        return jax.ShapeDtypeStruct(shape, jnp.float32)

    params = pltpu.CompilerParams(vmem_limit_bytes=48 << 20)
    cells, codes, edges = pl.pallas_call(
        first_pack,
        in_specs=[HBM] * 3,
        out_specs=[VMEM] * 3,
        out_shape=[f32(3, 32, 8, 128), f32(SHIFT, 8, 128), f32(10, 8, 128)],
        scratch_shapes=[
            pltpu.VMEM((32, 8, 128), jnp.int32),
            pltpu.VMEM((SHIFT, 8, 128), jnp.int32),
            pltpu.SemaphoreType.DMA((3,)),
        ],
        compiler_params=params,
        name="first_pack",
    )(*(pltpu.with_memory_space_constraint(x, pltpu.MemorySpace.HBM) for x in (labels, potential, melt_codes)))
    across = send(edges, 0, 0, 1)
    own_lo, own_hi, grow = pl.pallas_call(
        second_pack,
        in_specs=[VMEM] * 3,
        out_specs=[VMEM] * 3,
        out_shape=[f32(OWN_ROWS, 128)] * 2 + [f32(3, OWN + 2, 8, 128)],
        compiler_params=params,
        name="second_pack",
    )(cells, codes, across)
    own_lo = send(own_lo, 0, -1, 0)
    own_hi = send(own_hi, 0, 1, 0)
    grow = send(grow, -1, 0, 0)
    up_lo, up_hi = pl.pallas_call(
        third_pack,
        in_specs=[VMEM],
        out_specs=[VMEM] * 2,
        out_shape=[f32(UP_ROWS, 128)] * 2,
        compiler_params=params,
        name="third_pack",
    )(grow)
    up_lo = send(up_lo, 0, -1, 0)
    up_hi = send(up_hi, 0, 1, 0)

    def buffers(planes, strips):
        return (
            [pltpu.VMEM((8, planes, PITCH, 128), jnp.float32)] * 2
            + [pltpu.VMEM((8, strips, PITCH, 128), jnp.float32)] * 2
            + [pltpu.VMEM((5, strips, PITCH, 128), jnp.float32)]
        )

    phases, chems, seam = pl.pallas_call(
        lower_half,
        in_specs=[SMEM] + [VMEM] * 5,
        out_specs=[VMEM] * 3,
        out_shape=[f32(4, LOWER, 8, 128), f32(2, LOWER, 8, 128), f32(4, 8, 2, 16, 128)],
        scratch_shapes=buffers(OWN, 4),
        compiler_params=params,
        cost_estimate=pl.CostEstimate(
            flops=60_000_000, bytes_accessed=12_000_000, transcendentals=0
        ),
        name="lower_half",
    )(where, cells, codes, across, own_lo, own_hi)
    table = pltpu.with_memory_space_constraint(melt_table, pltpu.MemorySpace.HBM)
    return pl.pallas_call(
        upper_half,
        in_specs=[SMEM, VMEM, VMEM, HBM] + [VMEM] * 9,
        out_specs=[HBM, HBM],
        out_shape=[f32(4, 32, 8, 128), f32(2, 32, 8, 128)],
        scratch_shapes=buffers(27, 5)
        + [
            pltpu.VMEM((4, OWN, 8, 128), jnp.float32),
            pltpu.VMEM((2, OWN, 8, 128), jnp.float32),
            pltpu.SMEM((2, 8), jnp.float32),
            pltpu.SemaphoreType.DMA,
            pltpu.SemaphoreType.DMA((6,)),
        ],
        compiler_params=params,
        name="upper_half",
    )(where, cells, codes, table, across, own_lo, own_hi, up_lo, up_hi, grow, seam, phases, chems)


def solution(mesh):
    return jax.shard_map(
        on_device,
        mesh=mesh,
        in_specs=(P("grow", "gy", "gz"), P(None, "grow", "gy", "gz"), P(None, "gy", "gz"), P()),
        out_specs=(P(None, "grow", "gy", "gz"), P(None, "grow", "gy", "gz")),
        check_vma=False,
    )
```

```python
import jax
import jax.numpy as jnp
from jax import lax
from jax.experimental import pallas as pl
from jax.experimental.pallas import tpu as pltpu
from jax.sharding import PartitionSpec as P

K = 5.0**0.5
ALPHA = 5.0 * K**3
BETA = 2.5 / (K * ALPHA)
TOP = K / 0.12
DRIFT = 0.15 / (0.12 * K)
HALF = 0.5 * K**3

SHIFT = 16
OWN = 21
PLANES = 2 * OWN
PITCH = 32
ROW0 = 12
DEEP = 5
PACK = 11
AXES = ("grow", "gy", "gz")
VMEM = pl.BlockSpec(memory_space=pltpu.VMEM)
HBM = pl.BlockSpec(memory_space=pltpu.MemorySpace.HBM)
SMEM = pl.BlockSpec(memory_space=pltpu.SMEM)


def lanes():
    return lax.broadcasted_iota(jnp.int32, (8, 128), 1)


def reach(i, up):
    return min(DEEP, OWN - 1 - i if up else i)


def plan(up):
    places, at = {}, 8
    for f in range(3):
        for i in range(OWN):
            places["cell", f, i] = (at, reach(i, up))
            at += reach(i, up)
        for q in range(2):
            places["edge", f, q] = (at, DEEP)
            at += DEEP
    if not up:
        for e in range(SHIFT):
            places["code", 0, e] = (at, 2)
            at += 2
        places["code_edge", 0, 0] = (at, 2)
        at += 2
    return places, -(-at // 8) * 8


OWN_PLAN, OWN_ROWS = plan(False)
UP_PLAN, UP_ROWS = plan(True)


def first_pack(labels, potential, codes, cells, codes_out, edges, labels_in, codes_in, sems):
    copies = [
        pltpu.make_async_copy(labels, labels_in, sems.at[0]),
        pltpu.make_async_copy(potential, cells.at[1:3], sems.at[1]),
        pltpu.make_async_copy(codes, codes_in, sems.at[2]),
    ]
    for copy in copies:
        copy.start()
    lane = lanes()

    def packed(tiles, width, offset):
        total = jnp.zeros((8, 128), jnp.float32)
        for c, tile in enumerate(tiles):
            there = (lane >= width * c) & (lane < width * (c + 1))
            total = jnp.where(there, pltpu.roll(tile, (width * c + offset) % 128, 1), total)
        return total

    copies[0].wait()
    for p in range(32):
        cells[0, p] = labels_in[p].astype(jnp.float32)
    copies[2].wait()
    for e in range(SHIFT):
        codes_out[e] = codes_in[e].astype(jnp.float32)
    edges[9] = packed([codes_out[e] for e in range(SHIFT)], 8, 4)
    copies[1].wait()
    for f in range(3):
        for q in range(3):
            planes = range(PACK * q, min(PACK * q + PACK, 32))
            edges[3 * f + q] = packed([cells[f, p] for p in planes], 10, 5)


def put(lo, hi, place, tile):
    at, count = place
    if count:
        lo[at : at + count] = tile[0:count]
        hi[at : at + count] = tile[8 - count : 8]


def second_pack(cells, codes, across, own_lo, own_hi, grow):
    for f in range(3):
        for i in range(OWN):
            put(own_lo, own_hi, OWN_PLAN["cell", f, i], cells[f, i + 11])
            grow[f, i] = cells[f, i]
        for q in range(2):
            put(own_lo, own_hi, OWN_PLAN["edge", f, q], across[3 * f + q + 1])
            grow[f, OWN + q] = across[3 * f + q]
    for e in range(SHIFT):
        put(own_lo, own_hi, OWN_PLAN["code", 0, e], codes[e])
    put(own_lo, own_hi, OWN_PLAN["code_edge", 0, 0], across[9])
    for ref in (own_lo, own_hi):
        blank(ref, OWN_PLAN, OWN_ROWS)


def blank(ref, places, rows):
    used = max(at + count for at, count in places.values())
    ref[0:8] = jnp.zeros((8, 128), jnp.float32)
    ref[used:rows] = jnp.zeros((rows - used, 128), jnp.float32)


def third_pack(grow, up_lo, up_hi):
    for f in range(3):
        for i in range(OWN):
            put(up_lo, up_hi, UP_PLAN["cell", f, i], grow[f, i])
        for q in range(2):
            put(up_lo, up_hi, UP_PLAN["edge", f, q], grow[f, OWN + q])
    for ref in (up_lo, up_hi):
        blank(ref, UP_PLAN, UP_ROWS)


def react(phases, sums, chem, chem_sums, held):
    p0, p1, p2 = phases
    p3 = K - ((p0 + p1) + p2)
    n3 = 6.0 * K - ((sums[0] + sums[1]) + sums[2])
    ps = (p0, p1, p2, p3)
    ns = (sums[0], sums[1], sums[2], n3)
    squares = [p * p for p in ps]
    base = (0.28 / 0.12) - ((squares[0] + squares[1]) + (squares[2] + squares[3]))
    m0, m1 = chem
    both = BETA * (m0 + m1)
    w2 = both + DRIFT
    ws = (w2 + (7.0 * BETA) * m0, w2 + (7.0 * BETA) * m1, w2, 3.5 * both)
    moved = [
        ns[a] + ps[a] * ((base + squares[a]) + ws[a] * (K - ps[a])) for a in range(4)
    ]
    excess = 0.25 * ((moved[0] + moved[1]) + (moved[2] + moved[3])) - 0.25 * TOP
    clipped = [jnp.minimum(jnp.maximum(u - excess, 0.0), TOP) for u in moved]
    scale = K / ((clipped[0] + clipped[1]) + (clipped[2] + clipped[3]))
    new = [s * scale for s in clipped]
    h = [x * x * (1.5 * K - x) for x in new]
    shared = (h[0] + h[1]) + (h[2] + 3.5 * h[3])
    solute = (shared + 7.0 * h[0], shared + 7.0 * h[1])
    mobility = 0.0075 + (0.1425 / K) * p3
    new_held = [held[i] + mobility * (chem_sums[i] - 6.0 * chem[i]) for i in range(2)]
    new_chem = [new_held[i] - solute[i] for i in range(2)]
    return new, new_chem, new_held


class Half:
    def __init__(self, base, strip_base, n, cells, codes, across, own, up, grow, wing):
        self.base, self.strip_base, self.n = base, strip_base, n
        self.cells, self.codes, self.across = cells, codes, across
        self.own, self.up, self.grow, self.wing, self.lane = own, up, grow, wing, lanes()

    def source(self, p):
        up = p >= OWN
        i = p - OWN if up else p
        q, c = divmod(i, PACK)
        return up, i, q, c

    def store(self, dst, index, rows, label, m0, m1, mask=None):
        values = [jnp.where(label == a, K, 0.0) for a in range(3)]
        rest = jnp.where(label == 3.0, 3.5 * HALF, HALF)
        values += [ALPHA * m0, ALPHA * m1]
        values += [values[3 + i] + jnp.where(label == i, 8.0 * HALF, rest) for i in range(2)]
        for f, value in enumerate(values):
            if mask is not None:
                value = jnp.where(mask, value, dst[f, index, rows, :])
            dst[f, index, rows, :] = value

    def fill(self, dst, p):
        up, i, _, _ = self.source(p)
        body = [self.grow[f, i] if up else self.cells[f, i + 11] for f in range(3)]
        self.store(dst, p - self.base, slice(ROW0, ROW0 + 8), *body)
        for hi, ref in enumerate(self.up if up else self.own):
            count = reach(i, up)
            if count:
                places = UP_PLAN if up else OWN_PLAN
                body = []
                for f in range(3):
                    at, _ = places["cell", f, i]
                    body.append(ref[at : at + count])
                row = ROW0 - count if hi else ROW0 + 8
                self.store(dst, p - self.base, slice(row, row + count), *body)

    def pieces(self, p, f, block):
        up, i, q, _ = self.source(p)
        if block == 0:
            if up:
                return self.grow[f, i], self.grow[f, OWN + q]
            return self.cells[f, i + 11], self.across[3 * f + q + 1]
        places = UP_PLAN if up else OWN_PLAN
        ref = (self.up if up else self.own)[block - 1]
        at, count = places["cell", f, i]
        at = at if block == 1 else at + count - DEEP
        edge, _ = places["edge", f, q]
        return ref[at : at + DEEP], ref[edge : edge + DEEP]

    def joined(self, parts):
        rows = next(part for part in parts if part is not None)[0].shape[0]
        lane = lax.broadcasted_iota(jnp.int32, (rows, 128), 1)
        total = jnp.zeros((rows, 128), jnp.float32)
        for j, part in enumerate(parts):
            if part is None:
                continue
            value, edge, before, after = part
            at = 20 * j
            tile = jnp.where(
                lane < at + 10,
                jnp.where(lane < at + 5, pltpu.roll(edge, before % 128, 1), pltpu.roll(value, at + 5, 1)),
                jnp.where(lane < at + 15, pltpu.roll(value, (at + 15) % 128, 1), pltpu.roll(edge, after % 128, 1)),
            )
            total = jnp.where(lane >= at, tile, total)
        return total

    def fill_strips(self, dst, top):
        for index in range(self.n):
            for block, row, _ in BLOCKS:
                body = []
                for f in range(3):
                    parts = []
                    for j in range(6):
                        p = self.strip_base + self.n * j + index
                        if p >= top:
                            parts.append(None)
                            continue
                        c = self.source(p)[3]
                        parts.append(
                            (*self.pieces(p, f, block), 20 * j - 10 * c, 20 * j + 10 - 10 * c)
                        )
                    body.append(self.joined(parts))
                self.store(dst, index, slice(row, row + body[0].shape[0]), *body)

    def melt(self, dst, strips, table):
        def chem(code, i):
            value = jnp.zeros_like(code)
            for level in range(8):
                value = jnp.where(code == level, table[i, level], value)
            return value

        def rows(block, e):
            if block == 0:
                return self.codes[e], self.across[9]
            ref = self.own[block - 1]
            at, _ = OWN_PLAN["code", 0, e]
            edge, _ = OWN_PLAN["code_edge", 0, 0]
            return ref[at : at + 2], ref[edge : edge + 2]

        for e in range(SHIFT):
            for block, row, count in MELT_BLOCKS:
                code = rows(block, e)[0]
                label = jnp.full_like(code, 3.0)
                where = slice(row, row + count)
                self.store(dst, OWN + e - self.base, where, label, chem(code, 0), chem(code, 1))
        for index in range(self.n):
            for block, row, count in MELT_BLOCKS:
                parts, groups = [], []
                for j in range(6):
                    e = self.strip_base + self.n * j + index - OWN
                    if not 0 <= e < SHIFT:
                        parts.append(None)
                        continue
                    groups.append(j)
                    parts.append((*rows(block, e), 20 * j + 1 - 8 * e, 20 * j + 11 - 8 * e))
                code = self.joined(parts)
                lane = lax.broadcasted_iota(jnp.int32, code.shape, 1)
                mask = (lane >= 20 * groups[0]) & (lane < 20 * groups[-1] + 20)
                label = jnp.full_like(code, 3.0)
                where = slice(row, row + count)
                self.store(strips, index, where, label, chem(code, 0), chem(code, 1), mask)

    def repeat(self, dst, p, source):
        for f in range(5):
            dst[f, p - self.base, 7:25, :] = dst[f, source - self.base, 7:25, :]

    def repeat_strip(self, strips, p, source):
        j, index = divmod(p - self.strip_base, self.n)
        j_from, index_from = divmod(source - self.strip_base, self.n)
        lane = lax.broadcasted_iota(jnp.int32, (18, 128), 1)
        mask = (lane >= 20 * j) & (lane < 20 * j + 20)
        for f in range(5):
            value = strips[f, index_from, 7:25, :]
            if j != j_from:
                value = pltpu.roll(value, 20 * (j - j_from), 1)
            strips[f, index, 7:25, :] = jnp.where(mask, value, strips[f, index, 7:25, :])

    def advance(self, src, index, row, fetch, sides):
        here, sums = [], []
        for f in range(5):
            mid = src[f, index, row : row + 8, :]
            below, above = fetch(f)
            total = (below + above) + (
                src[f, index, row - 1 : row + 7, :] + src[f, index, row + 1 : row + 9, :]
            )
            left, right = sides(f, mid)
            here.append(mid)
            sums.append(total + (left + right))
        held = [src[f, index, row : row + 8, :] for f in (5, 6)]
        return react(here[:3], sums[:3], here[3:], sums[3:], held)

    def spread(self, strips, rows):
        second = self.lane == 3
        for j in range(1, 6):
            second = second | (self.lane == 20 * j + 3)
        for f in range(5):
            for index in range(self.n):
                for row in rows:
                    tile = strips[f, index, row : row + 8, :]
                    tile = jnp.where(second, pltpu.roll(tile, 116, 1), tile)
                    self.wing[f, index, row : row + 8, :] = tile

    def plane_step(self, src, p, row):
        index = p - self.base
        q = p - self.strip_base
        j = (q * 13) >> 6 if self.n == 5 else q >> 2
        at = q - self.n * j
        turn = 124 - 20 * j
        rows = slice(row, row + 8)

        def fetch(f):
            return src[f, index - 1, rows, :], src[f, index + 1, rows, :]

        def sides(f, mid):
            beyond = pltpu.roll(self.wing[f, at, rows, :], turn, 1)
            left = jnp.where(self.lane == 0, beyond, pltpu.roll(mid, 1, 1))
            return left, jnp.where(self.lane == 127, beyond, pltpu.roll(mid, 127, 1))

        return self.advance(src, index, row, fetch, sides)

    def planes(self, first, count, body):
        whole = count - count % 8
        if whole:
            pl.loop(first, first + whole, unroll=8)(body)
        for p in range(first + whole, first + count):
            body(p)

    def sweep(self, src, dst, src_strips, dst_strips, first, count):
        self.spread(src_strips, (8, 16))

        def body(p):
            for row in (8, 16):
                new, chem, held = self.plane_step(src, p, row)
                for f, value in enumerate((*new[:3], *chem, *held)):
                    dst[f, p - self.base, row : row + 8, :] = value

        self.planes(first, count, body)
        last = self.n - 1

        def inside(f, mid):
            return pltpu.roll(mid, 1, 1), pltpu.roll(mid, 127, 1)

        for index in range(self.n):
            for row in (8, 16):
                rows = slice(row, row + 8)

                def fetch(f, index=index, rows=rows):
                    if index:
                        below = src_strips[f, index - 1, rows, :]
                    else:
                        below = pltpu.roll(src_strips[f, last, rows, :], 20, 1)
                    if index < last:
                        above = src_strips[f, index + 1, rows, :]
                    else:
                        above = pltpu.roll(src_strips[f, 0, rows, :], 108, 1)
                    return below, above

                new, chem, held = self.advance(
                    src_strips, index, row, fetch, inside
                )
                for f, value in enumerate((*new[:3], *chem, *held)):
                    dst_strips[f, index, row : row + 8, :] = value

    def finish(self, src, first, count, phases, chems, at=0):
        def body(p):
            new, chem, _ = self.plane_step(src, p, ROW0)
            for a in range(4):
                phases[a, p - first + at] = new[a] * (1.0 / K)
            for i in range(2):
                chems[i, p - first + at] = chem[i] * (1.0 / ALPHA)

        self.planes(first, count, body)


BLOCKS = ((0, ROW0, 8), (1, ROW0 + 8, DEEP), (2, ROW0 - DEEP, DEEP))
MELT_BLOCKS = ((0, ROW0, 8), (1, ROW0 + 8, 2), (2, ROW0 - 2, 2))
LOWER = 11


def lower_half(
    where_ref, cells, codes, across, own_lo, own_hi, phases, chems, seam,
    one, two, strip_one, strip_two, wing,
):
    first = where_ref[0] == 0
    half = Half(0, 0, 4, cells, codes, across, (own_lo, own_hi), None, None, wing)
    for p in range(OWN):
        half.fill(one, p)
    half.fill_strips(strip_one, OWN)
    src, dst, src_strips, dst_strips = one, two, strip_one, strip_two
    for s in range(1, 5):
        if s == 4:

            @pl.when(first)
            def _(src=src, src_strips=src_strips):
                half.repeat(src, 4, 5)
                half.repeat_strip(src_strips, 4, 5)

        half.sweep(src, dst, src_strips, dst_strips, s, OWN - 2 * s)
        for f in range(7):
            for i in range(2):
                seam[s - 1, f, i] = dst[f, OWN - 1 - s + i - 1, 8:24, :]
        src, dst, src_strips, dst_strips = dst, src, dst_strips, src_strips

    @pl.when(first)
    def _(src=src):
        half.repeat(src, 4, 5)

    half.spread(src_strips, (ROW0,))
    half.finish(src, 5, LOWER, phases, chems)


def delivery(phases, chems, phases_out, chem_out, first, at, count, sems, s):
    source, target = pl.ds(at, count), pl.ds(first, count)
    copies = [
        pltpu.make_async_copy(phases.at[:, source], phases_out.at[:, target], sems.at[s]),
        pltpu.make_async_copy(chems.at[:, source], chem_out.at[:, target], sems.at[s + 1]),
    ]
    for copy in copies:
        copy.start()
    return copies


def upper_half(
    where_ref, cells, codes, table_in, across, own_lo, own_hi, up_lo, up_hi, grow, seam,
    lower_phases, lower_chems, phases_out, chem_out,
    one, two, strip_one, strip_two, wing, phases, chems, table, sem, sems,
):
    outs = (phases_out, chem_out)
    copies = delivery(lower_phases, lower_chems, *outs, 0, 0, LOWER, sems, 0)
    last = where_ref[0] == where_ref[1] - 1
    half = Half(
        15, 12, 5, cells, codes, across, (own_lo, own_hi), (up_lo, up_hi), grow, wing
    )
    for p in range(OWN - 2, PLANES):
        half.fill(one, p)
    half.fill_strips(strip_one, PLANES)
    src, dst, src_strips, dst_strips = one, two, strip_one, strip_two
    for s in range(1, 6):
        if s > 1:
            for f in range(7):
                for i in range(2):
                    src[f, OWN - 1 - s + i - half.base, 8:24, :] = seam[s - 2, f, i]
        if s < 4:

            @pl.when(last)
            def _(src=src, src_strips=src_strips):
                half.repeat(src, OWN, OWN - 1)
                half.repeat_strip(src_strips, OWN, OWN - 1)

        if s == 4:

            @pl.when(last)
            def _(src=src, src_strips=src_strips):
                copy = pltpu.make_async_copy(table_in, table, sem)
                copy.start()
                copy.wait()
                half.melt(src, src_strips, table)
                half.repeat_strip(src_strips, OWN + SHIFT, OWN + SHIFT - 1)

        if s >= 4:

            @pl.when(last)
            def _(src=src):
                half.repeat(src, OWN + SHIFT, OWN + SHIFT - 1)

        if s < 5:
            half.sweep(src, dst, src_strips, dst_strips, OWN - s, OWN)
            src, dst, src_strips, dst_strips = dst, src, dst_strips, src_strips
    half.spread(src_strips, (ROW0,))
    half.finish(src, OWN - 5, 12, phases, chems)
    copies += delivery(phases, chems, *outs, LOWER, 0, 12, sems, 2)
    half.finish(src, OWN + 7, 9, phases, chems, 12)
    copies += delivery(phases, chems, *outs, LOWER + 12, 12, 9, sems, 4)
    for copy in copies:
        copy.wait()


def on_device(labels, potential, melt_codes, melt_table):
    n_grow, n_gy, n_gz = (lax.axis_size(a) for a in AXES)
    where = jnp.stack([lax.axis_index("grow"), n_grow]).astype(jnp.int32)

    def send(value, dg, dy, dz):
        pairs = []
        for g in range(max(0, -dg), n_grow):
            for y in range(n_gy):
                for z in range(n_gz):
                    to = ((g + dg) * n_gy + (y + dy) % n_gy) * n_gz + (z + dz) % n_gz
                    pairs.append(((g * n_gy + y) * n_gz + z, to))
        return lax.ppermute(value, AXES, pairs)

    def f32(*shape):
        return jax.ShapeDtypeStruct(shape, jnp.float32)

    params = pltpu.CompilerParams(vmem_limit_bytes=48 << 20)
    cells, codes, edges = pl.pallas_call(
        first_pack,
        in_specs=[HBM] * 3,
        out_specs=[VMEM] * 3,
        out_shape=[f32(3, 32, 8, 128), f32(SHIFT, 8, 128), f32(10, 8, 128)],
        scratch_shapes=[
            pltpu.VMEM((32, 8, 128), jnp.int32),
            pltpu.VMEM((SHIFT, 8, 128), jnp.int32),
            pltpu.SemaphoreType.DMA((3,)),
        ],
        compiler_params=params,
        name="first_pack",
    )(*(pltpu.with_memory_space_constraint(x, pltpu.MemorySpace.HBM) for x in (labels, potential, melt_codes)))
    across = send(edges, 0, 0, 1)
    own_lo, own_hi, grow = pl.pallas_call(
        second_pack,
        in_specs=[VMEM] * 3,
        out_specs=[VMEM] * 3,
        out_shape=[f32(OWN_ROWS, 128)] * 2 + [f32(3, OWN + 2, 8, 128)],
        compiler_params=params,
        name="second_pack",
    )(cells, codes, across)
    own_lo = send(own_lo, 0, -1, 0)
    own_hi = send(own_hi, 0, 1, 0)
    grow = send(grow, -1, 0, 0)
    up_lo, up_hi = pl.pallas_call(
        third_pack,
        in_specs=[VMEM],
        out_specs=[VMEM] * 2,
        out_shape=[f32(UP_ROWS, 128)] * 2,
        compiler_params=params,
        name="third_pack",
    )(grow)
    up_lo = send(up_lo, 0, -1, 0)
    up_hi = send(up_hi, 0, 1, 0)

    def buffers(planes, strips):
        return (
            [pltpu.VMEM((7, planes, PITCH, 128), jnp.float32)] * 2
            + [pltpu.VMEM((7, strips, PITCH, 128), jnp.float32)] * 2
            + [pltpu.VMEM((5, strips, PITCH, 128), jnp.float32)]
        )

    phases, chems, seam = pl.pallas_call(
        lower_half,
        in_specs=[SMEM] + [VMEM] * 5,
        out_specs=[VMEM] * 3,
        out_shape=[f32(4, LOWER, 8, 128), f32(2, LOWER, 8, 128), f32(4, 7, 2, 16, 128)],
        scratch_shapes=buffers(OWN, 4),
        compiler_params=params,
        cost_estimate=pl.CostEstimate(
            flops=60_000_000, bytes_accessed=12_000_000, transcendentals=0
        ),
        name="lower_half",
    )(where, cells, codes, across, own_lo, own_hi)
    table = pltpu.with_memory_space_constraint(melt_table, pltpu.MemorySpace.HBM)
    return pl.pallas_call(
        upper_half,
        in_specs=[SMEM, VMEM, VMEM, HBM] + [VMEM] * 9,
        out_specs=[HBM, HBM],
        out_shape=[f32(4, 32, 8, 128), f32(2, 32, 8, 128)],
        scratch_shapes=buffers(27, 5)
        + [
            pltpu.VMEM((4, OWN, 8, 128), jnp.float32),
            pltpu.VMEM((2, OWN, 8, 128), jnp.float32),
            pltpu.SMEM((2, 8), jnp.float32),
            pltpu.SemaphoreType.DMA,
            pltpu.SemaphoreType.DMA((6,)),
        ],
        compiler_params=params,
        name="upper_half",
    )(where, cells, codes, table, across, own_lo, own_hi, up_lo, up_hi, grow, seam, phases, chems)


def solution(mesh):
    return jax.shard_map(
        on_device,
        mesh=mesh,
        in_specs=(P("grow", "gy", "gz"), P(None, "grow", "gy", "gz"), P(None, "gy", "gz"), P()),
        out_specs=(P(None, "grow", "gy", "gz"), P(None, "grow", "gy", "gz")),
        check_vma=False,
    )
```

```python
import jax
import jax.numpy as jnp
from jax import lax
from jax.experimental import pallas as pl
from jax.experimental.pallas import tpu as pltpu
from jax.sharding import PartitionSpec as P

K = 5.0**0.5
ALPHA = 5.0 * K**3
BETA = 2.5 / (K * ALPHA)
TOP = K / 0.12
DRIFT = 0.15 / (0.12 * K)
HALF = 0.5 * K**3

SHIFT = 16
OWN = 21
PLANES = 2 * OWN
PITCH = 32
ROW0 = 12
DEEP = 5
PACK = 11
AXES = ("grow", "gy", "gz")
VMEM = pl.BlockSpec(memory_space=pltpu.VMEM)
ANY = pl.BlockSpec(memory_space=pl.ANY)
HBM = pl.BlockSpec(memory_space=pltpu.MemorySpace.HBM)
SMEM = pl.BlockSpec(memory_space=pltpu.SMEM)


def lanes():
    return lax.broadcasted_iota(jnp.int32, (8, 128), 1)


def reach(i, up):
    return min(DEEP, OWN - 1 - i if up else i)


def plan(up):
    places, at = {}, 8
    for f in range(3):
        for i in range(OWN):
            places["cell", f, i] = (at, reach(i, up))
            at += reach(i, up)
        for q in range(2):
            places["edge", f, q] = (at, DEEP)
            at += DEEP
    return places, -(-at // 8) * 8


OWN_PLAN, OWN_ROWS = plan(False)
UP_PLAN, UP_ROWS = plan(True)
CODE_PLAN = {("code", 0, e): (8 + 2 * e, 2) for e in range(SHIFT)}
CODE_PLAN["code_edge", 0, 0] = (8 + 2 * SHIFT, 2)


def first_pack(labels, potential, codes, cells, codes_out, edges, labels_in, codes_in, sems):
    copies = [
        pltpu.make_async_copy(labels, labels_in, sems.at[0]),
        pltpu.make_async_copy(potential, cells.at[1:3], sems.at[1]),
        pltpu.make_async_copy(codes, codes_in, sems.at[2]),
    ]
    for copy in copies:
        copy.start()
    lane = lanes()

    def packed(tiles, width, offset):
        total = jnp.zeros((8, 128), jnp.float32)
        for c, tile in enumerate(tiles):
            there = (lane >= width * c) & (lane < width * (c + 1))
            total = jnp.where(there, pltpu.roll(tile, (width * c + offset) % 128, 1), total)
        return total

    copies[0].wait()
    for p in range(32):
        cells[0, p] = labels_in[p].astype(jnp.float32)
    copies[2].wait()
    for e in range(SHIFT):
        codes_out[e] = codes_in[e].astype(jnp.float32)
    edges[9] = packed([codes_out[e] for e in range(SHIFT)], 8, 4)
    copies[1].wait()
    for f in range(3):
        for q in range(3):
            planes = range(PACK * q, min(PACK * q + PACK, 32))
            edges[3 * f + q] = packed([cells[f, p] for p in planes], 10, 5)


def put(lo, hi, place, tile):
    at, count = place
    if count:
        lo[at : at + count] = tile[0:count]
        hi[at : at + count] = tile[8 - count : 8]


def second_pack(cells, across, own_lo, own_hi):
    for f in range(3):
        for i in range(OWN):
            put(own_lo, own_hi, OWN_PLAN["cell", f, i], cells[f, i + 11])
        for q in range(2):
            put(own_lo, own_hi, OWN_PLAN["edge", f, q], across[3 * f + q + 1])
    for ref in (own_lo, own_hi):
        blank(ref, OWN_PLAN, OWN_ROWS)


def grow_pack(cells, across, after_lo, after_hi, grow):
    del after_lo, after_hi
    for f in range(3):
        grow[f, 0:OWN] = cells[f, 0:OWN]
        grow[f, OWN : OWN + 2] = across[3 * f : 3 * f + 2]


def blank(ref, places, rows):
    used = max(at + count for at, count in places.values())
    ref[0:8] = jnp.zeros((8, 128), jnp.float32)
    if used < rows:
        ref[used:rows] = jnp.zeros((rows - used, 128), jnp.float32)


def third_pack(where_ref, grow, codes, across, up_lo, up_hi):
    last = where_ref[0] == where_ref[1] - 1
    for ref in (up_lo, up_hi):
        blank(ref, UP_PLAN, UP_ROWS)

    @pl.when(jnp.logical_not(last))
    def _():
        for f in range(3):
            for i in range(OWN):
                put(up_lo, up_hi, UP_PLAN["cell", f, i], grow[f, i])
            for q in range(2):
                put(up_lo, up_hi, UP_PLAN["edge", f, q], grow[f, OWN + q])

    @pl.when(last)
    def _():
        for ref in (up_lo, up_hi):
            ref[...] = jnp.zeros((UP_ROWS, 128), jnp.float32)
        for e in range(SHIFT):
            put(up_lo, up_hi, CODE_PLAN["code", 0, e], codes[e])
        put(up_lo, up_hi, CODE_PLAN["code_edge", 0, 0], across[9])


def react(phases, sums, chem, chem_sums, held):
    p0, p1, p2 = phases
    p3 = K - ((p0 + p1) + p2)
    n3 = 6.0 * K - ((sums[0] + sums[1]) + sums[2])
    ps = (p0, p1, p2, p3)
    ns = (sums[0], sums[1], sums[2], n3)
    squares = [p * p for p in ps]
    base = (0.28 / 0.12) - ((squares[0] + squares[1]) + (squares[2] + squares[3]))
    m0, m1 = chem
    both = BETA * (m0 + m1)
    w2 = both + DRIFT
    ws = (w2 + (7.0 * BETA) * m0, w2 + (7.0 * BETA) * m1, w2, 3.5 * both)
    moved = [
        ns[a] + ps[a] * ((base + squares[a]) + ws[a] * (K - ps[a])) for a in range(4)
    ]
    excess = 0.25 * ((moved[0] + moved[1]) + (moved[2] + moved[3])) - 0.25 * TOP
    clipped = [jnp.minimum(jnp.maximum(u - excess, 0.0), TOP) for u in moved]
    scale = K / ((clipped[0] + clipped[1]) + (clipped[2] + clipped[3]))
    new = [s * scale for s in clipped]
    h = [x * x * (1.5 * K - x) for x in new]
    shared = (h[0] + h[1]) + (h[2] + 3.5 * h[3])
    solute = (shared + 7.0 * h[0], shared + 7.0 * h[1])
    mobility = 0.0075 + (0.1425 / K) * p3
    new_held = [held[i] + mobility * (chem_sums[i] - 6.0 * chem[i]) for i in range(2)]
    new_chem = [new_held[i] - solute[i] for i in range(2)]
    return new, new_chem, new_held


class Half:
    def __init__(self, base, strip_base, n, cells, codes, across, own, up, grow, wing):
        self.base, self.strip_base, self.n = base, strip_base, n
        self.cells, self.codes, self.across = cells, codes, across
        self.own, self.up, self.grow, self.wing, self.lane = own, up, grow, wing, lanes()

    def source(self, p):
        up = p >= OWN
        i = p - OWN if up else p
        q, c = divmod(i, PACK)
        return up, i, q, c

    def store(self, dst, index, rows, label, m0, m1, mask=None):
        values = [jnp.where(label == a, K, 0.0) for a in range(3)]
        rest = jnp.where(label == 3.0, 3.5 * HALF, HALF)
        values += [ALPHA * m0, ALPHA * m1]
        values += [values[3 + i] + jnp.where(label == i, 8.0 * HALF, rest) for i in range(2)]
        for f, value in enumerate(values):
            if mask is not None:
                value = jnp.where(mask, value, dst[f, index, rows, :])
            dst[f, index, rows, :] = value

    def fill(self, dst, p):
        up, i, _, _ = self.source(p)
        body = [self.grow[f, i] if up else self.cells[f, i + 11] for f in range(3)]
        self.store(dst, p - self.base, slice(ROW0, ROW0 + 8), *body)
        for hi, ref in enumerate(self.up if up else self.own):
            count = reach(i, up)
            if count:
                places = UP_PLAN if up else OWN_PLAN
                body = []
                for f in range(3):
                    at, _ = places["cell", f, i]
                    body.append(ref[at : at + count])
                row = ROW0 - count if hi else ROW0 + 8
                self.store(dst, p - self.base, slice(row, row + count), *body)

    def pieces(self, p, f, block):
        up, i, q, _ = self.source(p)
        if block == 0:
            if up:
                return self.grow[f, i], self.grow[f, OWN + q]
            return self.cells[f, i + 11], self.across[3 * f + q + 1]
        places = UP_PLAN if up else OWN_PLAN
        ref = (self.up if up else self.own)[block - 1]
        at, count = places["cell", f, i]
        at = at if block == 1 else at + count - DEEP
        edge, _ = places["edge", f, q]
        return ref[at : at + DEEP], ref[edge : edge + DEEP]

    def joined(self, parts):
        rows = next(part for part in parts if part is not None)[0].shape[0]
        lane = lax.broadcasted_iota(jnp.int32, (rows, 128), 1)
        total = jnp.zeros((rows, 128), jnp.float32)
        for j, part in enumerate(parts):
            if part is None:
                continue
            value, edge, before, after = part
            at = 20 * j
            tile = jnp.where(
                lane < at + 10,
                jnp.where(lane < at + 5, pltpu.roll(edge, before % 128, 1), pltpu.roll(value, at + 5, 1)),
                jnp.where(lane < at + 15, pltpu.roll(value, (at + 15) % 128, 1), pltpu.roll(edge, after % 128, 1)),
            )
            total = jnp.where(lane >= at, tile, total)
        return total

    def fill_strips(self, dst, top):
        for index in range(self.n):
            for block, row, _ in BLOCKS:
                body = []
                for f in range(3):
                    parts = []
                    for j in range(6):
                        p = self.strip_base + self.n * j + index
                        if p >= top:
                            parts.append(None)
                            continue
                        c = self.source(p)[3]
                        parts.append(
                            (*self.pieces(p, f, block), 20 * j - 10 * c, 20 * j + 10 - 10 * c)
                        )
                    body.append(self.joined(parts))
                self.store(dst, index, slice(row, row + body[0].shape[0]), *body)

    def melt(self, dst, strips, table):
        def chem(code, i):
            value = jnp.zeros_like(code)
            for level in range(8):
                value = jnp.where(code == level, table[i, level], value)
            return value

        def rows(block, e):
            if block == 0:
                return self.codes[e], self.across[9]
            ref = self.up[block - 1]
            at, _ = CODE_PLAN["code", 0, e]
            edge, _ = CODE_PLAN["code_edge", 0, 0]
            return ref[at : at + 2], ref[edge : edge + 2]

        for e in range(SHIFT):
            for block, row, count in MELT_BLOCKS:
                code = rows(block, e)[0]
                label = jnp.full_like(code, 3.0)
                where = slice(row, row + count)
                self.store(dst, OWN + e - self.base, where, label, chem(code, 0), chem(code, 1))
        for index in range(self.n):
            for block, row, count in MELT_BLOCKS:
                parts, groups = [], []
                for j in range(6):
                    e = self.strip_base + self.n * j + index - OWN
                    if not 0 <= e < SHIFT:
                        parts.append(None)
                        continue
                    groups.append(j)
                    parts.append((*rows(block, e), 20 * j + 1 - 8 * e, 20 * j + 11 - 8 * e))
                code = self.joined(parts)
                lane = lax.broadcasted_iota(jnp.int32, code.shape, 1)
                mask = (lane >= 20 * groups[0]) & (lane < 20 * groups[-1] + 20)
                label = jnp.full_like(code, 3.0)
                where = slice(row, row + count)
                self.store(strips, index, where, label, chem(code, 0), chem(code, 1), mask)

    def repeat(self, dst, p, source):
        for f in range(5):
            dst[f, p - self.base, 7:25, :] = dst[f, source - self.base, 7:25, :]

    def repeat_strip(self, strips, p, source):
        j, index = divmod(p - self.strip_base, self.n)
        j_from, index_from = divmod(source - self.strip_base, self.n)
        lane = lax.broadcasted_iota(jnp.int32, (18, 128), 1)
        mask = (lane >= 20 * j) & (lane < 20 * j + 20)
        for f in range(5):
            value = strips[f, index_from, 7:25, :]
            if j != j_from:
                value = pltpu.roll(value, 20 * (j - j_from), 1)
            strips[f, index, 7:25, :] = jnp.where(mask, value, strips[f, index, 7:25, :])

    def advance(self, src, index, row, fetch, sides):
        here, sums = [], []
        for f in range(5):
            mid = src[f, index, row : row + 8, :]
            below, above = fetch(f)
            total = (below + above) + (
                src[f, index, row - 1 : row + 7, :] + src[f, index, row + 1 : row + 9, :]
            )
            left, right = sides(f, mid)
            here.append(mid)
            sums.append(total + (left + right))
        held = [src[f, index, row : row + 8, :] for f in (5, 6)]
        return react(here[:3], sums[:3], here[3:], sums[3:], held)

    def spread(self, strips, rows):
        second = self.lane == 3
        for j in range(1, 6):
            second = second | (self.lane == 20 * j + 3)
        for f in range(5):
            for index in range(self.n):
                for row in rows:
                    tile = strips[f, index, row : row + 8, :]
                    tile = jnp.where(second, pltpu.roll(tile, 116, 1), tile)
                    self.wing[f, index, row : row + 8, :] = tile

    def plane_step(self, src, p, row):
        index = p - self.base
        q = p - self.strip_base
        j = (q * 13) >> 6 if self.n == 5 else q >> 2
        at = q - self.n * j
        turn = 124 - 20 * j
        rows = slice(row, row + 8)

        def fetch(f):
            return src[f, index - 1, rows, :], src[f, index + 1, rows, :]

        def sides(f, mid):
            beyond = pltpu.roll(self.wing[f, at, rows, :], turn, 1)
            left = jnp.where(self.lane == 0, beyond, pltpu.roll(mid, 1, 1))
            return left, jnp.where(self.lane == 127, beyond, pltpu.roll(mid, 127, 1))

        return self.advance(src, index, row, fetch, sides)

    def planes(self, first, count, body):
        whole = count - count % 8
        if whole:
            pl.loop(first, first + whole, unroll=8)(body)
        for p in range(first + whole, first + count):
            body(p)

    def sweep(self, src, dst, src_strips, dst_strips, first, count):
        self.spread(src_strips, (8, 16))

        def body(p):
            for row in (8, 16):
                new, chem, held = self.plane_step(src, p, row)
                for f, value in enumerate((*new[:3], *chem, *held)):
                    dst[f, p - self.base, row : row + 8, :] = value

        self.planes(first, count, body)
        last = self.n - 1

        def inside(f, mid):
            return pltpu.roll(mid, 1, 1), pltpu.roll(mid, 127, 1)

        for index in range(self.n):
            for row in (8, 16):
                rows = slice(row, row + 8)

                def fetch(f, index=index, rows=rows):
                    if index:
                        below = src_strips[f, index - 1, rows, :]
                    else:
                        below = pltpu.roll(src_strips[f, last, rows, :], 20, 1)
                    if index < last:
                        above = src_strips[f, index + 1, rows, :]
                    else:
                        above = pltpu.roll(src_strips[f, 0, rows, :], 108, 1)
                    return below, above

                new, chem, held = self.advance(
                    src_strips, index, row, fetch, inside
                )
                for f, value in enumerate((*new[:3], *chem, *held)):
                    dst_strips[f, index, row : row + 8, :] = value

    def finish(self, src, first, count, phases, chems, at=0):
        def body(p):
            new, chem, _ = self.plane_step(src, p, ROW0)
            for a in range(4):
                phases[a, p - first + at] = new[a] * (1.0 / K)
            for i in range(2):
                chems[i, p - first + at] = chem[i] * (1.0 / ALPHA)

        self.planes(first, count, body)


BLOCKS = ((0, ROW0, 8), (1, ROW0 + 8, DEEP), (2, ROW0 - DEEP, DEEP))
MELT_BLOCKS = ((0, ROW0, 8), (1, ROW0 + 8, 2), (2, ROW0 - 2, 2))
LOWER = 11


def lower_half(
    where_ref, cells, across, own_lo, own_hi, middle_lo, middle_hi,
    phases, chems, seam, rows_lo, rows_hi,
    one, two, strip_one, strip_two, wing,
):
    first = where_ref[0] == 0
    middle = where_ref[0] == where_ref[1] // 2

    @pl.when(middle)
    def _():
        rows_lo[...] = middle_lo[...]
        rows_hi[...] = middle_hi[...]

    @pl.when(jnp.logical_not(middle))
    def _():
        rows_lo[...] = own_lo[...]
        rows_hi[...] = own_hi[...]

    half = Half(0, 0, 4, cells, None, across, (rows_lo, rows_hi), None, None, wing)
    for p in range(OWN):
        half.fill(one, p)
    half.fill_strips(strip_one, OWN)
    src, dst, src_strips, dst_strips = one, two, strip_one, strip_two
    for s in range(1, 5):
        if s == 4:

            @pl.when(first)
            def _(src=src, src_strips=src_strips):
                half.repeat(src, 4, 5)
                half.repeat_strip(src_strips, 4, 5)

        half.sweep(src, dst, src_strips, dst_strips, s, OWN - 2 * s)
        for f in range(7):
            for i in range(2):
                seam[s - 1, f, i] = dst[f, OWN - 1 - s + i - 1, 8:24, :]
        src, dst, src_strips, dst_strips = dst, src, dst_strips, src_strips

    @pl.when(first)
    def _(src=src):
        half.repeat(src, 4, 5)

    half.spread(src_strips, (ROW0,))
    half.finish(src, 5, LOWER, phases, chems)


def delivery(phases, chems, phases_out, chem_out, first, at, count, sems, s):
    source, target = pl.ds(at, count), pl.ds(first, count)
    copies = [
        pltpu.make_async_copy(phases.at[:, source], phases_out.at[:, target], sems.at[s]),
        pltpu.make_async_copy(chems.at[:, source], chem_out.at[:, target], sems.at[s + 1]),
    ]
    for copy in copies:
        copy.start()
    return copies


def upper_half(
    where_ref, cells, codes, table_in, across, own_lo, own_hi, up_lo, up_hi, grow, seam,
    lower_phases, lower_chems, phases_out, chem_out,
    one, two, strip_one, strip_two, wing, phases, chems, table, sem, sems,
):
    outs = (phases_out, chem_out)
    copies = delivery(lower_phases, lower_chems, *outs, 0, 0, LOWER, sems, 0)
    last = where_ref[0] == where_ref[1] - 1
    half = Half(
        15, 12, 5, cells, codes, across, (own_lo, own_hi), (up_lo, up_hi), grow, wing
    )
    for p in range(OWN - 2, PLANES):
        half.fill(one, p)
    half.fill_strips(strip_one, PLANES)
    src, dst, src_strips, dst_strips = one, two, strip_one, strip_two
    for s in range(1, 6):
        if s > 1:
            for f in range(7):
                for i in range(2):
                    src[f, OWN - 1 - s + i - half.base, 8:24, :] = seam[s - 2, f, i]
        if s < 4:

            @pl.when(last)
            def _(src=src, src_strips=src_strips):
                half.repeat(src, OWN, OWN - 1)
                half.repeat_strip(src_strips, OWN, OWN - 1)

        if s == 4:

            @pl.when(last)
            def _(src=src, src_strips=src_strips):
                copy = pltpu.make_async_copy(table_in, table, sem)
                copy.start()
                copy.wait()
                half.melt(src, src_strips, table)
                half.repeat_strip(src_strips, OWN + SHIFT, OWN + SHIFT - 1)

        if s >= 4:

            @pl.when(last)
            def _(src=src):
                half.repeat(src, OWN + SHIFT, OWN + SHIFT - 1)

        if s < 5:
            half.sweep(src, dst, src_strips, dst_strips, OWN - s, OWN)
            src, dst, src_strips, dst_strips = dst, src, dst_strips, src_strips
    half.spread(src_strips, (ROW0,))
    half.finish(src, OWN - 5, 12, phases, chems)
    copies += delivery(phases, chems, *outs, LOWER, 0, 12, sems, 2)
    half.finish(src, OWN + 7, 9, phases, chems, 12)
    copies += delivery(phases, chems, *outs, LOWER + 12, 12, 9, sems, 4)
    for copy in copies:
        copy.wait()


def on_device(labels, potential, melt_codes, melt_table):
    n_grow, n_gy, n_gz = (lax.axis_size(a) for a in AXES)
    where = jnp.stack([lax.axis_index("grow"), n_grow]).astype(jnp.int32)

    def send(value, dg, dy, dz, planes=None):
        pairs = []
        for g in planes or range(max(0, -dg), n_grow):
            for y in range(n_gy):
                for z in range(n_gz):
                    to = ((g + dg) * n_gy + (y + dy) % n_gy) * n_gz + (z + dz) % n_gz
                    pairs.append(((g * n_gy + y) * n_gz + z, to))
        return lax.ppermute(value, AXES, pairs)

    def f32(*shape):
        return jax.ShapeDtypeStruct(shape, jnp.float32)

    params = pltpu.CompilerParams(vmem_limit_bytes=48 << 20)
    cells, codes, edges = pl.pallas_call(
        first_pack,
        in_specs=[HBM] * 3,
        out_specs=[VMEM] * 3,
        out_shape=[f32(3, 32, 8, 128), f32(SHIFT, 8, 128), f32(10, 8, 128)],
        scratch_shapes=[
            pltpu.VMEM((32, 8, 128), jnp.int32),
            pltpu.VMEM((SHIFT, 8, 128), jnp.int32),
            pltpu.SemaphoreType.DMA((3,)),
        ],
        compiler_params=params,
        name="first_pack",
    )(*(pltpu.with_memory_space_constraint(x, pltpu.MemorySpace.HBM) for x in (labels, potential, melt_codes)))
    across = send(edges, 0, 0, 1)
    own_lo, own_hi = pl.pallas_call(
        second_pack,
        in_specs=[VMEM] * 2,
        out_specs=[VMEM] * 2,
        out_shape=[f32(OWN_ROWS, 128)] * 2,
        compiler_params=params,
        name="second_pack",
    )(cells, across)
    middle = n_grow // 2
    others = [g for g in range(n_grow) if g != middle]
    middle_lo = send(own_lo, 0, -1, 0, [middle])
    middle_hi = send(own_hi, 0, 1, 0, [middle])
    own_lo = send(own_lo, 0, -1, 0, others)
    own_hi = send(own_hi, 0, 1, 0, others)
    grow = pl.pallas_call(
        grow_pack,
        in_specs=[VMEM, VMEM, ANY, ANY],
        out_specs=VMEM,
        out_shape=f32(3, OWN + 2, 8, 128),
        compiler_params=params,
        name="grow_pack",
    )(cells, across, middle_lo, middle_hi)
    grow = send(grow, -1, 0, 0)
    up_lo, up_hi = pl.pallas_call(
        third_pack,
        in_specs=[SMEM] + [VMEM] * 3,
        out_specs=[VMEM] * 2,
        out_shape=[f32(UP_ROWS, 128)] * 2,
        compiler_params=params,
        name="third_pack",
    )(where, grow, codes, across)
    up_lo = send(up_lo, 0, -1, 0)
    up_hi = send(up_hi, 0, 1, 0)

    def buffers(planes, strips):
        return (
            [pltpu.VMEM((7, planes, PITCH, 128), jnp.float32)] * 2
            + [pltpu.VMEM((7, strips, PITCH, 128), jnp.float32)] * 2
            + [pltpu.VMEM((5, strips, PITCH, 128), jnp.float32)]
        )

    phases, chems, seam, own_lo, own_hi = pl.pallas_call(
        lower_half,
        in_specs=[SMEM] + [VMEM] * 6,
        out_specs=[VMEM] * 5,
        out_shape=[f32(4, LOWER, 8, 128), f32(2, LOWER, 8, 128), f32(4, 7, 2, 16, 128)]
        + [f32(OWN_ROWS, 128)] * 2,
        scratch_shapes=buffers(OWN, 4),
        compiler_params=params,
        cost_estimate=pl.CostEstimate(
            flops=60_000_000, bytes_accessed=12_000_000, transcendentals=0
        ),
        name="lower_half",
    )(where, cells, across, own_lo, own_hi, middle_lo, middle_hi)
    table = pltpu.with_memory_space_constraint(melt_table, pltpu.MemorySpace.HBM)
    return pl.pallas_call(
        upper_half,
        in_specs=[SMEM, VMEM, VMEM, HBM] + [VMEM] * 9,
        out_specs=[HBM, HBM],
        out_shape=[f32(4, 32, 8, 128), f32(2, 32, 8, 128)],
        scratch_shapes=buffers(27, 5)
        + [
            pltpu.VMEM((4, OWN, 8, 128), jnp.float32),
            pltpu.VMEM((2, OWN, 8, 128), jnp.float32),
            pltpu.SMEM((2, 8), jnp.float32),
            pltpu.SemaphoreType.DMA,
            pltpu.SemaphoreType.DMA((6,)),
        ],
        compiler_params=params,
        name="upper_half",
    )(where, cells, codes, table, across, own_lo, own_hi, up_lo, up_hi, grow, seam, phases, chems)


def solution(mesh):
    return jax.shard_map(
        on_device,
        mesh=mesh,
        in_specs=(P("grow", "gy", "gz"), P(None, "grow", "gy", "gz"), P(None, "gy", "gz"), P()),
        out_specs=(P(None, "grow", "gy", "gz"), P(None, "grow", "gy", "gz")),
        check_vma=False,
    )
```

```python
import jax
import jax.numpy as jnp
from jax import lax
from jax.experimental import pallas as pl
from jax.experimental.pallas import tpu as pltpu
from jax.sharding import PartitionSpec as P

K = 5.0**0.5
ALPHA = 5.0 * K**3
BETA = 2.5 / (K * ALPHA)
TOP = K / 0.12
DRIFT = 0.15 / (0.12 * K)
HALF = 0.5 * K**3

SHIFT = 16
OWN = 21
PLANES = 2 * OWN
PITCH = 32
ROW0 = 12
DEEP = 5
PACK = 11
AXES = ("grow", "gy", "gz")
VMEM = pl.BlockSpec(memory_space=pltpu.VMEM)
HBM = pl.BlockSpec(memory_space=pltpu.MemorySpace.HBM)


def lanes():
    return lax.broadcasted_iota(jnp.int32, (8, 128), 1)


def reach(i, up):
    return min(DEEP, OWN - 1 - i if up else i)


def plan(up):
    places, at = {}, 8
    for f in range(3):
        for i in range(OWN):
            places["cell", f, i] = (at, reach(i, up))
            at += reach(i, up)
        for q in range(2):
            places["edge", f, q] = (at, DEEP)
            at += DEEP
    return places, -(-at // 8) * 8


OWN_PLAN, OWN_ROWS = plan(False)
UP_PLAN, UP_ROWS = plan(True)
CODE_PLAN = {("code", 0, e): (8 + 2 * e, 2) for e in range(SHIFT)}
CODE_PLAN["code_edge", 0, 0] = (8 + 2 * SHIFT, 2)


def first_pack(labels, potential, codes, cells, codes_out, edges, labels_in, codes_in, sems):
    copies = [
        pltpu.make_async_copy(labels, labels_in, sems.at[0]),
        pltpu.make_async_copy(potential, cells.at[1:3], sems.at[1]),
        pltpu.make_async_copy(codes, codes_in, sems.at[2]),
    ]
    for copy in copies:
        copy.start()
    lane = lanes()

    def packed(tiles, width, offset):
        total = jnp.zeros((8, 128), jnp.float32)
        for c, tile in enumerate(tiles):
            there = (lane >= width * c) & (lane < width * (c + 1))
            total = jnp.where(there, pltpu.roll(tile, (width * c + offset) % 128, 1), total)
        return total

    copies[0].wait()
    for p in range(32):
        cells[0, p] = labels_in[p].astype(jnp.float32)
    copies[2].wait()
    for e in range(SHIFT):
        codes_out[e] = codes_in[e].astype(jnp.float32)
    edges[9] = packed([codes_out[e] for e in range(SHIFT)], 8, 4)
    copies[1].wait()
    for f in range(3):
        for q in range(3):
            planes = range(PACK * q, min(PACK * q + PACK, 32))
            edges[3 * f + q] = packed([cells[f, p] for p in planes], 10, 5)


def put(lo, hi, place, tile):
    at, count = place
    if count:
        lo[at : at + count] = tile[0:count]
        hi[at : at + count] = tile[8 - count : 8]


def by_parity(body):
    even = lax.rem(lax.axis_index("gy"), 2) == 0
    pl.when(even)(lambda: body(True))
    pl.when(jnp.logical_not(even))(lambda: body(False))


def second_pack(cells, across, one, two, grow):
    by_parity(lambda even: own_rows(cells, across, *((one, two) if even else (two, one))))
    for f in range(3):
        grow[f, 0:OWN] = cells[f, 0:OWN]
        grow[f, OWN : OWN + 2] = across[3 * f : 3 * f + 2]


def own_rows(cells, across, own_lo, own_hi):
    for f in range(3):
        for i in range(OWN):
            put(own_lo, own_hi, OWN_PLAN["cell", f, i], cells[f, i + 11])
        for q in range(2):
            put(own_lo, own_hi, OWN_PLAN["edge", f, q], across[3 * f + q + 1])
    for ref in (own_lo, own_hi):
        blank(ref, OWN_PLAN, OWN_ROWS)


def blank(ref, places, rows):
    used = max(at + count for at, count in places.values())
    ref[0:8] = jnp.zeros((8, 128), jnp.float32)
    if used < rows:
        ref[used:rows] = jnp.zeros((rows - used, 128), jnp.float32)


def third_pack(grow, codes, across, one, two):
    by_parity(lambda even: up_rows(grow, codes, across, *((one, two) if even else (two, one))))


def place():
    index = lax.axis_index("grow")
    return index == 0, index == lax.axis_size("grow") - 1


def up_rows(grow, codes, across, up_lo, up_hi):
    _, last = place()
    for ref in (up_lo, up_hi):
        blank(ref, UP_PLAN, UP_ROWS)

    @pl.when(jnp.logical_not(last))
    def _():
        for f in range(3):
            for i in range(OWN):
                put(up_lo, up_hi, UP_PLAN["cell", f, i], grow[f, i])
            for q in range(2):
                put(up_lo, up_hi, UP_PLAN["edge", f, q], grow[f, OWN + q])

    @pl.when(last)
    def _():
        for ref in (up_lo, up_hi):
            ref[...] = jnp.zeros((UP_ROWS, 128), jnp.float32)
        for e in range(SHIFT):
            put(up_lo, up_hi, CODE_PLAN["code", 0, e], codes[e])
        put(up_lo, up_hi, CODE_PLAN["code_edge", 0, 0], across[9])


def react(phases, sums, chem, chem_sums, held):
    p0, p1, p2 = phases
    p3 = K - ((p0 + p1) + p2)
    n3 = 6.0 * K - ((sums[0] + sums[1]) + sums[2])
    ps = (p0, p1, p2, p3)
    ns = (sums[0], sums[1], sums[2], n3)
    squares = [p * p for p in ps]
    base = (0.28 / 0.12) - ((squares[0] + squares[1]) + (squares[2] + squares[3]))
    m0, m1 = chem
    both = BETA * (m0 + m1)
    w2 = both + DRIFT
    ws = (w2 + (7.0 * BETA) * m0, w2 + (7.0 * BETA) * m1, w2, 3.5 * both)
    moved = [
        ns[a] + ps[a] * ((base + squares[a]) + ws[a] * (K - ps[a])) for a in range(4)
    ]
    excess = 0.25 * ((moved[0] + moved[1]) + (moved[2] + moved[3])) - 0.25 * TOP
    clipped = [jnp.minimum(jnp.maximum(u - excess, 0.0), TOP) for u in moved]
    scale = K / ((clipped[0] + clipped[1]) + (clipped[2] + clipped[3]))
    new = [s * scale for s in clipped]
    h = [x * x * (1.5 * K - x) for x in new]
    shared = (h[0] + h[1]) + (h[2] + 3.5 * h[3])
    solute = (shared + 7.0 * h[0], shared + 7.0 * h[1])
    mobility = 0.0075 + (0.1425 / K) * p3
    new_held = [held[i] + mobility * (chem_sums[i] - 6.0 * chem[i]) for i in range(2)]
    new_chem = [new_held[i] - solute[i] for i in range(2)]
    return new, new_chem, new_held


class Half:
    def __init__(self, base, strip_base, n, cells, codes, across, own, up, grow, wing):
        self.base, self.strip_base, self.n = base, strip_base, n
        self.cells, self.codes, self.across = cells, codes, across
        self.own, self.up, self.grow, self.wing, self.lane = own, up, grow, wing, lanes()

    def source(self, p):
        up = p >= OWN
        i = p - OWN if up else p
        q, c = divmod(i, PACK)
        return up, i, q, c

    def store(self, dst, index, rows, label, m0, m1, mask=None):
        values = [jnp.where(label == a, K, 0.0) for a in range(3)]
        rest = jnp.where(label == 3.0, 3.5 * HALF, HALF)
        values += [ALPHA * m0, ALPHA * m1]
        values += [values[3 + i] + jnp.where(label == i, 8.0 * HALF, rest) for i in range(2)]
        for f, value in enumerate(values):
            if mask is not None:
                value = jnp.where(mask, value, dst[f, index, rows, :])
            dst[f, index, rows, :] = value

    def fill(self, dst, p):
        up, i, _, _ = self.source(p)
        body = [self.grow[f, i] if up else self.cells[f, i + 11] for f in range(3)]
        self.store(dst, p - self.base, slice(ROW0, ROW0 + 8), *body)
        for hi, ref in enumerate(self.up if up else self.own):
            count = reach(i, up)
            if count:
                places = UP_PLAN if up else OWN_PLAN
                body = []
                for f in range(3):
                    at, _ = places["cell", f, i]
                    body.append(ref[at : at + count])
                row = ROW0 - count if hi else ROW0 + 8
                self.store(dst, p - self.base, slice(row, row + count), *body)

    def pieces(self, p, f, block):
        up, i, q, _ = self.source(p)
        if block == 0:
            if up:
                return self.grow[f, i], self.grow[f, OWN + q]
            return self.cells[f, i + 11], self.across[3 * f + q + 1]
        places = UP_PLAN if up else OWN_PLAN
        ref = (self.up if up else self.own)[block - 1]
        at, count = places["cell", f, i]
        at = at if block == 1 else at + count - DEEP
        edge, _ = places["edge", f, q]
        return ref[at : at + DEEP], ref[edge : edge + DEEP]

    def joined(self, parts):
        rows = next(part for part in parts if part is not None)[0].shape[0]
        lane = lax.broadcasted_iota(jnp.int32, (rows, 128), 1)
        total = jnp.zeros((rows, 128), jnp.float32)
        for j, part in enumerate(parts):
            if part is None:
                continue
            value, edge, before, after = part
            at = 20 * j
            tile = jnp.where(
                lane < at + 10,
                jnp.where(lane < at + 5, pltpu.roll(edge, before % 128, 1), pltpu.roll(value, at + 5, 1)),
                jnp.where(lane < at + 15, pltpu.roll(value, (at + 15) % 128, 1), pltpu.roll(edge, after % 128, 1)),
            )
            total = jnp.where(lane >= at, tile, total)
        return total

    def fill_strips(self, dst, top):
        for index in range(self.n):
            for block, row, _ in BLOCKS:
                body = []
                for f in range(3):
                    parts = []
                    for j in range(6):
                        p = self.strip_base + self.n * j + index
                        if p >= top:
                            parts.append(None)
                            continue
                        c = self.source(p)[3]
                        parts.append(
                            (*self.pieces(p, f, block), 20 * j - 10 * c, 20 * j + 10 - 10 * c)
                        )
                    body.append(self.joined(parts))
                self.store(dst, index, slice(row, row + body[0].shape[0]), *body)

    def melt(self, dst, strips, table):
        def chem(code, i):
            value = jnp.zeros_like(code)
            for level in range(8):
                value = jnp.where(code == level, table[i, level], value)
            return value

        def rows(block, e):
            if block == 0:
                return self.codes[e], self.across[9]
            ref = self.up[block - 1]
            at, _ = CODE_PLAN["code", 0, e]
            edge, _ = CODE_PLAN["code_edge", 0, 0]
            return ref[at : at + 2], ref[edge : edge + 2]

        for e in range(SHIFT):
            for block, row, count in MELT_BLOCKS:
                code = rows(block, e)[0]
                label = jnp.full_like(code, 3.0)
                where = slice(row, row + count)
                self.store(dst, OWN + e - self.base, where, label, chem(code, 0), chem(code, 1))
        for index in range(self.n):
            for block, row, count in MELT_BLOCKS:
                parts, groups = [], []
                for j in range(6):
                    e = self.strip_base + self.n * j + index - OWN
                    if not 0 <= e < SHIFT:
                        parts.append(None)
                        continue
                    groups.append(j)
                    parts.append((*rows(block, e), 20 * j + 1 - 8 * e, 20 * j + 11 - 8 * e))
                code = self.joined(parts)
                lane = lax.broadcasted_iota(jnp.int32, code.shape, 1)
                mask = (lane >= 20 * groups[0]) & (lane < 20 * groups[-1] + 20)
                label = jnp.full_like(code, 3.0)
                where = slice(row, row + count)
                self.store(strips, index, where, label, chem(code, 0), chem(code, 1), mask)

    def repeat(self, dst, p, source):
        for f in range(5):
            dst[f, p - self.base, 7:25, :] = dst[f, source - self.base, 7:25, :]

    def repeat_strip(self, strips, p, source):
        j, index = divmod(p - self.strip_base, self.n)
        j_from, index_from = divmod(source - self.strip_base, self.n)
        lane = lax.broadcasted_iota(jnp.int32, (18, 128), 1)
        mask = (lane >= 20 * j) & (lane < 20 * j + 20)
        for f in range(5):
            value = strips[f, index_from, 7:25, :]
            if j != j_from:
                value = pltpu.roll(value, 20 * (j - j_from), 1)
            strips[f, index, 7:25, :] = jnp.where(mask, value, strips[f, index, 7:25, :])

    def advance(self, src, index, row, fetch, sides):
        here, sums = [], []
        for f in range(5):
            mid = src[f, index, row : row + 8, :]
            below, above = fetch(f)
            total = (below + above) + (
                src[f, index, row - 1 : row + 7, :] + src[f, index, row + 1 : row + 9, :]
            )
            left, right = sides(f, mid)
            here.append(mid)
            sums.append(total + (left + right))
        held = [src[f, index, row : row + 8, :] for f in (5, 6)]
        return react(here[:3], sums[:3], here[3:], sums[3:], held)

    def spread(self, strips, rows):
        second = self.lane == 3
        for j in range(1, 6):
            second = second | (self.lane == 20 * j + 3)
        for f in range(5):
            for index in range(self.n):
                for row in rows:
                    tile = strips[f, index, row : row + 8, :]
                    tile = jnp.where(second, pltpu.roll(tile, 116, 1), tile)
                    self.wing[f, index, row : row + 8, :] = tile

    def plane_step(self, src, p, row):
        index = p - self.base
        q = p - self.strip_base
        j = (q * 13) >> 6 if self.n == 5 else q >> 2
        at = q - self.n * j
        turn = 124 - 20 * j
        rows = slice(row, row + 8)

        def fetch(f):
            return src[f, index - 1, rows, :], src[f, index + 1, rows, :]

        def sides(f, mid):
            beyond = pltpu.roll(self.wing[f, at, rows, :], turn, 1)
            left = jnp.where(self.lane == 0, beyond, pltpu.roll(mid, 1, 1))
            return left, jnp.where(self.lane == 127, beyond, pltpu.roll(mid, 127, 1))

        return self.advance(src, index, row, fetch, sides)

    def planes(self, first, count, body):
        whole = count - count % 8
        if whole:
            pl.loop(first, first + whole, unroll=8)(body)
        for p in range(first + whole, first + count):
            body(p)

    def sweep(self, src, dst, src_strips, dst_strips, first, count):
        self.spread(src_strips, (8, 16))

        def body(p):
            for row in (8, 16):
                new, chem, held = self.plane_step(src, p, row)
                for f, value in enumerate((*new[:3], *chem, *held)):
                    dst[f, p - self.base, row : row + 8, :] = value

        self.planes(first, count, body)
        last = self.n - 1

        def inside(f, mid):
            return pltpu.roll(mid, 1, 1), pltpu.roll(mid, 127, 1)

        for index in range(self.n):
            for row in (8, 16):
                rows = slice(row, row + 8)

                def fetch(f, index=index, rows=rows):
                    if index:
                        below = src_strips[f, index - 1, rows, :]
                    else:
                        below = pltpu.roll(src_strips[f, last, rows, :], 20, 1)
                    if index < last:
                        above = src_strips[f, index + 1, rows, :]
                    else:
                        above = pltpu.roll(src_strips[f, 0, rows, :], 108, 1)
                    return below, above

                new, chem, held = self.advance(
                    src_strips, index, row, fetch, inside
                )
                for f, value in enumerate((*new[:3], *chem, *held)):
                    dst_strips[f, index, row : row + 8, :] = value

    def finish(self, src, first, count, phases, chems, at=0):
        def body(p):
            new, chem, _ = self.plane_step(src, p, ROW0)
            for a in range(4):
                phases[a, p - first + at] = new[a] * (1.0 / K)
            for i in range(2):
                chems[i, p - first + at] = chem[i] * (1.0 / ALPHA)

        self.planes(first, count, body)


BLOCKS = ((0, ROW0, 8), (1, ROW0 + 8, DEEP), (2, ROW0 - DEEP, DEEP))
MELT_BLOCKS = ((0, ROW0, 8), (1, ROW0 + 8, 2), (2, ROW0 - 2, 2))
LOWER = 11


def lower_half(
    cells, across, swap_one, swap_two,
    phases, chems, seam, rows_lo, rows_hi,
    one, two, strip_one, strip_two, wing,
):
    first, _ = place()

    def sort_rows(even):
        rows_lo[...] = (swap_two if even else swap_one)[...]
        rows_hi[...] = (swap_one if even else swap_two)[...]

    by_parity(sort_rows)
    half = Half(0, 0, 4, cells, None, across, (rows_lo, rows_hi), None, None, wing)
    for p in range(OWN):
        half.fill(one, p)
    half.fill_strips(strip_one, OWN)
    src, dst, src_strips, dst_strips = one, two, strip_one, strip_two
    for s in range(1, 5):
        if s == 4:

            @pl.when(first)
            def _(src=src, src_strips=src_strips):
                half.repeat(src, 4, 5)
                half.repeat_strip(src_strips, 4, 5)

        half.sweep(src, dst, src_strips, dst_strips, s, OWN - 2 * s)
        for f in range(7):
            for i in range(2):
                seam[s - 1, f, i] = dst[f, OWN - 1 - s + i - 1, 8:24, :]
        src, dst, src_strips, dst_strips = dst, src, dst_strips, src_strips

    @pl.when(first)
    def _(src=src):
        half.repeat(src, 4, 5)

    half.spread(src_strips, (ROW0,))
    half.finish(src, 5, LOWER, phases, chems)


def delivery(phases, chems, phases_out, chem_out, first, at, count, sems, s):
    source, target = pl.ds(at, count), pl.ds(first, count)
    copies = [
        pltpu.make_async_copy(phases.at[:, source], phases_out.at[:, target], sems.at[s]),
        pltpu.make_async_copy(chems.at[:, source], chem_out.at[:, target], sems.at[s + 1]),
    ]
    for copy in copies:
        copy.start()
    return copies


def upper_half(
    cells, codes, table_in, across, own_lo, own_hi, swap_one, swap_two, grow, seam,
    lower_phases, lower_chems, phases_out, chem_out,
    one, two, strip_one, strip_two, wing, phases, chems, up_lo, up_hi, table, sem, sems,
):
    outs = (phases_out, chem_out)
    copies = delivery(lower_phases, lower_chems, *outs, 0, 0, LOWER, sems, 0)
    _, last = place()

    def sort_rows(even):
        up_lo[...] = (swap_two if even else swap_one)[...]
        up_hi[...] = (swap_one if even else swap_two)[...]

    by_parity(sort_rows)
    half = Half(
        15, 12, 5, cells, codes, across, (own_lo, own_hi), (up_lo, up_hi), grow, wing
    )
    for p in range(OWN - 2, PLANES):
        half.fill(one, p)
    half.fill_strips(strip_one, PLANES)
    src, dst, src_strips, dst_strips = one, two, strip_one, strip_two
    for s in range(1, 6):
        if s > 1:
            for f in range(7):
                for i in range(2):
                    src[f, OWN - 1 - s + i - half.base, 8:24, :] = seam[s - 2, f, i]
        if s < 4:

            @pl.when(last)
            def _(src=src, src_strips=src_strips):
                half.repeat(src, OWN, OWN - 1)
                half.repeat_strip(src_strips, OWN, OWN - 1)

        if s == 4:

            @pl.when(last)
            def _(src=src, src_strips=src_strips):
                copy = pltpu.make_async_copy(table_in, table, sem)
                copy.start()
                copy.wait()
                half.melt(src, src_strips, table)
                half.repeat_strip(src_strips, OWN + SHIFT, OWN + SHIFT - 1)

        if s >= 4:

            @pl.when(last)
            def _(src=src):
                half.repeat(src, OWN + SHIFT, OWN + SHIFT - 1)

        if s < 5:
            half.sweep(src, dst, src_strips, dst_strips, OWN - s, OWN)
            src, dst, src_strips, dst_strips = dst, src, dst_strips, src_strips
    half.spread(src_strips, (ROW0,))
    half.finish(src, OWN - 5, 12, phases, chems)
    copies += delivery(phases, chems, *outs, LOWER, 0, 12, sems, 2)
    half.finish(src, OWN + 7, 9, phases, chems, 12)
    copies += delivery(phases, chems, *outs, LOWER + 12, 12, 9, sems, 4)
    for copy in copies:
        copy.wait()


def on_device(labels, potential, melt_codes, melt_table):
    n_grow, n_gy, n_gz = (lax.axis_size(a) for a in AXES)

    def send(value, dg, dy, dz):
        pairs = []
        for g in range(max(0, -dg), n_grow):
            for y in range(n_gy):
                for z in range(n_gz):
                    to = ((g + dg) * n_gy + (y + dy) % n_gy) * n_gz + (z + dz) % n_gz
                    pairs.append(((g * n_gy + y) * n_gz + z, to))
        return lax.ppermute(value, AXES, pairs)

    def f32(*shape):
        return jax.ShapeDtypeStruct(shape, jnp.float32)

    params = pltpu.CompilerParams(vmem_limit_bytes=48 << 20)
    cells, codes, edges = pl.pallas_call(
        first_pack,
        in_specs=[HBM] * 3,
        out_specs=[VMEM] * 3,
        out_shape=[f32(3, 32, 8, 128), f32(SHIFT, 8, 128), f32(10, 8, 128)],
        scratch_shapes=[
            pltpu.VMEM((32, 8, 128), jnp.int32),
            pltpu.VMEM((SHIFT, 8, 128), jnp.int32),
            pltpu.SemaphoreType.DMA((3,)),
        ],
        compiler_params=params,
        name="first_pack",
    )(*(pltpu.with_memory_space_constraint(x, pltpu.MemorySpace.HBM) for x in (labels, potential, melt_codes)))
    across = send(edges, 0, 0, 1)
    own_one, own_two, grow = pl.pallas_call(
        second_pack,
        in_specs=[VMEM] * 2,
        out_specs=[VMEM] * 3,
        out_shape=[f32(OWN_ROWS, 128)] * 2 + [f32(3, OWN + 2, 8, 128)],
        compiler_params=params,
        name="second_pack",
    )(cells, across)

    def swap(one, two):
        below = [(y, (y + (1 if y % 2 else -1)) % n_gy) for y in range(n_gy)]
        above = [(y, (y + (-1 if y % 2 else 1)) % n_gy) for y in range(n_gy)]
        return lax.ppermute(one, "gy", below), lax.ppermute(two, "gy", above)

    own_one, own_two = swap(own_one, own_two)
    grow = send(grow, -1, 0, 0)
    up_one, up_two = pl.pallas_call(
        third_pack,
        in_specs=[VMEM] * 3,
        out_specs=[VMEM] * 2,
        out_shape=[f32(UP_ROWS, 128)] * 2,
        compiler_params=params,
        name="third_pack",
    )(grow, codes, across)
    up_one, up_two = swap(up_one, up_two)

    def buffers(planes, strips):
        return (
            [pltpu.VMEM((7, planes, PITCH, 128), jnp.float32)] * 2
            + [pltpu.VMEM((7, strips, PITCH, 128), jnp.float32)] * 2
            + [pltpu.VMEM((5, strips, PITCH, 128), jnp.float32)]
        )

    phases, chems, seam, own_lo, own_hi = pl.pallas_call(
        lower_half,
        in_specs=[VMEM] * 4,
        out_specs=[VMEM] * 5,
        out_shape=[f32(4, LOWER, 8, 128), f32(2, LOWER, 8, 128), f32(4, 7, 2, 16, 128)]
        + [f32(OWN_ROWS, 128)] * 2,
        scratch_shapes=buffers(OWN, 4),
        compiler_params=params,
        cost_estimate=pl.CostEstimate(
            flops=60_000_000, bytes_accessed=12_000_000, transcendentals=0
        ),
        name="lower_half",
    )(cells, across, own_one, own_two)
    table = pltpu.with_memory_space_constraint(melt_table, pltpu.MemorySpace.HBM)
    return pl.pallas_call(
        upper_half,
        in_specs=[VMEM, VMEM, HBM] + [VMEM] * 9,
        out_specs=[HBM, HBM],
        out_shape=[f32(4, 32, 8, 128), f32(2, 32, 8, 128)],
        scratch_shapes=buffers(27, 5)
        + [
            pltpu.VMEM((4, OWN, 8, 128), jnp.float32),
            pltpu.VMEM((2, OWN, 8, 128), jnp.float32),
            pltpu.VMEM((UP_ROWS, 128), jnp.float32),
            pltpu.VMEM((UP_ROWS, 128), jnp.float32),
            pltpu.SMEM((2, 8), jnp.float32),
            pltpu.SemaphoreType.DMA,
            pltpu.SemaphoreType.DMA((6,)),
        ],
        compiler_params=params,
        name="upper_half",
    )(cells, codes, table, across, own_lo, own_hi, up_one, up_two, grow, seam, phases, chems)


def solution(mesh):
    return jax.shard_map(
        on_device,
        mesh=mesh,
        in_specs=(P("grow", "gy", "gz"), P(None, "grow", "gy", "gz"), P(None, "gy", "gz"), P()),
        out_specs=(P(None, "grow", "gy", "gz"), P(None, "grow", "gy", "gz")),
        check_vma=False,
    )
```

```python
import jax
import jax.numpy as jnp
from jax import lax
from jax.experimental import pallas as pl
from jax.experimental.pallas import tpu as pltpu
from jax.sharding import PartitionSpec as P

K = 5.0**0.5
ALPHA = 5.0 * K**3
BETA = 2.5 / (K * ALPHA)
TOP = K / 0.12
DRIFT = 0.15 / (0.12 * K)
HALF = 0.5 * K**3

SHIFT = 16
OWN = 21
PLANES = 2 * OWN
PITCH = 32
ROW0 = 12
DEEP = 5
PACK = 11
AXES = ("grow", "gy", "gz")
VMEM = pl.BlockSpec(memory_space=pltpu.VMEM)
HBM = pl.BlockSpec(memory_space=pltpu.MemorySpace.HBM)


def lanes():
    return lax.broadcasted_iota(jnp.int32, (8, 128), 1)


def reach(i, up):
    return min(DEEP, OWN - 1 - i if up else i)


def plan(up):
    places, at = {}, 8
    for f in range(3):
        for i in range(OWN):
            places["cell", f, i] = (at, reach(i, up))
            at += reach(i, up)
        for q in range(2):
            places["edge", f, q] = (at, DEEP)
            at += DEEP
    return places, -(-at // 8) * 8


OWN_PLAN, OWN_ROWS = plan(False)
UP_PLAN, UP_ROWS = plan(True)
CODE_PLAN = {("code", 0, e): (8 + 2 * e, 2) for e in range(SHIFT)}
CODE_PLAN["code_edge", 0, 0] = (8 + 2 * SHIFT, 2)


def first_pack(labels, potential, codes, cells, codes_out, edges, labels_in, codes_in, sems):
    copies = [
        pltpu.make_async_copy(labels, labels_in, sems.at[0]),
        pltpu.make_async_copy(potential, cells.at[1:3], sems.at[1]),
        pltpu.make_async_copy(codes, codes_in, sems.at[2]),
    ]
    for copy in copies:
        copy.start()
    lane = lanes()

    def packed(tiles, width, offset):
        total = jnp.zeros((8, 128), jnp.float32)
        for c, tile in enumerate(tiles):
            there = (lane >= width * c) & (lane < width * (c + 1))
            total = jnp.where(there, pltpu.roll(tile, (width * c + offset) % 128, 1), total)
        return total

    copies[0].wait()
    for p in range(32):
        cells[0, p] = labels_in[p].astype(jnp.float32)
    copies[2].wait()
    for e in range(SHIFT):
        codes_out[e] = codes_in[e].astype(jnp.float32)
    edges[9] = packed([codes_out[e] for e in range(SHIFT)], 8, 4)
    copies[1].wait()
    for f in range(3):
        for q in range(3):
            planes = range(PACK * q, min(PACK * q + PACK, 32))
            edges[3 * f + q] = packed([cells[f, p] for p in planes], 10, 5)


def put(lo, hi, place, tile):
    at, count = place
    if count:
        lo[at : at + count] = tile[0:count]
        hi[at : at + count] = tile[8 - count : 8]


def by_parity(body):
    even = lax.rem(lax.axis_index("gy"), 2) == 0
    pl.when(even)(lambda: body(True))
    pl.when(jnp.logical_not(even))(lambda: body(False))


def second_pack(cells, across, one, two, grow):
    by_parity(lambda even: own_rows(cells, across, *((one, two) if even else (two, one))))
    for f in range(3):
        grow[f, 0:OWN] = cells[f, 0:OWN]
        grow[f, OWN : OWN + 2] = across[3 * f : 3 * f + 2]


def own_rows(cells, across, own_lo, own_hi):
    for f in range(3):
        for i in range(OWN):
            put(own_lo, own_hi, OWN_PLAN["cell", f, i], cells[f, i + 11])
        for q in range(2):
            put(own_lo, own_hi, OWN_PLAN["edge", f, q], across[3 * f + q + 1])
    for ref in (own_lo, own_hi):
        blank(ref, OWN_PLAN, OWN_ROWS)


def blank(ref, places, rows):
    used = max(at + count for at, count in places.values())
    ref[0:8] = jnp.zeros((8, 128), jnp.float32)
    if used < rows:
        ref[used:rows] = jnp.zeros((rows - used, 128), jnp.float32)


def third_pack(grow, codes, across, one, two):
    by_parity(lambda even: up_rows(grow, codes, across, *((one, two) if even else (two, one))))


def place():
    index = lax.axis_index("grow")
    return index == 0, index == lax.axis_size("grow") - 1


def up_rows(grow, codes, across, up_lo, up_hi):
    _, last = place()
    for ref in (up_lo, up_hi):
        blank(ref, UP_PLAN, UP_ROWS)

    @pl.when(jnp.logical_not(last))
    def _():
        for f in range(3):
            for i in range(OWN):
                put(up_lo, up_hi, UP_PLAN["cell", f, i], grow[f, i])
            for q in range(2):
                put(up_lo, up_hi, UP_PLAN["edge", f, q], grow[f, OWN + q])

    @pl.when(last)
    def _():
        for ref in (up_lo, up_hi):
            ref[...] = jnp.zeros((UP_ROWS, 128), jnp.float32)
        for e in range(SHIFT):
            put(up_lo, up_hi, CODE_PLAN["code", 0, e], codes[e])
        put(up_lo, up_hi, CODE_PLAN["code_edge", 0, 0], across[9])


def react(phases, sums, chem, chem_sums, held):
    p0, p1, p2 = phases
    p3 = K - ((p0 + p1) + p2)
    n3 = 6.0 * K - ((sums[0] + sums[1]) + sums[2])
    ps = (p0, p1, p2, p3)
    ns = (sums[0], sums[1], sums[2], n3)
    squares = [p * p for p in ps]
    base = (0.28 / 0.12) - ((squares[0] + squares[1]) + (squares[2] + squares[3]))
    m0, m1 = chem
    both = BETA * (m0 + m1)
    w2 = both + DRIFT
    ws = (w2 + (7.0 * BETA) * m0, w2 + (7.0 * BETA) * m1, w2, 3.5 * both)
    moved = [
        ns[a] + ps[a] * ((base + squares[a]) + ws[a] * (K - ps[a])) for a in range(4)
    ]
    excess = 0.25 * ((moved[0] + moved[1]) + (moved[2] + moved[3])) - 0.25 * TOP
    clipped = [jnp.minimum(jnp.maximum(u - excess, 0.0), TOP) for u in moved]
    scale = K / ((clipped[0] + clipped[1]) + (clipped[2] + clipped[3]))
    new = [s * scale for s in clipped]
    h = [x * x * (1.5 * K - x) for x in new]
    shared = (h[0] + h[1]) + (h[2] + 3.5 * h[3])
    solute = (shared + 7.0 * h[0], shared + 7.0 * h[1])
    mobility = 0.0075 + (0.1425 / K) * p3
    new_held = [held[i] + mobility * (chem_sums[i] - 6.0 * chem[i]) for i in range(2)]
    new_chem = [new_held[i] - solute[i] for i in range(2)]
    return new, new_chem, new_held


class Half:
    def __init__(self, base, strip_base, n, cells, codes, across, own, up, grow, wing):
        self.base, self.strip_base, self.n = base, strip_base, n
        self.cells, self.codes, self.across = cells, codes, across
        self.own, self.up, self.grow, self.wing, self.lane = own, up, grow, wing, lanes()

    def source(self, p):
        up = p >= OWN
        i = p - OWN if up else p
        q, c = divmod(i, PACK)
        return up, i, q, c

    def store(self, dst, index, rows, label, m0, m1, mask=None):
        values = [jnp.where(label == a, K, 0.0) for a in range(3)]
        rest = jnp.where(label == 3.0, 3.5 * HALF, HALF)
        values += [ALPHA * m0, ALPHA * m1]
        values += [values[3 + i] + jnp.where(label == i, 8.0 * HALF, rest) for i in range(2)]
        for f, value in enumerate(values):
            if mask is not None:
                value = jnp.where(mask, value, dst[f, index, rows, :])
            dst[f, index, rows, :] = value

    def fill(self, dst, p):
        up, i, _, _ = self.source(p)
        body = [self.grow[f, i] if up else self.cells[f, i + 11] for f in range(3)]
        self.store(dst, p - self.base, slice(ROW0, ROW0 + 8), *body)
        for hi, ref in enumerate(self.up if up else self.own):
            count = reach(i, up)
            if count:
                places = UP_PLAN if up else OWN_PLAN
                body = []
                for f in range(3):
                    at, _ = places["cell", f, i]
                    body.append(ref[at : at + count])
                row = ROW0 - count if hi else ROW0 + 8
                self.store(dst, p - self.base, slice(row, row + count), *body)

    def pieces(self, p, f, block):
        up, i, q, _ = self.source(p)
        if block == 0:
            if up:
                return self.grow[f, i], self.grow[f, OWN + q]
            return self.cells[f, i + 11], self.across[3 * f + q + 1]
        places = UP_PLAN if up else OWN_PLAN
        ref = (self.up if up else self.own)[block - 1]
        at, count = places["cell", f, i]
        at = at if block == 1 else at + count - DEEP
        edge, _ = places["edge", f, q]
        return ref[at : at + DEEP], ref[edge : edge + DEEP]

    def joined(self, parts):
        rows = next(part for part in parts if part is not None)[0].shape[0]
        lane = lax.broadcasted_iota(jnp.int32, (rows, 128), 1)
        total = jnp.zeros((rows, 128), jnp.float32)
        for j, part in enumerate(parts):
            if part is None:
                continue
            value, edge, before, after = part
            at = 20 * j
            tile = jnp.where(
                lane < at + 10,
                jnp.where(lane < at + 5, pltpu.roll(edge, before % 128, 1), pltpu.roll(value, at + 5, 1)),
                jnp.where(lane < at + 15, pltpu.roll(value, (at + 15) % 128, 1), pltpu.roll(edge, after % 128, 1)),
            )
            total = jnp.where(lane >= at, tile, total)
        return total

    def fill_strips(self, dst, top):
        for index in range(self.n):
            for block, row, _ in BLOCKS:
                body = []
                for f in range(3):
                    parts = []
                    for j in range(6):
                        p = self.strip_base + self.n * j + index
                        if p >= top:
                            parts.append(None)
                            continue
                        c = self.source(p)[3]
                        parts.append(
                            (*self.pieces(p, f, block), 20 * j - 10 * c, 20 * j + 10 - 10 * c)
                        )
                    body.append(self.joined(parts))
                self.store(dst, index, slice(row, row + body[0].shape[0]), *body)

    def melt(self, dst, strips, table):
        def chem(code, i):
            value = jnp.zeros_like(code)
            for level in range(8):
                value = jnp.where(code == level, table[i, level], value)
            return value

        def rows(block, e):
            if block == 0:
                return self.codes[e], self.across[9]
            ref = self.up[block - 1]
            at, _ = CODE_PLAN["code", 0, e]
            edge, _ = CODE_PLAN["code_edge", 0, 0]
            return ref[at : at + 2], ref[edge : edge + 2]

        for e in range(SHIFT):
            for block, row, count in MELT_BLOCKS:
                code = rows(block, e)[0]
                label = jnp.full_like(code, 3.0)
                where = slice(row, row + count)
                self.store(dst, OWN + e - self.base, where, label, chem(code, 0), chem(code, 1))
        for index in range(self.n):
            for block, row, count in MELT_BLOCKS:
                parts, groups = [], []
                for j in range(6):
                    e = self.strip_base + self.n * j + index - OWN
                    if not 0 <= e < SHIFT:
                        parts.append(None)
                        continue
                    groups.append(j)
                    parts.append((*rows(block, e), 20 * j + 1 - 8 * e, 20 * j + 11 - 8 * e))
                code = self.joined(parts)
                lane = lax.broadcasted_iota(jnp.int32, code.shape, 1)
                mask = (lane >= 20 * groups[0]) & (lane < 20 * groups[-1] + 20)
                label = jnp.full_like(code, 3.0)
                where = slice(row, row + count)
                self.store(strips, index, where, label, chem(code, 0), chem(code, 1), mask)

    def repeat(self, dst, p, source):
        for f in range(5):
            dst[f, p - self.base, 7:25, :] = dst[f, source - self.base, 7:25, :]

    def repeat_strip(self, strips, p, source):
        j, index = divmod(p - self.strip_base, self.n)
        j_from, index_from = divmod(source - self.strip_base, self.n)
        lane = lax.broadcasted_iota(jnp.int32, (18, 128), 1)
        mask = (lane >= 20 * j) & (lane < 20 * j + 20)
        for f in range(5):
            value = strips[f, index_from, 7:25, :]
            if j != j_from:
                value = pltpu.roll(value, 20 * (j - j_from), 1)
            strips[f, index, 7:25, :] = jnp.where(mask, value, strips[f, index, 7:25, :])

    def advance(self, src, index, row, fetch, sides):
        here, sums = [], []
        for f in range(5):
            mid = src[f, index, row : row + 8, :]
            below, above = fetch(f)
            total = (below + above) + (
                src[f, index, row - 1 : row + 7, :] + src[f, index, row + 1 : row + 9, :]
            )
            left, right = sides(f, mid)
            here.append(mid)
            sums.append(total + (left + right))
        held = [src[f, index, row : row + 8, :] for f in (5, 6)]
        return react(here[:3], sums[:3], here[3:], sums[3:], held)

    def spread(self, strips, rows):
        second = self.lane == 3
        for j in range(1, 6):
            second = second | (self.lane == 20 * j + 3)
        for f in range(5):
            for index in range(self.n):
                for row in rows:
                    tile = strips[f, index, row : row + 8, :]
                    tile = jnp.where(second, pltpu.roll(tile, 116, 1), tile)
                    self.wing[f, index, row : row + 8, :] = tile

    def plane_step(self, src, p, row):
        index = p - self.base
        q = p - self.strip_base
        j = (q * 13) >> 6 if self.n == 5 else q >> 2
        at = q - self.n * j
        turn = 124 - 20 * j
        rows = slice(row, row + 8)

        def fetch(f):
            return src[f, index - 1, rows, :], src[f, index + 1, rows, :]

        def sides(f, mid):
            beyond = pltpu.roll(self.wing[f, at, rows, :], turn, 1)
            left = jnp.where(self.lane == 0, beyond, pltpu.roll(mid, 1, 1))
            return left, jnp.where(self.lane == 127, beyond, pltpu.roll(mid, 127, 1))

        return self.advance(src, index, row, fetch, sides)

    def planes(self, first, count, body):
        whole = count - count % 8
        if whole:
            pl.loop(first, first + whole, unroll=8)(body)
        for p in range(first + whole, first + count):
            body(p)

    def sweep(self, src, dst, src_strips, dst_strips, first, count):
        self.spread(src_strips, (8, 16))

        def body(p):
            for row in (8, 16):
                new, chem, held = self.plane_step(src, p, row)
                for f, value in enumerate((*new[:3], *chem, *held)):
                    dst[f, p - self.base, row : row + 8, :] = value

        self.planes(first, count, body)
        last = self.n - 1

        def inside(f, mid):
            return pltpu.roll(mid, 1, 1), pltpu.roll(mid, 127, 1)

        for index in range(self.n):
            for row in (8, 16):
                rows = slice(row, row + 8)

                def fetch(f, index=index, rows=rows):
                    if index:
                        below = src_strips[f, index - 1, rows, :]
                    else:
                        below = pltpu.roll(src_strips[f, last, rows, :], 20, 1)
                    if index < last:
                        above = src_strips[f, index + 1, rows, :]
                    else:
                        above = pltpu.roll(src_strips[f, 0, rows, :], 108, 1)
                    return below, above

                new, chem, held = self.advance(
                    src_strips, index, row, fetch, inside
                )
                for f, value in enumerate((*new[:3], *chem, *held)):
                    dst_strips[f, index, row : row + 8, :] = value

    def finish(self, src, first, count, phases, chems, at=0):
        def body(p):
            new, chem, _ = self.plane_step(src, p, ROW0)
            for a in range(4):
                phases[a, p - first + at] = new[a] * (1.0 / K)
            for i in range(2):
                chems[i, p - first + at] = chem[i] * (1.0 / ALPHA)

        self.planes(first, count, body)


BLOCKS = ((0, ROW0, 8), (1, ROW0 + 8, DEEP), (2, ROW0 - DEEP, DEEP))
MELT_BLOCKS = ((0, ROW0, 8), (1, ROW0 + 8, 2), (2, ROW0 - 2, 2))
LOWER = 11


def lower_half(
    cells, across, swap_one, swap_two,
    phases, chems, seam, rows_lo, rows_hi,
    one, two, strip_one, strip_two, wing,
):
    first, _ = place()

    def sort_rows(even):
        rows_lo[...] = (swap_two if even else swap_one)[...]
        rows_hi[...] = (swap_one if even else swap_two)[...]

    by_parity(sort_rows)
    half = Half(0, 0, 4, cells, None, across, (rows_lo, rows_hi), None, None, wing)
    for p in range(OWN):
        half.fill(one, p)
    half.fill_strips(strip_one, OWN)
    src, dst, src_strips, dst_strips = one, two, strip_one, strip_two
    for s in range(1, 5):
        if s == 4:

            @pl.when(first)
            def _(src=src, src_strips=src_strips):
                half.repeat(src, 4, 5)
                half.repeat_strip(src_strips, 4, 5)

        half.sweep(src, dst, src_strips, dst_strips, s, OWN - 2 * s)
        for f in range(7):
            for i in range(2):
                seam[s - 1, f, i] = dst[f, OWN - 1 - s + i - 1, 8:24, :]
        src, dst, src_strips, dst_strips = dst, src, dst_strips, src_strips

    @pl.when(first)
    def _(src=src):
        half.repeat(src, 4, 5)

    half.spread(src_strips, (ROW0,))
    half.finish(src, 5, LOWER, phases, chems)


def delivery(phases, chems, phases_out, chem_out, first, at, count, sems, s):
    source, target = pl.ds(at, count), pl.ds(first, count)
    copies = [
        pltpu.make_async_copy(phases.at[:, source], phases_out.at[:, target], sems.at[s]),
        pltpu.make_async_copy(chems.at[:, source], chem_out.at[:, target], sems.at[s + 1]),
    ]
    for copy in copies:
        copy.start()
    return copies


def upper_half(
    cells, codes, table_in, across, own_lo, own_hi, swap_one, swap_two, grow, seam,
    lower_phases, lower_chems, phases_out, chem_out,
    one, two, strip_one, strip_two, wing, phases, chems, up_lo, up_hi, table, sem, sems,
):
    outs = (phases_out, chem_out)
    copies = delivery(lower_phases, lower_chems, *outs, 0, 0, LOWER, sems, 0)
    _, last = place()

    def sort_rows(even):
        up_lo[...] = (swap_two if even else swap_one)[...]
        up_hi[...] = (swap_one if even else swap_two)[...]

    by_parity(sort_rows)
    half = Half(
        15, 12, 5, cells, codes, across, (own_lo, own_hi), (up_lo, up_hi), grow, wing
    )
    for p in range(OWN - 2, PLANES):
        half.fill(one, p)
    half.fill_strips(strip_one, PLANES)
    src, dst, src_strips, dst_strips = one, two, strip_one, strip_two
    for s in range(1, 6):
        if s > 1:
            for f in range(7):
                for i in range(2):
                    src[f, OWN - 1 - s + i - half.base, 8:24, :] = seam[s - 2, f, i]
        if s < 4:

            @pl.when(last)
            def _(src=src, src_strips=src_strips):
                half.repeat(src, OWN, OWN - 1)
                half.repeat_strip(src_strips, OWN, OWN - 1)

        if s == 4:

            @pl.when(last)
            def _(src=src, src_strips=src_strips):
                copy = pltpu.make_async_copy(table_in, table, sem)
                copy.start()
                copy.wait()
                half.melt(src, src_strips, table)
                half.repeat_strip(src_strips, OWN + SHIFT, OWN + SHIFT - 1)

        if s >= 4:

            @pl.when(last)
            def _(src=src):
                half.repeat(src, OWN + SHIFT, OWN + SHIFT - 1)

        if s < 5:
            half.sweep(src, dst, src_strips, dst_strips, OWN - s, OWN)
            src, dst, src_strips, dst_strips = dst, src, dst_strips, src_strips
    half.spread(src_strips, (ROW0,))
    half.finish(src, OWN - 5, 12, phases, chems)
    copies += delivery(phases, chems, *outs, LOWER, 0, 12, sems, 2)
    half.finish(src, OWN + 7, 9, phases, chems, 12)
    copies += delivery(phases, chems, *outs, LOWER + 12, 12, 9, sems, 4)
    for copy in copies:
        copy.wait()


def on_device(labels, potential, melt_codes, melt_table):
    n_grow, n_gy, n_gz = (lax.axis_size(a) for a in AXES)

    def send(value, dg, dy, dz):
        pairs = []
        for g in range(n_grow):
            for y in range(n_gy):
                for z in range(n_gz):
                    side = (z + dz + (not 0 <= g + dg < n_grow)) % n_gz
                    to = ((g + dg) % n_grow * n_gy + (y + dy) % n_gy) * n_gz + side
                    pairs.append(((g * n_gy + y) * n_gz + z, to))
        return lax.ppermute(value, AXES, pairs)

    def f32(*shape):
        return jax.ShapeDtypeStruct(shape, jnp.float32)

    params = pltpu.CompilerParams(vmem_limit_bytes=48 << 20)
    cells, codes, edges = pl.pallas_call(
        first_pack,
        in_specs=[HBM] * 3,
        out_specs=[VMEM] * 3,
        out_shape=[f32(3, 32, 8, 128), f32(SHIFT, 8, 128), f32(10, 8, 128)],
        scratch_shapes=[
            pltpu.VMEM((32, 8, 128), jnp.int32),
            pltpu.VMEM((SHIFT, 8, 128), jnp.int32),
            pltpu.SemaphoreType.DMA((3,)),
        ],
        compiler_params=params,
        name="first_pack",
    )(*(pltpu.with_memory_space_constraint(x, pltpu.MemorySpace.HBM) for x in (labels, potential, melt_codes)))
    across = send(edges, 0, 0, 1)
    own_one, own_two, grow = pl.pallas_call(
        second_pack,
        in_specs=[VMEM] * 2,
        out_specs=[VMEM] * 3,
        out_shape=[f32(OWN_ROWS, 128)] * 2 + [f32(3, OWN + 2, 8, 128)],
        compiler_params=params,
        name="second_pack",
    )(cells, across)

    def swap(one, two):
        below = [(y, (y + (1 if y % 2 else -1)) % n_gy) for y in range(n_gy)]
        above = [(y, (y + (-1 if y % 2 else 1)) % n_gy) for y in range(n_gy)]
        return lax.ppermute(one, "gy", below), lax.ppermute(two, "gy", above)

    own_one, own_two = swap(own_one, own_two)
    grow = send(grow, -1, 0, 0)
    up_one, up_two = pl.pallas_call(
        third_pack,
        in_specs=[VMEM] * 3,
        out_specs=[VMEM] * 2,
        out_shape=[f32(UP_ROWS, 128)] * 2,
        compiler_params=params,
        name="third_pack",
    )(grow, codes, across)
    up_one, up_two = swap(up_one, up_two)

    def buffers(planes, strips):
        return (
            [pltpu.VMEM((7, planes, PITCH, 128), jnp.float32)] * 2
            + [pltpu.VMEM((7, strips, PITCH, 128), jnp.float32)] * 2
            + [pltpu.VMEM((5, strips, PITCH, 128), jnp.float32)]
        )

    phases, chems, seam, own_lo, own_hi = pl.pallas_call(
        lower_half,
        in_specs=[VMEM] * 4,
        out_specs=[VMEM] * 5,
        out_shape=[f32(4, LOWER, 8, 128), f32(2, LOWER, 8, 128), f32(4, 7, 2, 16, 128)]
        + [f32(OWN_ROWS, 128)] * 2,
        scratch_shapes=buffers(OWN, 4),
        compiler_params=params,
        cost_estimate=pl.CostEstimate(
            flops=60_000_000, bytes_accessed=12_000_000, transcendentals=0
        ),
        name="lower_half",
    )(cells, across, own_one, own_two)
    table = pltpu.with_memory_space_constraint(melt_table, pltpu.MemorySpace.HBM)
    return pl.pallas_call(
        upper_half,
        in_specs=[VMEM, VMEM, HBM] + [VMEM] * 9,
        out_specs=[HBM, HBM],
        out_shape=[f32(4, 32, 8, 128), f32(2, 32, 8, 128)],
        scratch_shapes=buffers(27, 5)
        + [
            pltpu.VMEM((4, OWN, 8, 128), jnp.float32),
            pltpu.VMEM((2, OWN, 8, 128), jnp.float32),
            pltpu.VMEM((UP_ROWS, 128), jnp.float32),
            pltpu.VMEM((UP_ROWS, 128), jnp.float32),
            pltpu.SMEM((2, 8), jnp.float32),
            pltpu.SemaphoreType.DMA,
            pltpu.SemaphoreType.DMA((6,)),
        ],
        compiler_params=params,
        name="upper_half",
    )(cells, codes, table, across, own_lo, own_hi, up_one, up_two, grow, seam, phases, chems)


def solution(mesh):
    return jax.shard_map(
        on_device,
        mesh=mesh,
        in_specs=(P("grow", "gy", "gz"), P(None, "grow", "gy", "gz"), P(None, "gy", "gz"), P()),
        out_specs=(P(None, "grow", "gy", "gz"), P(None, "grow", "gy", "gz")),
        check_vma=False,
    )
```

```python
import jax
import jax.numpy as jnp
from jax import lax
from jax.experimental import pallas as pl
from jax.experimental.pallas import tpu as pltpu
from jax.sharding import PartitionSpec as P

K = 5.0**0.5
ALPHA = 5.0 * K**3
BETA = 2.5 / (K * ALPHA)
TOP = K / 0.12
DRIFT = 0.15 / (0.12 * K)
HALF = 0.5 * K**3

SHIFT = 16
OWN = 21
PLANES = 2 * OWN
PITCH = 32
ROW0 = 12
DEEP = 5
PACK = 11
AXES = ("grow", "gy", "gz")
VMEM = pl.BlockSpec(memory_space=pltpu.VMEM)
HBM = pl.BlockSpec(memory_space=pltpu.MemorySpace.HBM)


def lanes():
    return lax.broadcasted_iota(jnp.int32, (8, 128), 1)


def reach(i, up):
    return min(DEEP, OWN - 1 - i if up else i)


def plan(up):
    places, at = {}, 8
    for f in range(3):
        for i in range(OWN):
            places["cell", f, i] = (at, reach(i, up))
            at += reach(i, up)
        for q in range(2):
            places["edge", f, q] = (at, DEEP)
            at += DEEP
    return places, -(-at // 8) * 8


OWN_PLAN, OWN_ROWS = plan(False)
UP_PLAN, UP_ROWS = plan(True)
CODE_PLAN = {("code", 0, e): (8 + 2 * e, 2) for e in range(SHIFT)}
CODE_PLAN["code_edge", 0, 0] = (8 + 2 * SHIFT, 2)


def first_pack(labels, potential, codes, cells, codes_out, edges, labels_in, codes_in, sems):
    copies = [
        pltpu.make_async_copy(labels, labels_in, sems.at[0]),
        pltpu.make_async_copy(potential, cells.at[1:3], sems.at[1]),
        pltpu.make_async_copy(codes, codes_in, sems.at[2]),
    ]
    for copy in copies:
        copy.start()
    lane = lanes()

    def packed(tiles, width, offset):
        total = jnp.zeros((8, 128), jnp.float32)
        for c, tile in enumerate(tiles):
            there = (lane >= width * c) & (lane < width * (c + 1))
            total = jnp.where(there, pltpu.roll(tile, (width * c + offset) % 128, 1), total)
        return total

    copies[0].wait()
    for p in range(32):
        cells[0, p] = labels_in[p].astype(jnp.float32)
    copies[2].wait()
    for e in range(SHIFT):
        codes_out[e] = codes_in[e].astype(jnp.float32)
    edges[9] = packed([codes_out[e] for e in range(SHIFT)], 8, 4)
    copies[1].wait()
    for f in range(3):
        for q in range(3):
            planes = range(PACK * q, min(PACK * q + PACK, 32))
            edges[3 * f + q] = packed([cells[f, p] for p in planes], 10, 5)


def put(lo, hi, place, tile):
    at, count = place
    if count:
        lo[at : at + count] = tile[0:count]
        hi[at : at + count] = tile[8 - count : 8]


def by_parity(body):
    even = lax.rem(lax.axis_index("gy"), 2) == 0
    pl.when(even)(lambda: body(True))
    pl.when(jnp.logical_not(even))(lambda: body(False))


def second_pack(cells, across, one, two, grow):
    by_parity(lambda even: own_rows(cells, across, *((one, two) if even else (two, one))))
    for f in range(3):
        grow[f, 0:OWN] = cells[f, 0:OWN]
        grow[f, OWN : OWN + 2] = across[3 * f : 3 * f + 2]


def own_rows(cells, across, own_lo, own_hi):
    for f in range(3):
        for i in range(OWN):
            put(own_lo, own_hi, OWN_PLAN["cell", f, i], cells[f, i + 11])
        for q in range(2):
            put(own_lo, own_hi, OWN_PLAN["edge", f, q], across[3 * f + q + 1])
    for ref in (own_lo, own_hi):
        blank(ref, OWN_PLAN, OWN_ROWS)


def blank(ref, places, rows):
    used = max(at + count for at, count in places.values())
    ref[0:8] = jnp.zeros((8, 128), jnp.float32)
    if used < rows:
        ref[used:rows] = jnp.zeros((rows - used, 128), jnp.float32)


def third_pack(grow, codes, across, one, two):
    by_parity(lambda even: up_rows(grow, codes, across, *((one, two) if even else (two, one))))


def place():
    index = lax.axis_index("grow")
    return index == 0, index == lax.axis_size("grow") - 1


def up_rows(grow, codes, across, up_lo, up_hi):
    _, last = place()
    for ref in (up_lo, up_hi):
        blank(ref, UP_PLAN, UP_ROWS)

    @pl.when(jnp.logical_not(last))
    def _():
        for f in range(3):
            for i in range(OWN):
                put(up_lo, up_hi, UP_PLAN["cell", f, i], grow[f, i])
            for q in range(2):
                put(up_lo, up_hi, UP_PLAN["edge", f, q], grow[f, OWN + q])

    @pl.when(last)
    def _():
        for ref in (up_lo, up_hi):
            ref[...] = jnp.zeros((UP_ROWS, 128), jnp.float32)
        for e in range(SHIFT):
            put(up_lo, up_hi, CODE_PLAN["code", 0, e], codes[e])
        put(up_lo, up_hi, CODE_PLAN["code_edge", 0, 0], across[9])


def react(phases, sums, chem, chem_sums, held):
    p0, p1, p2 = phases
    p3 = K - ((p0 + p1) + p2)
    n3 = 6.0 * K - ((sums[0] + sums[1]) + sums[2])
    ps = (p0, p1, p2, p3)
    ns = (sums[0], sums[1], sums[2], n3)
    squares = [p * p for p in ps]
    base = (0.28 / 0.12) - ((squares[0] + squares[1]) + (squares[2] + squares[3]))
    m0, m1 = chem
    both = BETA * (m0 + m1)
    w2 = both + DRIFT
    ws = (w2 + (7.0 * BETA) * m0, w2 + (7.0 * BETA) * m1, w2, 3.5 * both)
    moved = [
        ns[a] + ps[a] * ((base + squares[a]) + ws[a] * (K - ps[a])) for a in range(4)
    ]
    excess = 0.25 * ((moved[0] + moved[1]) + (moved[2] + moved[3])) - 0.25 * TOP
    clipped = [jnp.minimum(jnp.maximum(u - excess, 0.0), TOP) for u in moved]
    scale = K / ((clipped[0] + clipped[1]) + (clipped[2] + clipped[3]))
    new = [s * scale for s in clipped]
    h = [x * x * (1.5 * K - x) for x in new]
    shared = (h[0] + h[1]) + (h[2] + 3.5 * h[3])
    solute = (shared + 7.0 * h[0], shared + 7.0 * h[1])
    mobility = 0.0075 + (0.1425 / K) * p3
    new_held = [held[i] + mobility * (chem_sums[i] - 6.0 * chem[i]) for i in range(2)]
    new_chem = [new_held[i] - solute[i] for i in range(2)]
    return new, new_chem, new_held


class Half:
    def __init__(self, base, strip_base, n, cells, codes, across, own, up, grow, wing):
        self.base, self.strip_base, self.n = base, strip_base, n
        self.cells, self.codes, self.across = cells, codes, across
        self.own, self.up, self.grow, self.wing, self.lane = own, up, grow, wing, lanes()

    def source(self, p):
        up = p >= OWN
        i = p - OWN if up else p
        q, c = divmod(i, PACK)
        return up, i, q, c

    def store(self, dst, index, rows, label, m0, m1, mask=None):
        values = [jnp.where(label == a, K, 0.0) for a in range(3)]
        rest = jnp.where(label == 3.0, 3.5 * HALF, HALF)
        values += [ALPHA * m0, ALPHA * m1]
        values += [values[3 + i] + jnp.where(label == i, 8.0 * HALF, rest) for i in range(2)]
        for f, value in enumerate(values):
            if mask is not None:
                value = jnp.where(mask, value, dst[f, index, rows, :])
            dst[f, index, rows, :] = value

    def fill(self, dst, p):
        up, i, _, _ = self.source(p)
        body = [self.grow[f, i] if up else self.cells[f, i + 11] for f in range(3)]
        self.store(dst, p - self.base, slice(ROW0, ROW0 + 8), *body)
        for hi, ref in enumerate(self.up if up else self.own):
            count = reach(i, up)
            if count:
                places = UP_PLAN if up else OWN_PLAN
                body = []
                for f in range(3):
                    at, _ = places["cell", f, i]
                    body.append(ref[at : at + count])
                row = ROW0 - count if hi else ROW0 + 8
                self.store(dst, p - self.base, slice(row, row + count), *body)

    def pieces(self, p, f, block):
        up, i, q, _ = self.source(p)
        if block == 0:
            if up:
                return self.grow[f, i], self.grow[f, OWN + q]
            return self.cells[f, i + 11], self.across[3 * f + q + 1]
        places = UP_PLAN if up else OWN_PLAN
        ref = (self.up if up else self.own)[block - 1]
        at, count = places["cell", f, i]
        at = at if block == 1 else at + count - DEEP
        edge, _ = places["edge", f, q]
        return ref[at : at + DEEP], ref[edge : edge + DEEP]

    def joined(self, parts):
        rows = next(part for part in parts if part is not None)[0].shape[0]
        lane = lax.broadcasted_iota(jnp.int32, (rows, 128), 1)
        total = jnp.zeros((rows, 128), jnp.float32)
        for j, part in enumerate(parts):
            if part is None:
                continue
            value, edge, before, after = part
            at = 20 * j
            tile = jnp.where(
                lane < at + 10,
                jnp.where(lane < at + 5, pltpu.roll(edge, before % 128, 1), pltpu.roll(value, at + 5, 1)),
                jnp.where(lane < at + 15, pltpu.roll(value, (at + 15) % 128, 1), pltpu.roll(edge, after % 128, 1)),
            )
            total = jnp.where(lane >= at, tile, total)
        return total

    def fill_strips(self, dst, top, blocks):
        for index in range(self.n):
            for block, row, _ in blocks:
                body = []
                for f in range(3):
                    parts = []
                    for j in range(6):
                        p = self.strip_base + self.n * j + index
                        if p >= top:
                            parts.append(None)
                            continue
                        c = self.source(p)[3]
                        parts.append(
                            (*self.pieces(p, f, block), 20 * j - 10 * c, 20 * j + 10 - 10 * c)
                        )
                    body.append(self.joined(parts))
                self.store(dst, index, slice(row, row + body[0].shape[0]), *body)

    def melt(self, dst, strips, table):
        def chem(code, i):
            value = jnp.zeros_like(code)
            for level in range(8):
                value = jnp.where(code == level, table[i, level], value)
            return value

        def rows(block, e):
            if block == 0:
                return self.codes[e], self.across[9]
            ref = self.up[block - 1]
            at, _ = CODE_PLAN["code", 0, e]
            edge, _ = CODE_PLAN["code_edge", 0, 0]
            return ref[at : at + 2], ref[edge : edge + 2]

        for e in range(SHIFT):
            for block, row, count in MELT_BLOCKS:
                code = rows(block, e)[0]
                label = jnp.full_like(code, 3.0)
                where = slice(row, row + count)
                self.store(dst, OWN + e - self.base, where, label, chem(code, 0), chem(code, 1))
        for index in range(self.n):
            for block, row, count in MELT_BLOCKS:
                parts, groups = [], []
                for j in range(6):
                    e = self.strip_base + self.n * j + index - OWN
                    if not 0 <= e < SHIFT:
                        parts.append(None)
                        continue
                    groups.append(j)
                    parts.append((*rows(block, e), 20 * j + 1 - 8 * e, 20 * j + 11 - 8 * e))
                code = self.joined(parts)
                lane = lax.broadcasted_iota(jnp.int32, code.shape, 1)
                mask = (lane >= 20 * groups[0]) & (lane < 20 * groups[-1] + 20)
                label = jnp.full_like(code, 3.0)
                where = slice(row, row + count)
                self.store(strips, index, where, label, chem(code, 0), chem(code, 1), mask)

    def repeat(self, dst, p, source):
        for f in range(5):
            dst[f, p - self.base, 7:25, :] = dst[f, source - self.base, 7:25, :]

    def repeat_strip(self, strips, p, source):
        j, index = divmod(p - self.strip_base, self.n)
        j_from, index_from = divmod(source - self.strip_base, self.n)
        lane = lax.broadcasted_iota(jnp.int32, (18, 128), 1)
        mask = (lane >= 20 * j) & (lane < 20 * j + 20)
        for f in range(5):
            value = strips[f, index_from, 7:25, :]
            if j != j_from:
                value = pltpu.roll(value, 20 * (j - j_from), 1)
            strips[f, index, 7:25, :] = jnp.where(mask, value, strips[f, index, 7:25, :])

    def advance(self, src, index, row, fetch, sides):
        here, sums = [], []
        for f in range(5):
            mid = src[f, index, row : row + 8, :]
            below, above = fetch(f)
            total = (below + above) + (
                src[f, index, row - 1 : row + 7, :] + src[f, index, row + 1 : row + 9, :]
            )
            left, right = sides(f, mid)
            here.append(mid)
            sums.append(total + (left + right))
        held = [src[f, index, row : row + 8, :] for f in (5, 6)]
        return react(here[:3], sums[:3], here[3:], sums[3:], held)

    def spread(self, strips, rows):
        second = self.lane == 3
        for j in range(1, 6):
            second = second | (self.lane == 20 * j + 3)
        for f in range(5):
            for index in range(self.n):
                for row in rows:
                    tile = strips[f, index, row : row + 8, :]
                    tile = jnp.where(second, pltpu.roll(tile, 116, 1), tile)
                    self.wing[f, index, row : row + 8, :] = tile

    def plane_step(self, src, p, row):
        index = p - self.base
        q = p - self.strip_base
        j = (q * 13) >> 6 if self.n == 5 else q >> 2
        at = q - self.n * j
        turn = 124 - 20 * j
        rows = slice(row, row + 8)

        def fetch(f):
            return src[f, index - 1, rows, :], src[f, index + 1, rows, :]

        def sides(f, mid):
            beyond = pltpu.roll(self.wing[f, at, rows, :], turn, 1)
            left = jnp.where(self.lane == 0, beyond, pltpu.roll(mid, 1, 1))
            return left, jnp.where(self.lane == 127, beyond, pltpu.roll(mid, 127, 1))

        return self.advance(src, index, row, fetch, sides)

    def planes(self, first, count, body):
        whole = count - count % 8
        if whole:
            pl.loop(first, first + whole, unroll=8)(body)
        for p in range(first + whole, first + count):
            body(p)

    def sweep(self, src, dst, src_strips, dst_strips, first, count):
        self.spread(src_strips, (8, 16))

        def body(p):
            for row in (8, 16):
                new, chem, held = self.plane_step(src, p, row)
                for f, value in enumerate((*new[:3], *chem, *held)):
                    dst[f, p - self.base, row : row + 8, :] = value

        self.planes(first, count, body)
        last = self.n - 1

        def inside(f, mid):
            return pltpu.roll(mid, 1, 1), pltpu.roll(mid, 127, 1)

        for index in range(self.n):
            for row in (8, 16):
                rows = slice(row, row + 8)

                def fetch(f, index=index, rows=rows):
                    if index:
                        below = src_strips[f, index - 1, rows, :]
                    else:
                        below = pltpu.roll(src_strips[f, last, rows, :], 20, 1)
                    if index < last:
                        above = src_strips[f, index + 1, rows, :]
                    else:
                        above = pltpu.roll(src_strips[f, 0, rows, :], 108, 1)
                    return below, above

                new, chem, held = self.advance(
                    src_strips, index, row, fetch, inside
                )
                for f, value in enumerate((*new[:3], *chem, *held)):
                    dst_strips[f, index, row : row + 8, :] = value

    def finish(self, src, first, count, phases, chems, at=0):
        def body(p):
            new, chem, _ = self.plane_step(src, p, ROW0)
            for a in range(4):
                phases[a, p - first + at] = new[a] * (1.0 / K)
            for i in range(2):
                chems[i, p - first + at] = chem[i] * (1.0 / ALPHA)

        self.planes(first, count, body)


BLOCKS = ((0, ROW0, 8), (1, ROW0 + 8, DEEP), (2, ROW0 - DEEP, DEEP))
MELT_BLOCKS = ((0, ROW0, 8), (1, ROW0 + 8, 2), (2, ROW0 - 2, 2))
LOWER = 11


def strip_pack(cells, across, own_strips):
    half = Half(0, 0, 4, cells, None, across, None, None, None, None)
    half.fill_strips(own_strips, OWN, ((0, 0, 8),))


def lower_half(
    cells, across, own_strips, swap_one, swap_two,
    phases, chems, seam, rows_lo, rows_hi,
    one, two, strip_one, strip_two, wing,
):
    first, _ = place()

    def sort_rows(even):
        rows_lo[...] = (swap_two if even else swap_one)[...]
        rows_hi[...] = (swap_one if even else swap_two)[...]

    by_parity(sort_rows)
    half = Half(0, 0, 4, cells, None, across, (rows_lo, rows_hi), None, None, wing)
    for p in range(OWN):
        half.fill(one, p)
    strip_one[:, :, ROW0 : ROW0 + 8, :] = own_strips[...]
    half.fill_strips(strip_one, OWN, BLOCKS[1:])
    src, dst, src_strips, dst_strips = one, two, strip_one, strip_two
    for s in range(1, 5):
        if s == 4:

            @pl.when(first)
            def _(src=src, src_strips=src_strips):
                half.repeat(src, 4, 5)
                half.repeat_strip(src_strips, 4, 5)

        half.sweep(src, dst, src_strips, dst_strips, s, OWN - 2 * s)
        for f in range(7):
            for i in range(2):
                seam[s - 1, f, i] = dst[f, OWN - 1 - s + i - 1, 8:24, :]
        src, dst, src_strips, dst_strips = dst, src, dst_strips, src_strips

    @pl.when(first)
    def _(src=src):
        half.repeat(src, 4, 5)

    half.spread(src_strips, (ROW0,))
    half.finish(src, 5, LOWER, phases, chems)


def delivery(phases, chems, phases_out, chem_out, first, at, count, sems, s):
    source, target = pl.ds(at, count), pl.ds(first, count)
    copies = [
        pltpu.make_async_copy(phases.at[:, source], phases_out.at[:, target], sems.at[s]),
        pltpu.make_async_copy(chems.at[:, source], chem_out.at[:, target], sems.at[s + 1]),
    ]
    for copy in copies:
        copy.start()
    return copies


def upper_half(
    cells, codes, table_in, across, own_lo, own_hi, swap_one, swap_two, grow, seam,
    lower_phases, lower_chems, phases_out, chem_out,
    one, two, strip_one, strip_two, wing, phases, chems, up_lo, up_hi, table, sem, sems,
):
    outs = (phases_out, chem_out)
    copies = delivery(lower_phases, lower_chems, *outs, 0, 0, LOWER, sems, 0)
    _, last = place()

    def sort_rows(even):
        up_lo[...] = (swap_two if even else swap_one)[...]
        up_hi[...] = (swap_one if even else swap_two)[...]

    by_parity(sort_rows)
    half = Half(
        15, 12, 5, cells, codes, across, (own_lo, own_hi), (up_lo, up_hi), grow, wing
    )
    for p in range(OWN - 2, PLANES):
        half.fill(one, p)
    half.fill_strips(strip_one, PLANES, BLOCKS)
    src, dst, src_strips, dst_strips = one, two, strip_one, strip_two
    for s in range(1, 6):
        if s > 1:
            for f in range(7):
                for i in range(2):
                    src[f, OWN - 1 - s + i - half.base, 8:24, :] = seam[s - 2, f, i]
        if s < 4:

            @pl.when(last)
            def _(src=src, src_strips=src_strips):
                half.repeat(src, OWN, OWN - 1)
                half.repeat_strip(src_strips, OWN, OWN - 1)

        if s == 4:

            @pl.when(last)
            def _(src=src, src_strips=src_strips):
                copy = pltpu.make_async_copy(table_in, table, sem)
                copy.start()
                copy.wait()
                half.melt(src, src_strips, table)
                half.repeat_strip(src_strips, OWN + SHIFT, OWN + SHIFT - 1)

        if s >= 4:

            @pl.when(last)
            def _(src=src):
                half.repeat(src, OWN + SHIFT, OWN + SHIFT - 1)

        if s < 5:
            half.sweep(src, dst, src_strips, dst_strips, OWN - s, OWN)
            src, dst, src_strips, dst_strips = dst, src, dst_strips, src_strips
    half.spread(src_strips, (ROW0,))
    half.finish(src, OWN - 5, 12, phases, chems)
    copies += delivery(phases, chems, *outs, LOWER, 0, 12, sems, 2)
    half.finish(src, OWN + 7, 9, phases, chems, 12)
    copies += delivery(phases, chems, *outs, LOWER + 12, 12, 9, sems, 4)
    for copy in copies:
        copy.wait()


def on_device(labels, potential, melt_codes, melt_table):
    n_grow, n_gy, n_gz = (lax.axis_size(a) for a in AXES)

    def send(value, dg, dy, dz):
        pairs = []
        for g in range(n_grow):
            for y in range(n_gy):
                for z in range(n_gz):
                    side = (z + dz + (not 0 <= g + dg < n_grow)) % n_gz
                    to = ((g + dg) % n_grow * n_gy + (y + dy) % n_gy) * n_gz + side
                    pairs.append(((g * n_gy + y) * n_gz + z, to))
        return lax.ppermute(value, AXES, pairs)

    def f32(*shape):
        return jax.ShapeDtypeStruct(shape, jnp.float32)

    params = pltpu.CompilerParams(vmem_limit_bytes=48 << 20)
    cells, codes, edges = pl.pallas_call(
        first_pack,
        in_specs=[HBM] * 3,
        out_specs=[VMEM] * 3,
        out_shape=[f32(3, 32, 8, 128), f32(SHIFT, 8, 128), f32(10, 8, 128)],
        scratch_shapes=[
            pltpu.VMEM((32, 8, 128), jnp.int32),
            pltpu.VMEM((SHIFT, 8, 128), jnp.int32),
            pltpu.SemaphoreType.DMA((3,)),
        ],
        compiler_params=params,
        name="first_pack",
    )(*(pltpu.with_memory_space_constraint(x, pltpu.MemorySpace.HBM) for x in (labels, potential, melt_codes)))
    across = send(edges, 0, 0, 1)
    own_one, own_two, grow = pl.pallas_call(
        second_pack,
        in_specs=[VMEM] * 2,
        out_specs=[VMEM] * 3,
        out_shape=[f32(OWN_ROWS, 128)] * 2 + [f32(3, OWN + 2, 8, 128)],
        compiler_params=params,
        name="second_pack",
    )(cells, across)

    def swap(one, two):
        below = [(y, (y + (1 if y % 2 else -1)) % n_gy) for y in range(n_gy)]
        above = [(y, (y + (-1 if y % 2 else 1)) % n_gy) for y in range(n_gy)]
        return lax.ppermute(one, "gy", below), lax.ppermute(two, "gy", above)

    own_one, own_two = swap(own_one, own_two)
    grow = send(grow, -1, 0, 0)
    up_one, up_two = pl.pallas_call(
        third_pack,
        in_specs=[VMEM] * 3,
        out_specs=[VMEM] * 2,
        out_shape=[f32(UP_ROWS, 128)] * 2,
        compiler_params=params,
        name="third_pack",
    )(grow, codes, across)
    up_one, up_two = swap(up_one, up_two)

    def buffers(planes, strips):
        return (
            [pltpu.VMEM((7, planes, PITCH, 128), jnp.float32)] * 2
            + [pltpu.VMEM((7, strips, PITCH, 128), jnp.float32)] * 2
            + [pltpu.VMEM((5, strips, PITCH, 128), jnp.float32)]
        )

    own_strips = pl.pallas_call(
        strip_pack,
        in_specs=[VMEM] * 2,
        out_specs=VMEM,
        out_shape=f32(7, 4, 8, 128),
        compiler_params=params,
        name="strip_pack",
    )(cells, across)
    phases, chems, seam, own_lo, own_hi = pl.pallas_call(
        lower_half,
        in_specs=[VMEM] * 5,
        out_specs=[VMEM] * 5,
        out_shape=[f32(4, LOWER, 8, 128), f32(2, LOWER, 8, 128), f32(4, 7, 2, 16, 128)]
        + [f32(OWN_ROWS, 128)] * 2,
        scratch_shapes=buffers(OWN, 4),
        compiler_params=params,
        cost_estimate=pl.CostEstimate(
            flops=60_000_000, bytes_accessed=12_000_000, transcendentals=0
        ),
        name="lower_half",
    )(cells, across, own_strips, own_one, own_two)
    table = pltpu.with_memory_space_constraint(melt_table, pltpu.MemorySpace.HBM)
    return pl.pallas_call(
        upper_half,
        in_specs=[VMEM, VMEM, HBM] + [VMEM] * 9,
        out_specs=[HBM, HBM],
        out_shape=[f32(4, 32, 8, 128), f32(2, 32, 8, 128)],
        scratch_shapes=buffers(27, 5)
        + [
            pltpu.VMEM((4, OWN, 8, 128), jnp.float32),
            pltpu.VMEM((2, OWN, 8, 128), jnp.float32),
            pltpu.VMEM((UP_ROWS, 128), jnp.float32),
            pltpu.VMEM((UP_ROWS, 128), jnp.float32),
            pltpu.SMEM((2, 8), jnp.float32),
            pltpu.SemaphoreType.DMA,
            pltpu.SemaphoreType.DMA((6,)),
        ],
        compiler_params=params,
        name="upper_half",
    )(cells, codes, table, across, own_lo, own_hi, up_one, up_two, grow, seam, phases, chems)


def solution(mesh):
    return jax.shard_map(
        on_device,
        mesh=mesh,
        in_specs=(P("grow", "gy", "gz"), P(None, "grow", "gy", "gz"), P(None, "gy", "gz"), P()),
        out_specs=(P(None, "grow", "gy", "gz"), P(None, "grow", "gy", "gz")),
        check_vma=False,
    )
```

```python
import jax
import jax.numpy as jnp
from jax import lax
from jax.experimental import pallas as pl
from jax.experimental.pallas import tpu as pltpu
from jax.sharding import PartitionSpec as P

K = 5.0**0.5
ALPHA = 5.0 * K**3
BETA = 2.5 / (K * ALPHA)
TOP = K / 0.12
DRIFT = 0.15 / (0.12 * K)
HALF = 0.5 * K**3

SHIFT = 16
OWN = 21
PLANES = 2 * OWN
PITCH = 32
ROW0 = 12
DEEP = 5
PACK = 11
AXES = ("grow", "gy", "gz")
VMEM = pl.BlockSpec(memory_space=pltpu.VMEM)
HBM = pl.BlockSpec(memory_space=pltpu.MemorySpace.HBM)


def lanes():
    return lax.broadcasted_iota(jnp.int32, (8, 128), 1)


def reach(i, up):
    return min(DEEP, OWN - 1 - i if up else i)


def plan(up):
    places, at = {}, 8
    for f in range(3):
        for i in range(OWN):
            places["cell", f, i] = (at, reach(i, up))
            at += reach(i, up)
        for q in range(2):
            places["edge", f, q] = (at, DEEP)
            at += DEEP
    return places, -(-at // 8) * 8


OWN_PLAN, OWN_ROWS = plan(False)
UP_PLAN, UP_ROWS = plan(True)
CODE_PLAN = {("code", 0, e): (8 + 2 * e, 2) for e in range(SHIFT)}
CODE_PLAN["code_edge", 0, 0] = (8 + 2 * SHIFT, 2)


def first_pack(labels, potential, codes, cells, codes_out, edges, labels_in, codes_in, sems):
    copies = [
        pltpu.make_async_copy(labels, labels_in, sems.at[0]),
        pltpu.make_async_copy(potential, cells.at[1:3], sems.at[1]),
        pltpu.make_async_copy(codes, codes_in, sems.at[2]),
    ]
    for copy in copies:
        copy.start()
    lane = lanes()

    def packed(tiles, width, offset):
        total = jnp.zeros((8, 128), jnp.float32)
        for c, tile in enumerate(tiles):
            there = (lane >= width * c) & (lane < width * (c + 1))
            total = jnp.where(there, pltpu.roll(tile, (width * c + offset) % 128, 1), total)
        return total

    copies[0].wait()
    for p in range(32):
        cells[0, p] = labels_in[p].astype(jnp.float32)
    copies[2].wait()
    for e in range(SHIFT):
        codes_out[e] = codes_in[e].astype(jnp.float32)
    edges[9] = packed([codes_out[e] for e in range(SHIFT)], 8, 4)
    copies[1].wait()
    for f in range(3):
        for q in range(3):
            planes = range(PACK * q, min(PACK * q + PACK, 32))
            edges[3 * f + q] = packed([cells[f, p] for p in planes], 10, 5)


def put(lo, hi, place, tile):
    at, count = place
    if count:
        lo[at : at + count] = tile[0:count]
        hi[at : at + count] = tile[8 - count : 8]


def by_parity(body):
    even = lax.rem(lax.axis_index("gy"), 2) == 0
    pl.when(even)(lambda: body(True))
    pl.when(jnp.logical_not(even))(lambda: body(False))


def second_pack(cells, across, one, two, grow):
    by_parity(lambda even: own_rows(cells, across, *((one, two) if even else (two, one))))
    for f in range(3):
        grow[f, 0:OWN] = cells[f, 0:OWN]
        grow[f, OWN : OWN + 2] = across[3 * f : 3 * f + 2]


def own_rows(cells, across, own_lo, own_hi):
    for f in range(3):
        for i in range(OWN):
            put(own_lo, own_hi, OWN_PLAN["cell", f, i], cells[f, i + 11])
        for q in range(2):
            put(own_lo, own_hi, OWN_PLAN["edge", f, q], across[3 * f + q + 1])
    for ref in (own_lo, own_hi):
        blank(ref, OWN_PLAN, OWN_ROWS)


def blank(ref, places, rows):
    used = max(at + count for at, count in places.values())
    ref[0:8] = jnp.zeros((8, 128), jnp.float32)
    if used < rows:
        ref[used:rows] = jnp.zeros((rows - used, 128), jnp.float32)


def third_pack(grow, codes, across, one, two):
    by_parity(lambda even: up_rows(grow, codes, across, *((one, two) if even else (two, one))))


def place():
    index = lax.axis_index("grow")
    return index == 0, index == lax.axis_size("grow") - 1


def up_rows(grow, codes, across, up_lo, up_hi):
    _, last = place()
    for ref in (up_lo, up_hi):
        blank(ref, UP_PLAN, UP_ROWS)

    @pl.when(jnp.logical_not(last))
    def _():
        for f in range(3):
            for i in range(OWN):
                put(up_lo, up_hi, UP_PLAN["cell", f, i], grow[f, i])
            for q in range(2):
                put(up_lo, up_hi, UP_PLAN["edge", f, q], grow[f, OWN + q])

    @pl.when(last)
    def _():
        for ref in (up_lo, up_hi):
            ref[...] = jnp.zeros((UP_ROWS, 128), jnp.float32)
        for e in range(SHIFT):
            put(up_lo, up_hi, CODE_PLAN["code", 0, e], codes[e])
        put(up_lo, up_hi, CODE_PLAN["code_edge", 0, 0], across[9])


def react(phases, sums, chem, chem_sums, held):
    p0, p1, p2 = phases
    p3 = K - ((p0 + p1) + p2)
    n3 = 6.0 * K - ((sums[0] + sums[1]) + sums[2])
    ps = (p0, p1, p2, p3)
    ns = (sums[0], sums[1], sums[2], n3)
    squares = [p * p for p in ps]
    base = (0.28 / 0.12) - ((squares[0] + squares[1]) + (squares[2] + squares[3]))
    m0, m1 = chem
    both = BETA * (m0 + m1)
    w2 = both + DRIFT
    ws = (w2 + (7.0 * BETA) * m0, w2 + (7.0 * BETA) * m1, w2, 3.5 * both)
    moved = [
        ns[a] + ps[a] * ((base + squares[a]) + ws[a] * (K - ps[a])) for a in range(4)
    ]
    excess = 0.25 * ((moved[0] + moved[1]) + (moved[2] + moved[3])) - 0.25 * TOP
    clipped = [jnp.minimum(jnp.maximum(u - excess, 0.0), TOP) for u in moved]
    scale = K / ((clipped[0] + clipped[1]) + (clipped[2] + clipped[3]))
    new = [s * scale for s in clipped]
    h = [x * x * (1.5 * K - x) for x in new]
    shared = (h[0] + h[1]) + (h[2] + 3.5 * h[3])
    solute = (shared + 7.0 * h[0], shared + 7.0 * h[1])
    mobility = 0.0075 + (0.1425 / K) * p3
    new_held = [held[i] + mobility * (chem_sums[i] - 6.0 * chem[i]) for i in range(2)]
    new_chem = [new_held[i] - solute[i] for i in range(2)]
    return new, new_chem, new_held


class Half:
    def __init__(self, base, strip_base, n, cells, codes, across, own, up, grow, wing):
        self.base, self.strip_base, self.n = base, strip_base, n
        self.cells, self.codes, self.across = cells, codes, across
        self.own, self.up, self.grow, self.wing, self.lane = own, up, grow, wing, lanes()

    def source(self, p):
        up = p >= OWN
        i = p - OWN if up else p
        q, c = divmod(i, PACK)
        return up, i, q, c

    def store(self, dst, index, rows, label, m0, m1, mask=None):
        values = [jnp.where(label == a, K, 0.0) for a in range(3)]
        rest = jnp.where(label == 3.0, 3.5 * HALF, HALF)
        values += [ALPHA * m0, ALPHA * m1]
        values += [values[3 + i] + jnp.where(label == i, 8.0 * HALF, rest) for i in range(2)]
        for f, value in enumerate(values):
            if mask is not None:
                value = jnp.where(mask, value, dst[f, index, rows, :])
            dst[f, index, rows, :] = value

    def fill(self, dst, p):
        up, i, _, _ = self.source(p)
        body = [self.grow[f, i] if up else self.cells[f, i + 11] for f in range(3)]
        self.store(dst, p - self.base, slice(ROW0, ROW0 + 8), *body)
        for hi, ref in enumerate(self.up if up else self.own):
            count = reach(i, up)
            if count:
                places = UP_PLAN if up else OWN_PLAN
                body = []
                for f in range(3):
                    at, _ = places["cell", f, i]
                    body.append(ref[at : at + count])
                row = ROW0 - count if hi else ROW0 + 8
                self.store(dst, p - self.base, slice(row, row + count), *body)

    def pieces(self, p, f, block):
        up, i, q, _ = self.source(p)
        if block == 0:
            if up:
                return self.grow[f, i], self.grow[f, OWN + q]
            return self.cells[f, i + 11], self.across[3 * f + q + 1]
        places = UP_PLAN if up else OWN_PLAN
        ref = (self.up if up else self.own)[block - 1]
        at, count = places["cell", f, i]
        at = at if block == 1 else at + count - DEEP
        edge, _ = places["edge", f, q]
        return ref[at : at + DEEP], ref[edge : edge + DEEP]

    def joined(self, parts):
        rows = next(part for part in parts if part is not None)[0].shape[0]
        lane = lax.broadcasted_iota(jnp.int32, (rows, 128), 1)
        total = jnp.zeros((rows, 128), jnp.float32)
        for j, part in enumerate(parts):
            if part is None:
                continue
            value, edge, before, after = part
            at = 20 * j
            tile = jnp.where(
                lane < at + 10,
                jnp.where(lane < at + 5, pltpu.roll(edge, before % 128, 1), pltpu.roll(value, at + 5, 1)),
                jnp.where(lane < at + 15, pltpu.roll(value, (at + 15) % 128, 1), pltpu.roll(edge, after % 128, 1)),
            )
            total = jnp.where(lane >= at, tile, total)
        return total

    def fill_strips(self, dst, top, blocks):
        for index in range(self.n):
            for block, row, _ in blocks:
                body = []
                for f in range(3):
                    parts = []
                    for j in range(6):
                        p = self.strip_base + self.n * j + index
                        if p >= top:
                            parts.append(None)
                            continue
                        c = self.source(p)[3]
                        parts.append(
                            (*self.pieces(p, f, block), 20 * j - 10 * c, 20 * j + 10 - 10 * c)
                        )
                    body.append(self.joined(parts))
                self.store(dst, index, slice(row, row + body[0].shape[0]), *body)

    def melt(self, dst, strips, table):
        def chem(code, i):
            value = jnp.zeros_like(code)
            for level in range(8):
                value = jnp.where(code == level, table[i, level], value)
            return value

        def rows(block, e):
            if block == 0:
                return self.codes[e], self.across[9]
            ref = self.up[block - 1]
            at, _ = CODE_PLAN["code", 0, e]
            edge, _ = CODE_PLAN["code_edge", 0, 0]
            return ref[at : at + 2], ref[edge : edge + 2]

        for e in range(SHIFT):
            for block, row, count in MELT_BLOCKS:
                code = rows(block, e)[0]
                label = jnp.full_like(code, 3.0)
                where = slice(row, row + count)
                self.store(dst, OWN + e - self.base, where, label, chem(code, 0), chem(code, 1))
        for index in range(self.n):
            for block, row, count in MELT_BLOCKS:
                parts, groups = [], []
                for j in range(6):
                    e = self.strip_base + self.n * j + index - OWN
                    if not 0 <= e < SHIFT:
                        parts.append(None)
                        continue
                    groups.append(j)
                    parts.append((*rows(block, e), 20 * j + 1 - 8 * e, 20 * j + 11 - 8 * e))
                code = self.joined(parts)
                lane = lax.broadcasted_iota(jnp.int32, code.shape, 1)
                mask = (lane >= 20 * groups[0]) & (lane < 20 * groups[-1] + 20)
                label = jnp.full_like(code, 3.0)
                where = slice(row, row + count)
                self.store(strips, index, where, label, chem(code, 0), chem(code, 1), mask)

    def repeat(self, dst, p, source):
        for f in range(5):
            dst[f, p - self.base, 7:25, :] = dst[f, source - self.base, 7:25, :]

    def repeat_strip(self, strips, p, source):
        j, index = divmod(p - self.strip_base, self.n)
        j_from, index_from = divmod(source - self.strip_base, self.n)
        lane = lax.broadcasted_iota(jnp.int32, (18, 128), 1)
        mask = (lane >= 20 * j) & (lane < 20 * j + 20)
        for f in range(5):
            value = strips[f, index_from, 7:25, :]
            if j != j_from:
                value = pltpu.roll(value, 20 * (j - j_from), 1)
            strips[f, index, 7:25, :] = jnp.where(mask, value, strips[f, index, 7:25, :])

    def advance(self, src, index, row, fetch, sides):
        here, sums = [], []
        for f in range(5):
            mid = src[f, index, row : row + 8, :]
            below, above = fetch(f)
            total = (below + above) + (
                src[f, index, row - 1 : row + 7, :] + src[f, index, row + 1 : row + 9, :]
            )
            left, right = sides(f, mid)
            here.append(mid)
            sums.append(total + (left + right))
        held = [src[f, index, row : row + 8, :] for f in (5, 6)]
        return react(here[:3], sums[:3], here[3:], sums[3:], held)

    def spread(self, strips, rows):
        second = self.lane == 3
        for j in range(1, 6):
            second = second | (self.lane == 20 * j + 3)
        for f in range(5):
            for index in range(self.n):
                for row in rows:
                    tile = strips[f, index, row : row + 8, :]
                    tile = jnp.where(second, pltpu.roll(tile, 116, 1), tile)
                    self.wing[f, index, row : row + 8, :] = tile

    def plane_step(self, src, p, row):
        index = p - self.base
        q = p - self.strip_base
        j = (q * 13) >> 6 if self.n == 5 else q >> 2
        at = q - self.n * j
        turn = 124 - 20 * j
        rows = slice(row, row + 8)

        def fetch(f):
            return src[f, index - 1, rows, :], src[f, index + 1, rows, :]

        def sides(f, mid):
            beyond = pltpu.roll(self.wing[f, at, rows, :], turn, 1)
            left = jnp.where(self.lane == 0, beyond, pltpu.roll(mid, 1, 1))
            return left, jnp.where(self.lane == 127, beyond, pltpu.roll(mid, 127, 1))

        return self.advance(src, index, row, fetch, sides)

    def planes(self, first, count, body):
        whole = count - count % 8
        if whole:
            pl.loop(first, first + whole, unroll=8)(body)
        for p in range(first + whole, first + count):
            body(p)

    def sweep(self, src, dst, src_strips, dst_strips, first, count):
        self.spread(src_strips, (8, 16))

        def body(p):
            for row in (8, 16):
                new, chem, held = self.plane_step(src, p, row)
                for f, value in enumerate((*new[:3], *chem, *held)):
                    dst[f, p - self.base, row : row + 8, :] = value

        self.planes(first, count, body)
        last = self.n - 1

        def inside(f, mid):
            return pltpu.roll(mid, 1, 1), pltpu.roll(mid, 127, 1)

        for index in range(self.n):
            for row in (8, 16):
                rows = slice(row, row + 8)

                def fetch(f, index=index, rows=rows):
                    if index:
                        below = src_strips[f, index - 1, rows, :]
                    else:
                        below = pltpu.roll(src_strips[f, last, rows, :], 20, 1)
                    if index < last:
                        above = src_strips[f, index + 1, rows, :]
                    else:
                        above = pltpu.roll(src_strips[f, 0, rows, :], 108, 1)
                    return below, above

                new, chem, held = self.advance(
                    src_strips, index, row, fetch, inside
                )
                for f, value in enumerate((*new[:3], *chem, *held)):
                    dst_strips[f, index, row : row + 8, :] = value

    def finish(self, src, first, count, phases, chems, at=0):
        def body(p):
            new, chem, _ = self.plane_step(src, p, ROW0)
            for a in range(4):
                phases[a, p - first + at] = new[a] * (1.0 / K)
            for i in range(2):
                chems[i, p - first + at] = chem[i] * (1.0 / ALPHA)

        self.planes(first, count, body)


BLOCKS = ((0, ROW0, 8), (1, ROW0 + 8, DEEP), (2, ROW0 - DEEP, DEEP))
MELT_BLOCKS = ((0, ROW0, 8), (1, ROW0 + 8, 2), (2, ROW0 - 2, 2))
LOWER = 11


def strip_pack(cells, across, own_strips):
    half = Half(0, 0, 4, cells, None, across, None, None, None, None)
    half.fill_strips(own_strips, OWN, ((0, 0, 8),))


def lower_half(
    cells, across, own_strips, swap_one, swap_two,
    phases, chems, seam, rows_lo, rows_hi,
    one, two, strip_one, strip_two, wing,
):
    first, _ = place()

    def sort_rows(even):
        rows_lo[...] = (swap_two if even else swap_one)[...]
        rows_hi[...] = (swap_one if even else swap_two)[...]

    by_parity(sort_rows)
    half = Half(0, 0, 4, cells, None, across, (rows_lo, rows_hi), None, None, wing)
    for p in range(OWN):
        half.fill(one, p)
    strip_one[:, :, ROW0 : ROW0 + 8, :] = own_strips[...]
    half.fill_strips(strip_one, OWN, BLOCKS[1:])
    src, dst, src_strips, dst_strips = one, two, strip_one, strip_two
    for s in range(1, 5):
        if s == 4:

            @pl.when(first)
            def _(src=src, src_strips=src_strips):
                half.repeat(src, 4, 5)
                half.repeat_strip(src_strips, 4, 5)

        half.sweep(src, dst, src_strips, dst_strips, s, OWN - 2 * s)
        for f in range(7):
            for i in range(2):
                seam[s - 1, f, i] = dst[f, OWN - 1 - s + i - 1, 8:24, :]
        src, dst, src_strips, dst_strips = dst, src, dst_strips, src_strips

    @pl.when(first)
    def _(src=src):
        half.repeat(src, 4, 5)

    half.spread(src_strips, (ROW0,))
    half.finish(src, 5, LOWER, phases, chems)


def delivery(phases, chems, phases_out, chem_out, first, at, count, sems, s):
    source, target = pl.ds(at, count), pl.ds(first, count)
    copies = [
        pltpu.make_async_copy(phases.at[:, source], phases_out.at[:, target], sems.at[s]),
        pltpu.make_async_copy(chems.at[:, source], chem_out.at[:, target], sems.at[s + 1]),
    ]
    for copy in copies:
        copy.start()
    return copies


def upper_half(
    cells, codes, table_in, across, own_lo, own_hi, swap_one, swap_two, grow, seam,
    lower_phases, lower_chems, phases_out, chem_out,
    one, two, strip_one, strip_two, wing, phases, chems, up_lo, up_hi, table, sem, sems,
):
    outs = (phases_out, chem_out)
    copies = delivery(lower_phases, lower_chems, *outs, 0, 0, LOWER, sems, 0)
    _, last = place()

    def sort_rows(even):
        up_lo[...] = (swap_two if even else swap_one)[...]
        up_hi[...] = (swap_one if even else swap_two)[...]

    by_parity(sort_rows)
    half = Half(
        15, 12, 5, cells, codes, across, (own_lo, own_hi), (up_lo, up_hi), grow, wing
    )
    for p in range(OWN - 2, PLANES):
        half.fill(one, p)
    half.fill_strips(strip_one, PLANES, BLOCKS)
    src, dst, src_strips, dst_strips = one, two, strip_one, strip_two
    for s in range(1, 6):
        if s > 1:
            for f in range(7):
                for i in range(2):
                    src[f, OWN - 1 - s + i - half.base, 8:24, :] = seam[s - 2, f, i]
        if s < 4:

            @pl.when(last)
            def _(src=src, src_strips=src_strips):
                half.repeat(src, OWN, OWN - 1)
                half.repeat_strip(src_strips, OWN, OWN - 1)

        if s == 4:

            @pl.when(last)
            def _(src=src, src_strips=src_strips):
                copy = pltpu.make_async_copy(table_in, table, sem)
                copy.start()
                copy.wait()
                half.melt(src, src_strips, table)
                half.repeat_strip(src_strips, OWN + SHIFT, OWN + SHIFT - 1)

        if s >= 4:

            @pl.when(last)
            def _(src=src):
                half.repeat(src, OWN + SHIFT, OWN + SHIFT - 1)

        if s < 5:
            half.sweep(src, dst, src_strips, dst_strips, OWN - s, OWN)
            src, dst, src_strips, dst_strips = dst, src, dst_strips, src_strips
    half.spread(src_strips, (ROW0,))
    half.finish(src, OWN - 5, 16, phases, chems)
    copies += delivery(phases, chems, *outs, LOWER, 0, 16, sems, 2)
    half.finish(src, OWN + 11, 5, phases, chems, 16)
    copies += delivery(phases, chems, *outs, LOWER + 16, 16, 5, sems, 4)
    for copy in copies:
        copy.wait()


def on_device(labels, potential, melt_codes, melt_table):
    n_grow, n_gy, n_gz = (lax.axis_size(a) for a in AXES)

    def send(value, dg, dy, dz):
        pairs = []
        for g in range(n_grow):
            for y in range(n_gy):
                for z in range(n_gz):
                    side = (z + dz + (not 0 <= g + dg < n_grow)) % n_gz
                    to = ((g + dg) % n_grow * n_gy + (y + dy) % n_gy) * n_gz + side
                    pairs.append(((g * n_gy + y) * n_gz + z, to))
        return lax.ppermute(value, AXES, pairs)

    def f32(*shape):
        return jax.ShapeDtypeStruct(shape, jnp.float32)

    params = pltpu.CompilerParams(vmem_limit_bytes=48 << 20)
    cells, codes, edges = pl.pallas_call(
        first_pack,
        in_specs=[HBM] * 3,
        out_specs=[VMEM] * 3,
        out_shape=[f32(3, 32, 8, 128), f32(SHIFT, 8, 128), f32(10, 8, 128)],
        scratch_shapes=[
            pltpu.VMEM((32, 8, 128), jnp.int32),
            pltpu.VMEM((SHIFT, 8, 128), jnp.int32),
            pltpu.SemaphoreType.DMA((3,)),
        ],
        compiler_params=params,
        name="first_pack",
    )(*(pltpu.with_memory_space_constraint(x, pltpu.MemorySpace.HBM) for x in (labels, potential, melt_codes)))
    across = send(edges, 0, 0, 1)
    own_one, own_two, grow = pl.pallas_call(
        second_pack,
        in_specs=[VMEM] * 2,
        out_specs=[VMEM] * 3,
        out_shape=[f32(OWN_ROWS, 128)] * 2 + [f32(3, OWN + 2, 8, 128)],
        compiler_params=params,
        name="second_pack",
    )(cells, across)

    def swap(one, two):
        below = [(y, (y + (1 if y % 2 else -1)) % n_gy) for y in range(n_gy)]
        above = [(y, (y + (-1 if y % 2 else 1)) % n_gy) for y in range(n_gy)]
        return lax.ppermute(one, "gy", below), lax.ppermute(two, "gy", above)

    own_one, own_two = swap(own_one, own_two)
    grow = send(grow, -1, 0, 0)
    up_one, up_two = pl.pallas_call(
        third_pack,
        in_specs=[VMEM] * 3,
        out_specs=[VMEM] * 2,
        out_shape=[f32(UP_ROWS, 128)] * 2,
        compiler_params=params,
        name="third_pack",
    )(grow, codes, across)
    up_one, up_two = swap(up_one, up_two)

    def buffers(planes, strips):
        return (
            [pltpu.VMEM((7, planes, PITCH, 128), jnp.float32)] * 2
            + [pltpu.VMEM((7, strips, PITCH, 128), jnp.float32)] * 2
            + [pltpu.VMEM((5, strips, PITCH, 128), jnp.float32)]
        )

    own_strips = pl.pallas_call(
        strip_pack,
        in_specs=[VMEM] * 2,
        out_specs=VMEM,
        out_shape=f32(7, 4, 8, 128),
        compiler_params=params,
        name="strip_pack",
    )(cells, across)
    phases, chems, seam, own_lo, own_hi = pl.pallas_call(
        lower_half,
        in_specs=[VMEM] * 5,
        out_specs=[VMEM] * 5,
        out_shape=[f32(4, LOWER, 8, 128), f32(2, LOWER, 8, 128), f32(4, 7, 2, 16, 128)]
        + [f32(OWN_ROWS, 128)] * 2,
        scratch_shapes=buffers(OWN, 4),
        compiler_params=params,
        cost_estimate=pl.CostEstimate(
            flops=60_000_000, bytes_accessed=12_000_000, transcendentals=0
        ),
        name="lower_half",
    )(cells, across, own_strips, own_one, own_two)
    table = pltpu.with_memory_space_constraint(melt_table, pltpu.MemorySpace.HBM)
    return pl.pallas_call(
        upper_half,
        in_specs=[VMEM, VMEM, HBM] + [VMEM] * 9,
        out_specs=[HBM, HBM],
        out_shape=[f32(4, 32, 8, 128), f32(2, 32, 8, 128)],
        scratch_shapes=buffers(27, 5)
        + [
            pltpu.VMEM((4, OWN, 8, 128), jnp.float32),
            pltpu.VMEM((2, OWN, 8, 128), jnp.float32),
            pltpu.VMEM((UP_ROWS, 128), jnp.float32),
            pltpu.VMEM((UP_ROWS, 128), jnp.float32),
            pltpu.SMEM((2, 8), jnp.float32),
            pltpu.SemaphoreType.DMA,
            pltpu.SemaphoreType.DMA((6,)),
        ],
        compiler_params=params,
        name="upper_half",
    )(cells, codes, table, across, own_lo, own_hi, up_one, up_two, grow, seam, phases, chems)


def solution(mesh):
    return jax.shard_map(
        on_device,
        mesh=mesh,
        in_specs=(P("grow", "gy", "gz"), P(None, "grow", "gy", "gz"), P(None, "gy", "gz"), P()),
        out_specs=(P(None, "grow", "gy", "gz"), P(None, "grow", "gy", "gz")),
        check_vma=False,
    )
```
